32 devices in a mesh: wide: 8 (over z, x), narrow: 4 (over y, core).
Axes of the slice: x: 2, y: 2, z: 4, core: 2. Of those that a mesh axis runs over, the one named last changes fastest.
Arguments:
- tokens: bfloat16 [16384, 768], P(('wide', 'narrow')), may hold values from -6 to 6
- timestep: int32 [16], P('wide'), may hold values from 0 to 999
- token_mask: int32 [16384], P(('wide', 'narrow')), may hold values 0 or 1
- time_table: float32 [1000, 128], replicated, may hold values from -6 to 6
- w_ada: bfloat16 [128, 4608], replicated, may hold values from -0.5 to 0.5
- b_ada: float32 [4608], replicated, may hold values from -3 to 3
- gain_one: float32 [768], replicated, may hold values from 0.5 to 1.5
- w_qkv: bfloat16 [3, 768, 768], P(None, None, 'narrow'), may hold values from -0.21875 to 0.21875
- w_out: bfloat16 [768, 768], P('narrow'), may hold values from -3.5 to 3.5
- gain_two: float32 [768], replicated, may hold values from 0.5 to 1.5
- w_up: bfloat16 [768, 3072], P(None, 'narrow'), may hold values from -0.21875 to 0.21875
- b_up: float32 [3072], P('narrow'), may hold values from -3 to 3
- w_down: bfloat16 [3072, 768], P('narrow'), may hold values from -0.109375 to 0.109375
- b_down: float32 [768], replicated, may hold values from -3 to 3
- cotangent: bfloat16 [16384, 768], P(('wide', 'narrow')), may hold values from -6 to 6
Outputs:
- mixed: bfloat16 [16384, 768], P(('wide', 'narrow'))
- grad_tokens: float32 [16384, 768], P(('wide', 'narrow'))
- grad_time_table: float32 [1000, 128], replicated
- grad_w_ada: float32 [128, 4608], replicated
- grad_b_ada: float32 [4608], replicated
- grad_gain_one: float32 [768], replicated
- grad_w_qkv: float32 [3, 768, 768], P(None, None, 'narrow')
- grad_w_out: float32 [768, 768], P('narrow')
- grad_gain_two: float32 [768], replicated
- grad_w_up: float32 [768, 3072], P(None, 'narrow')
- grad_b_up: float32 [3072], P('narrow')
- grad_w_down: float32 [3072, 768], P('narrow')
- grad_b_down: float32 [768], replicated
The draws below stay inside these ranges and needn't reach their ends.
Inputs may be any that keep to these rules, and one draw needn't show every extreme that they name: One timestep for each sequence of 1024 tokens.
All inputs are finite; a program needn't handle non-finite values. No bound on the sum of `token_mask` on one device may be relied on, other than what follows from the above.
Results may differ from the reference program's by a relative error of at most 0.02.
The reference program's roundings to bfloat16 on the way count: a program that leaves them out, or rounds other values in their place, can miss the bound.
Values may be sent and summed in bfloat16 or wider, within the bound.
A program may use at most 192 MiB of HBM per device.

```python
import math
import jax
import jax.numpy as jnp
from jax import lax

D = 768
HEADS = 12
HD = 64
FF = 3072
COND = 128
STEPS = 1000
LEN = 1024
SEQS = 2
ROWS = 16
TOKENS = 16384
N_WIDE = 8
N_NARROW = 4


def set_ends(array, stream_key, low, largest):
    longest = array.shape.index(max(array.shape))
    spots = []
    for shift in (0, 1):
        where = [jax.random.randint(jax.random.fold_in(stream_key, axis), (), 0, length) for axis, length in enumerate(array.shape)]
        where[longest] = (where[longest] + shift) % array.shape[longest]
        spots.append(tuple(where))
    return array.at[spots[0]].set(low).at[spots[1]].set(largest)


def block_scale(rng, extent, cuts, smallest, largest):
    level, own = 1.0, jax.random.fold_in(rng, 6)
    for axis_at, parts in cuts:
        heights = jnp.exp(jax.random.uniform(jax.random.fold_in(own, axis_at), (parts,), jnp.float32, smallest / len(cuts), largest / len(cuts)))
        level = level * jnp.repeat(heights, extent[axis_at] // parts).reshape([-1 if axis == axis_at else 1 for axis in range(len(extent))])
    return level


def centred(stream_key, dims, spread, reach, shards=(), held_as=jnp.bfloat16):
    level = block_scale(stream_key, dims, shards, -0.22, 0.18) if shards else 1.0
    entries = jax.random.normal(stream_key, dims, jnp.float32) * spread * level
    return jnp.minimum(jnp.maximum(entries, -reach), reach).astype(held_as)


def setup_inputs(seed: int = 0) -> dict:
    key_of = jax.random.split(jax.random.key(seed), 16)
    tokens = centred(key_of[0], (TOKENS, D), 1.0, 6.0, ((0, 32),))
    timestep = set_ends(jax.random.randint(key_of[1], (ROWS,), 0, STEPS), jax.random.fold_in(key_of[1], 1), 0, STEPS - 1).astype(jnp.int32)
    token_mask = set_ends((jax.random.randint(key_of[2], (TOKENS,), 0, 2) < 1).astype(jnp.int32), jax.random.fold_in(key_of[2], 1), 0, 1)
    time_table = centred(key_of[3], (STEPS, COND), 1.0, 6.0, (), jnp.float32)
    w_ada = centred(key_of[4], (COND, 6 * D), COND ** -0.5, 0.5)
    b_ada = centred(key_of[5], (6 * D,), 0.5, 3.0, (), jnp.float32)
    gain_one = jnp.clip(1.0 + 0.1 * jax.random.normal(key_of[6], (D,), jnp.float32), 0.5, 1.5)
    w_qkv = centred(key_of[7], (3, D, D), D ** -0.5, 0.21875, ((2, 4),))
    w_out = centred(key_of[8], (D, D), (max(D // 256, 1)) ** -0.5, 3.5, ((0, 4),))
    gain_two = jnp.clip(1.0 + 0.1 * jax.random.normal(key_of[9], (D,), jnp.float32), 0.5, 1.5)
    w_up = centred(key_of[10], (D, FF), D ** -0.5, 0.21875, ((1, 4),))
    b_up = centred(key_of[11], (FF,), 0.5, 3.0, ((0, 4),), jnp.float32)
    w_down = centred(key_of[12], (FF, D), FF ** -0.5, 0.109375, ((0, 4),))
    b_down = centred(key_of[13], (D,), 0.5, 3.0, (), jnp.float32)
    cotangent = centred(key_of[14], (TOKENS, D), 1.0, 6.0, ((0, 32),))
    return {"tokens": tokens, "timestep": timestep, "token_mask": token_mask, "time_table": time_table, "w_ada": w_ada, "b_ada": b_ada, "gain_one": gain_one, "w_qkv": w_qkv, "w_out": w_out, "gain_two": gain_two, "w_up": w_up, "b_up": b_up, "w_down": w_down, "b_down": b_down, "cotangent": cotangent}


@jax.custom_vjp
def low(v):
    return lax.optimization_barrier(v.astype(jnp.bfloat16)).astype(jnp.float32)

@jax.custom_vjp
def low_back(v):
    return v

def low_keep(v):
    return (low(v), None)

def low_pass(kept, grad):
    return (grad,)

def back_keep(v):
    return (v, None)

def back_low(kept, grad):
    return (low(grad),)
low.defvjp(low_keep, low_pass)
low_back.defvjp(back_keep, back_low)
norm_eps = 1e-06
highest = lax.Precision.HIGHEST

def layer_norm(values, norm_gain):
    centered = values - lax.optimization_barrier(jnp.mean(values, axis=-1, keepdims=True))
    variance = lax.optimization_barrier(jnp.mean(centered * centered, axis=-1, keepdims=True))
    return centered * lax.rsqrt(variance + norm_eps) * norm_gain

def rope_tables():
    half_width = HD // 2
    frequency = 10000.0 ** (-2.0 * jnp.arange(half_width, dtype=jnp.float32) / HD)
    angles = jnp.arange(LEN, dtype=jnp.float32)[:, None] * frequency[None, :]
    cos_table = jnp.concatenate([jnp.cos(angles), jnp.cos(angles)], axis=1)[:, None, :]
    sin_table = jnp.concatenate([jnp.sin(angles), jnp.sin(angles)], axis=1)[:, None, :]
    return (cos_table, sin_table)

def rotate(values, cos_table, sin_table):
    half_width = values.shape[-1] // 2
    turned = jnp.concatenate([-values[..., half_width:], values[..., :half_width]], axis=-1)
    return values * cos_table + turned * sin_table

def layer_rows(token_rows, step_ids, time_table, w_ada, b_ada, gain_one, w_qkv, w_out, gain_two, w_up, b_up, w_down, b_down):
    width_local = D // N_NARROW
    head_local = HEADS // N_NARROW
    hidden_local = FF // N_NARROW
    scale_factor = 1.0 / math.sqrt(HD)
    condition = low(jax.nn.silu(time_table[step_ids]))
    modulation = low_back(jnp.dot(condition, w_ada, precision=highest)) + b_ada
    mod_tok = jnp.repeat(modulation.reshape(SEQS, 6, D), LEN, axis=0)
    cos_table, sin_table = rope_tables()
    normed = low(layer_norm(token_rows, gain_one) * (1.0 + mod_tok[:, 1]) + mod_tok[:, 0])
    attention = jnp.zeros(token_rows.shape, jnp.float32)
    for head_group in range(N_NARROW):
        columns = slice(head_group * width_local, (head_group + 1) * width_local)
        projected = low_back(jnp.einsum('td,kde->kte', normed, w_qkv[:, :, columns], precision=highest))
        shaped = projected.reshape(3, SEQS, LEN, head_local, HD)
        queries = low(rotate(shaped[0], cos_table, sin_table))
        key_rows = low(rotate(shaped[1], cos_table, sin_table))
        values = low(shaped[2])
        scores = low_back(jnp.einsum('bqhe,bkhe->bhqk', queries, key_rows, precision=highest)) * scale_factor
        probs_low = low(jax.nn.softmax(scores, axis=-1))
        head_out = low(low_back(jnp.einsum('bhqk,bkhe->bqhe', probs_low, values, precision=highest)))
        group_out = low_back(jnp.dot(head_out.reshape(SEQS * LEN, width_local), w_out[columns], precision=highest))
        attention = attention + low(group_out)
    mid_residual = token_rows + mod_tok[:, 2] * attention
    normed_two = low(layer_norm(mid_residual, gain_two) * (1.0 + mod_tok[:, 4]) + mod_tok[:, 3])
    branch = jnp.zeros(token_rows.shape, jnp.float32)
    for unit_group in range(N_NARROW):
        units = slice(unit_group * hidden_local, (unit_group + 1) * hidden_local)
        pre_act = low_back(jnp.dot(normed_two, w_up[:, units], precision=highest) + b_up[units])
        hidden = low(jax.nn.gelu(pre_act, approximate=True))
        group_out = low_back(jnp.dot(hidden, w_down[units], precision=highest))
        branch = branch + low(group_out)
    return mid_residual + mod_tok[:, 5] * (branch + b_down)

def reference(tokens, timestep, token_mask, time_table, w_ada, b_ada, gain_one, w_qkv, w_out, gain_two, w_up, b_up, w_down, b_down, cotangent):
    floats = (tokens.astype(jnp.float32), time_table, w_ada.astype(jnp.float32), b_ada, gain_one, w_qkv.astype(jnp.float32), w_out.astype(jnp.float32), gain_two, w_up.astype(jnp.float32), b_up, w_down.astype(jnp.float32), b_down)
    step_groups = timestep.reshape(N_WIDE, SEQS)

    def whole_layer(token_all, *params):

        def scan_step(scan_carry, pieces):
            return (scan_carry, jax.checkpoint(layer_rows)(pieces[0], pieces[1], *params))
        _, outputs = lax.scan(scan_step, jnp.zeros((), jnp.float32), (token_all.reshape(N_WIDE, SEQS * LEN, D), step_groups))
        return outputs.reshape(TOKENS, D)
    mixed, pullback = jax.vjp(whole_layer, *floats)
    grads = pullback(cotangent.astype(jnp.float32) * token_mask.astype(jnp.float32)[:, None])
    return (mixed.astype(jnp.bfloat16), grads[0], grads[1], grads[2], grads[3], grads[4], grads[5], grads[6], grads[7], grads[8], grads[9], grads[10], grads[11])
```

```python
from functools import partial
import math

import jax
import jax.numpy as jnp
from jax import lax
from jax.sharding import PartitionSpec as P

D = 768
HD = 64
LEN = 1024
SEQS = 2


norm_eps = 1e-06
highest = lax.Precision.HIGHEST


def layer_norm(values, norm_gain):
    centered = values - jnp.mean(values, axis=-1, keepdims=True)
    variance = jnp.mean(centered * centered, axis=-1, keepdims=True)
    return centered * lax.rsqrt(variance + norm_eps) * norm_gain


def norm_back(values, norm_gain, grad_norm):
    _, pullback = jax.vjp(layer_norm, values, norm_gain)
    return pullback(grad_norm)


def rope_tables():
    half_width = HD // 2
    frequency = 10000.0 ** (-2.0 * jnp.arange(half_width, dtype=jnp.float32) / HD)
    angles = jnp.arange(LEN, dtype=jnp.float32)[:, None] * frequency[None, :]
    cos_table = jnp.concatenate([jnp.cos(angles), jnp.cos(angles)], axis=1)[:, None, :]
    sin_table = jnp.concatenate([jnp.sin(angles), jnp.sin(angles)], axis=1)[:, None, :]
    return (cos_table, sin_table)


def rotate(values, cos_table, sin_table):
    half_width = values.shape[-1] // 2
    turned = jnp.concatenate([-values[..., half_width:], values[..., :half_width]], axis=-1)
    return values * cos_table + turned * sin_table


def attend(q_low, k_low, v_low):
    scale_factor = 1.0 / math.sqrt(HD)
    block_rows = min(512, LEN)

    def one_sequence(pieces):
        q_seq, k_seq, v_seq = pieces
        outputs = []
        log_parts = []
        for first_row in range(0, LEN, block_rows):
            scores = (
                jnp.einsum(
                    "qhe,khe->hqk",
                    q_seq[first_row : first_row + block_rows],
                    k_seq,
                    preferred_element_type=jnp.float32,
                )
                * scale_factor
            )
            row_max = jnp.max(scores, axis=-1, keepdims=True)
            exp_scores = jnp.exp(scores - row_max)
            row_sum = jnp.sum(exp_scores, axis=-1, keepdims=True)
            probs_low = (exp_scores / row_sum).astype(jnp.bfloat16)
            outputs.append(
                jnp.einsum("hqk,khe->qhe", probs_low, v_seq, preferred_element_type=jnp.float32)
            )
            log_parts.append((row_max + jnp.log(row_sum))[..., 0])
        return (jnp.concatenate(outputs, axis=0), jnp.concatenate(log_parts, axis=1))

    return lax.map(one_sequence, (q_low, k_low, v_low))


def attend_back(q_low, k_low, v_low, log_sums, grad_heads):
    scale_factor = 1.0 / math.sqrt(HD)
    block_rows = min(512, LEN)

    def one_sequence(pieces):
        q_seq, k_seq, v_seq, sums_seq, grad_seq = pieces
        grad_keys = jnp.zeros(k_seq.shape, jnp.float32)
        grad_values = jnp.zeros(v_seq.shape, jnp.float32)
        grad_queries = []
        for first_row in range(0, LEN, block_rows):
            q_block = q_seq[first_row : first_row + block_rows]
            grad_block = grad_seq[first_row : first_row + block_rows]
            scores = (
                jnp.einsum("qhe,khe->hqk", q_block, k_seq, preferred_element_type=jnp.float32)
                * scale_factor
            )
            probs = jnp.exp(scores - sums_seq[:, first_row : first_row + block_rows, None])
            probs_low = probs.astype(jnp.bfloat16)
            grad_values = grad_values + jnp.einsum(
                "hqk,qhe->khe", probs_low, grad_block, preferred_element_type=jnp.float32
            )
            grad_probs = jnp.einsum(
                "qhe,khe->hqk", grad_block, v_seq, preferred_element_type=jnp.float32
            )
            inner_sum = jnp.sum(probs * grad_probs, axis=-1, keepdims=True)
            grad_scores = (probs * (grad_probs - inner_sum) * scale_factor).astype(jnp.bfloat16)
            grad_queries.append(
                jnp.einsum("hqk,khe->qhe", grad_scores, k_seq, preferred_element_type=jnp.float32)
            )
            grad_keys = grad_keys + jnp.einsum(
                "hqk,qhe->khe", grad_scores, q_block, preferred_element_type=jnp.float32
            )
        return (jnp.concatenate(grad_queries, axis=0), grad_keys, grad_values)

    return lax.map(one_sequence, (q_low, k_low, v_low, log_sums, grad_heads))


def forward(
    tokens,
    timestep,
    time_table,
    w_ada,
    b_ada,
    gain_one,
    w_qkv,
    w_out,
    gain_two,
    w_up,
    b_up,
    w_down,
    b_down,
):
    tok_rows = tokens.shape[0]
    group_heads = w_qkv.shape[2] // HD
    step_pick = (
        timestep[:, None] == jnp.arange(time_table.shape[0], dtype=jnp.int32)[None, :]
    ).astype(jnp.float32)
    picked = jnp.dot(step_pick, time_table, precision=highest)
    cond_low = jax.nn.silu(picked).astype(jnp.bfloat16)
    modulation = jnp.dot(cond_low, w_ada, preferred_element_type=jnp.float32) + b_ada
    positions = lax.axis_index("narrow") * tok_rows + jnp.arange(tok_rows, dtype=jnp.int32)
    row_pick = (positions[:, None] // LEN == jnp.arange(SEQS, dtype=jnp.int32)[None, :]).astype(
        jnp.float32
    )
    mod_tok = jnp.dot(row_pick, modulation, precision=highest).reshape(tok_rows, 6, D)
    residual_in = tokens.astype(jnp.float32)
    norm_one = layer_norm(residual_in, gain_one)
    normed_low = (norm_one * (1.0 + mod_tok[:, 1]) + mod_tok[:, 0]).astype(jnp.bfloat16)
    normed_all = lax.all_gather(normed_low, "narrow", axis=0, tiled=True)
    projected = jnp.einsum("td,kde->kte", normed_all, w_qkv, preferred_element_type=jnp.float32)
    shaped = projected.reshape(3, SEQS, LEN, group_heads, HD)
    cos_table, sin_table = rope_tables()
    q_low = rotate(shaped[0], cos_table, sin_table).astype(jnp.bfloat16)
    k_low = rotate(shaped[1], cos_table, sin_table).astype(jnp.bfloat16)
    v_low = shaped[2].astype(jnp.bfloat16)
    head_out, log_sums = attend(q_low, k_low, v_low)
    heads_low = head_out.astype(jnp.bfloat16).reshape(SEQS * LEN, group_heads * HD)
    attn_part = lax.psum_scatter(
        jnp.dot(
            lax.slice_in_dim(heads_low, 0, tok_rows * lax.axis_size("narrow"), axis=0),
            w_out,
            preferred_element_type=jnp.float32,
        ).astype(jnp.bfloat16),
        "narrow",
        scatter_dimension=0,
        tiled=True,
    ).astype(jnp.float32)
    mid_residual = residual_in + mod_tok[:, 2] * attn_part
    norm_two = layer_norm(mid_residual, gain_two)
    normed_two_low = (norm_two * (1.0 + mod_tok[:, 4]) + mod_tok[:, 3]).astype(jnp.bfloat16)
    normed_two_all = lax.all_gather(normed_two_low, "narrow", axis=0, tiled=True)
    pre_act = jnp.dot(normed_two_all, w_up, preferred_element_type=jnp.float32) + b_up
    act_low = jax.nn.gelu(pre_act, approximate=True).astype(jnp.bfloat16)
    branch = (
        lax.psum_scatter(
            jnp.dot(
                lax.slice_in_dim(act_low, 0, tok_rows * lax.axis_size("narrow"), axis=0),
                w_down,
                preferred_element_type=jnp.float32,
            ).astype(jnp.bfloat16),
            "narrow",
            scatter_dimension=0,
            tiled=True,
        ).astype(jnp.float32)
        + b_down
    )
    mixed = mid_residual + mod_tok[:, 5] * branch
    return (
        mixed,
        step_pick,
        picked,
        cond_low,
        row_pick,
        mod_tok,
        residual_in,
        norm_one,
        normed_all,
        q_low,
        k_low,
        v_low,
        log_sums,
        heads_low,
        attn_part,
        mid_residual,
        norm_two,
        normed_two_all,
        pre_act,
        act_low,
        branch,
    )


def body(
    tokens,
    timestep,
    token_mask,
    time_table,
    w_ada,
    b_ada,
    gain_one,
    w_qkv,
    w_out,
    gain_two,
    w_up,
    b_up,
    w_down,
    b_down,
    cotangent,
):
    weights = (
        time_table,
        w_ada,
        b_ada,
        gain_one,
        w_qkv,
        w_out,
        gain_two,
        w_up,
        b_up,
        w_down,
        b_down,
    )
    saved = forward(tokens, timestep, *weights)
    (
        mixed,
        step_pick,
        picked,
        cond_low,
        row_pick,
        mod_tok,
        residual_in,
        norm_one,
        normed_all,
        q_low,
        k_low,
        v_low,
        log_sums,
        heads_low,
        attn_part,
        mid_residual,
        norm_two,
        normed_two_all,
        pre_act,
        act_low,
        branch,
    ) = saved
    tok_rows = tokens.shape[0]
    group_heads = w_qkv.shape[2] // HD
    grad_mixed = cotangent.astype(jnp.float32) * token_mask.astype(jnp.float32)[:, None]
    grad_gate_two = grad_mixed * branch
    grad_branch = grad_mixed * mod_tok[:, 5]
    b_down_part = jnp.sum(grad_branch, axis=0)
    branch_all = lax.all_gather(grad_branch.astype(jnp.bfloat16), "narrow", axis=0, tiled=True)
    grad_w_down = jnp.einsum("tf,td->fd", act_low, branch_all, preferred_element_type=jnp.float32)
    grad_act = jnp.einsum("td,fd->tf", branch_all, w_down, preferred_element_type=jnp.float32)
    _, gelu_pull = jax.vjp(partial(jax.nn.gelu, approximate=True), pre_act)
    grad_pre_low = gelu_pull(grad_act)[0].astype(jnp.bfloat16)
    grad_b_up = jnp.sum(grad_pre_low, axis=0, dtype=jnp.float32)
    grad_w_up = jnp.einsum(
        "td,tf->df", normed_two_all, grad_pre_low, preferred_element_type=jnp.float32
    )
    grad_normed_two = lax.psum_scatter(
        jnp.einsum(
            "tf,df->td",
            lax.slice_in_dim(grad_pre_low, 0, tok_rows * lax.axis_size("narrow"), axis=0),
            w_up,
            preferred_element_type=jnp.float32,
        ).astype(jnp.bfloat16),
        "narrow",
        scatter_dimension=0,
        tiled=True,
    ).astype(jnp.float32)
    grad_res_two, gain_two_part = norm_back(
        mid_residual, gain_two, grad_normed_two * (1.0 + mod_tok[:, 4])
    )
    grad_mid = grad_mixed + grad_res_two
    grad_gate_one = grad_mid * attn_part
    attention_all = lax.all_gather(
        (grad_mid * mod_tok[:, 2]).astype(jnp.bfloat16), "narrow", axis=0, tiled=True
    )
    grad_w_out = jnp.einsum(
        "te,td->ed", heads_low, attention_all, preferred_element_type=jnp.float32
    )
    grad_heads = jnp.einsum("td,ed->te", attention_all, w_out, preferred_element_type=jnp.float32)
    grad_heads = grad_heads.astype(jnp.bfloat16).reshape(SEQS, LEN, group_heads, HD)
    grad_queries, grad_keys, grad_values = attend_back(q_low, k_low, v_low, log_sums, grad_heads)
    cos_table, sin_table = rope_tables()
    _, rope_pull = jax.vjp(lambda values: rotate(values, cos_table, sin_table), grad_queries)
    grad_projected = jnp.stack([rope_pull(grad_queries)[0], rope_pull(grad_keys)[0], grad_values])
    grad_projected = grad_projected.reshape(3, SEQS * LEN, group_heads * HD).astype(jnp.bfloat16)
    grad_w_qkv = jnp.einsum(
        "td,kte->kde", normed_all, grad_projected, preferred_element_type=jnp.float32
    )
    grad_normed = lax.psum_scatter(
        jnp.einsum("kte,kde->td", grad_projected, w_qkv, preferred_element_type=jnp.float32).astype(
            jnp.bfloat16
        ),
        "narrow",
        scatter_dimension=0,
        tiled=True,
    ).astype(jnp.float32)
    grad_res_one, gain_one_part = norm_back(
        residual_in, gain_one, grad_normed * (1.0 + mod_tok[:, 1])
    )
    grad_tokens = grad_mid + grad_res_one
    grad_mod_flat = jnp.stack(
        [
            grad_normed,
            grad_normed * norm_one,
            grad_gate_one,
            grad_normed_two,
            grad_normed_two * norm_two,
            grad_gate_two,
        ],
        axis=1,
    ).reshape(tok_rows, 6 * D)
    mod_part = jnp.einsum("ts,tm->sm", row_pick, grad_mod_flat, precision=highest)
    grad_modulation, grad_gain_one, grad_gain_two, grad_b_down = (
        lax.psum(mod_part.astype(jnp.bfloat16), "narrow").astype(jnp.float32),
        lax.psum(gain_one_part.astype(jnp.bfloat16), "narrow").astype(jnp.float32),
        lax.psum(gain_two_part.astype(jnp.bfloat16), "narrow").astype(jnp.float32),
        lax.psum(b_down_part.astype(jnp.bfloat16), "narrow").astype(jnp.float32),
    )
    all_modulation = lax.all_gather(grad_modulation, "wide", axis=0, tiled=True)
    all_steps = lax.all_gather(timestep, "wide", axis=0, tiled=True)
    all_pick = (
        all_steps[:, None] == jnp.arange(time_table.shape[0], dtype=jnp.int32)[None, :]
    ).astype(jnp.float32)
    all_picked = jnp.dot(all_pick, time_table, precision=highest)
    all_cond = jax.nn.silu(all_picked).astype(jnp.bfloat16)
    grad_b_ada = jnp.sum(all_modulation, axis=0)
    modulation_low = all_modulation.astype(jnp.bfloat16)
    grad_w_ada = jnp.einsum("sc,sm->cm", all_cond, modulation_low, preferred_element_type=jnp.float32)
    grad_condition = jnp.einsum(
        "sm,cm->sc", modulation_low, w_ada, preferred_element_type=jnp.float32
    )
    _, silu_pull = jax.vjp(jax.nn.silu, all_picked)
    grad_time_table = jnp.einsum(
        "sn,sc->nc", all_pick, silu_pull(grad_condition)[0], precision=highest
    )

    def reduce_low(values):
        return lax.psum(values.astype(jnp.bfloat16), "wide").astype(jnp.float32)

    grad_gain_one = reduce_low(grad_gain_one)
    grad_gain_two = reduce_low(grad_gain_two)
    grad_b_up = reduce_low(grad_b_up)
    grad_b_down = reduce_low(grad_b_down)
    grad_w_qkv = reduce_low(grad_w_qkv)
    grad_w_out = reduce_low(grad_w_out)
    grad_w_up = reduce_low(grad_w_up)
    grad_w_down = reduce_low(grad_w_down)
    return (
        mixed.astype(jnp.bfloat16),
        grad_tokens,
        grad_time_table,
        grad_w_ada,
        grad_b_ada,
        grad_gain_one,
        grad_w_qkv,
        grad_w_out,
        grad_gain_two,
        grad_w_up,
        grad_b_up,
        grad_w_down,
        grad_b_down,
    )


def solution(mesh):
    return jax.shard_map(
        body,
        mesh=mesh,
        in_specs=(
            P(("wide", "narrow"), None),
            P("wide"),
            P(("wide", "narrow")),
            P(),
            P(),
            P(),
            P(),
            P(None, None, "narrow"),
            P("narrow", None),
            P(),
            P(None, "narrow"),
            P("narrow"),
            P("narrow", None),
            P(),
            P(("wide", "narrow"), None),
        ),
        out_specs=(
            P(("wide", "narrow"), None),
            P(("wide", "narrow"), None),
            P(),
            P(),
            P(),
            P(),
            P(None, None, "narrow"),
            P("narrow", None),
            P(),
            P(None, "narrow"),
            P("narrow"),
            P("narrow", None),
            P(),
        ),
        check_vma=False,
    )
```

```python
import functools
import math

import jax
import jax.numpy as jnp
import numpy as np
from jax import lax
from jax.experimental import pallas as pl
from jax.experimental.pallas import tpu as pltpu
from jax.sharding import PartitionSpec as P

D = 768
HD = 64
LEN = 1024
ROWS_LOCAL = 512
SHARD_HEADS = 3
QKV_ROWS = 576
GRAD_ROWS = 2304
MESH = pl.DeviceIdType.MESH
f32 = jnp.float32
bf16 = jnp.bfloat16
norm_eps = 1e-06
highest = lax.Precision.HIGHEST

NN = (((1,), (0,)), ((), ()))
NT = (((1,), (1,)), ((), ()))
TN = (((0,), (0,)), ((), ()))

CHUNKS = {
    "d0": (0, 192),
    "d1": (192, 192),
    "d2": (384, 192),
    "d3": (576, 192),
    "u0": (768, 192),
    "u1": (960, 192),
    "u2": (1152, 192),
    "u3": (1344, 192),
    "o": (1536, 192),
    "q": (1728, 192),
    "k": (1920, 192),
    "v": (2112, 192),
}
ORDERS = {
    "d0": (1, 0, "y", 2),
    "d1": (1, 0, "y", 2),
    "d2": (0, 1, "y", 2),
    "d3": ("y", 0, 1, 2),
    "u0": ("y", 0, 1, 2),
    "u1": (0, 1, "y", 2),
    "u2": (0, 1, "y", 2),
    "u3": ("y", 0, 1, 2),
    "o": (0, 1, "y", 2),
    "q": (0, "y", 1, 2),
    "k": ("y", 0, 1, 2),
    "v": ("y", 1, 0, 2),
}
PIECES = {
    "q": (0, 1, 0, 1, 0, 1,),
    "o": (0,),
    "u": (1, 0, 1, 0,),
    "d": (1, 0, 1, 0,),
}
PLACES = (
    "n0", "n1", "p0", "p1", "a0", "a1", "a2", "wq", "p2", "p3", "a3", "a4", "a5", "wo", "o0", "o1", "u3",
    "wu", "u4", "u5", "u6", "u7", "f0", "f1", "f2", "wd", "f3", "f4", "f5", "f6", "f7", "f8", "h0", "h1",
    "h2", "b0", "b1", "b2", "bx", "b3", "b4", "b5", "by", "g0", "g1", "g2", "g3",
)
SCHEDULE = {
    "n1": (
        "Wq0",
    ),
    "p0": (
        "Wq1",
    ),
    "a0": (
        "Wq2",
    ),
    "a1": (
        "Wq3",
    ),
    "a2": (
        "Wq4", "Wq5",
    ),
    "p2": (
        "Wo0",
    ),
    "a3": (
        "Wu0",
    ),
    "a5": (
        "Wu1",
    ),
    "o1": (
        "Wu2",
    ),
    "u3": (
        "Wu3", "Wd0",
    ),
    "u4": (
        "Wd1",
    ),
    "u5": (
        "Wd2",
    ),
    "f0": (
        "Wd3", "d3",
    ),
    "f1": (
        "d2", "d1", "d0",
    ),
    "f4": (
        "u0", "u3", "d3",
    ),
    "f5": (
        "u2", "u1", "d1",
    ),
    "f6": (
        "d2",
    ),
    "f7": (
        "u0", "d3", "d0",
    ),
    "f8": (
        "d2",
    ),
    "h0": (
        "u2", "d3",
    ),
    "h1": (
        "u3", "o",
    ),
    "b0": (
        "d2", "u2", "re", "u1",
    ),
    "b1": (
        "u2", "re", "d3", "d1",
    ),
    "b2": (
        "d2", "u0", "u1", "d1",
    ),
    "bx": (
        "k", "v", "d0", "u2", "d3",
    ),
    "b3": (
        "d2", "u0", "u3", "u1",
    ),
    "b4": (
        "u2", "d1", "o", "re",
    ),
    "b5": (
        "u0", "u3", "d3",
    ),
    "by": (
        "k", "u1", "q", "o",
    ),
    "g0": (
        "d2", "re", "u0", "v", "d0",
    ),
    "g1": (
        "u2", "u3", "u1", "o", "d1",
    ),
    "g2": (
        "re", "rl",
    ),
    "g3": (
        "k", "v", "re", "rl", "d0", "u3", "q", "o", "d1", "u0", "k", "q", "o", "u1", "v", "rl", "k", "q", "d0",
        "rl", "v", "u3", "k", "o", "q", "v", "d0", "rl", "q", "k", "rl", "v", "q",
    ),
}


def chunk_stages(name, n_bits):
    rows = CHUNKS[name][1]
    out = []
    before_y = True
    order = [dim for dim in ORDERS[name] if dim == "y" or dim < n_bits]
    for dim in order + list(range(3, n_bits)):
        if dim == "y":
            out.append((dim, False, rows, False))
            before_y = False
        else:
            halved = rows % 32 == 0
            rows = rows // 2 if halved else rows
            out.append((dim, halved, rows, before_y))
    return out


def stage_rows(index, n_bits):
    total = 0
    for name in CHUNKS:
        _, _, rows, both = chunk_stages(name, n_bits)[index]
        total += 2 * rows if both else rows
    return total


def outbox_rows(n_bits):
    return sum(rows for name in CHUNKS for _, halved, rows, both in chunk_stages(name, n_bits) if halved and both)


def dot(left, right, dims):
    return lax.dot_general(left, right, dims, preferred_element_type=f32)


def loop(count, body):
    def step(index, carry):
        body(index)
        return carry

    lax.fori_loop(0, count, step, 0)


def rows_at(offset, size, align):
    if isinstance(offset, int):
        return pl.ds(offset, size)
    return pl.ds(pl.multiple_of(offset, align), size)


def normalize(values):
    centered = values - jnp.mean(values, axis=-1, keepdims=True)
    variance = jnp.mean(centered * centered, axis=-1, keepdims=True)
    inverse = lax.rsqrt(variance + norm_eps)
    return centered * inverse, inverse


def norm_grad(vhat, inverse, e_hat):
    mean_e = jnp.mean(e_hat, axis=-1, keepdims=True)
    mean_ev = jnp.mean(e_hat * vhat, axis=-1, keepdims=True)
    return inverse * (e_hat - mean_e - vhat * mean_ev)


def block_kernel(
    n_bits,
    tok_in, cot_in, mask_in, step_in, table_in, w_ada_in, b_ada_in, gain_one_in, wqkv_in, wout_in, gain_two_in,
    wup_in, bup_in, wdown_in, b_down_in, cos_in, sin_in,
    mixed_out, grad_tok_out, gathered_out, grads_out,
    tok, cot, gb, n2, normed, wqkv, wout, wup, wdown, proj, ho, do, lse, attn, mid, part, hidden, gel,
    grad_mid, send_a, recv_a, recv_b, recv_c, acc, oth, stage,
    mod, vec, bup, ada_line, lines, mask_line, cos_t, sin_t, sums, sums_recv, sums_low,
    ssem, rsem, lsem, *stage_recv,
):
    wide = lax.axis_index("wide")
    narrow = lax.axis_index("narrow")
    core = lax.rem(narrow, 2)
    chip_y = lax.div(narrow, 2)
    sib = (wide, narrow + 1 - 2 * core)
    across = (wide, lax.rem(narrow + 2, 4))

    def wide_bit(level):
        return lax.rem(lax.div(wide, 1 << level), 2)

    def wide_peer(level):
        return (wide + (1 << level) * (1 - 2 * wide_bit(level)), narrow)

    peers = [sib, across] + [wide_peer(level) for level in range(n_bits)]
    own0 = core * ROWS_LOCAL
    sib0 = (1 - core) * ROWS_LOCAL

    n_sems = {"remote": 0, "local": 0}

    def remote(src, dst, peer):
        at = n_sems["remote"]
        n_sems["remote"] += 1
        return pltpu.make_async_remote_copy(
            src_ref=src, dst_ref=dst, send_sem=ssem.at[at], recv_sem=rsem.at[at],
            device_id=peer, device_id_type=MESH,
        )

    def local(src, dst):
        at = n_sems["local"]
        n_sems["local"] += 1
        return pltpu.make_async_copy(src, dst, lsem.at[at])

    c_tok = local(tok_in, tok)
    c_cot = local(cot_in, cot)
    c_small = [
        local(b_ada_in, ada_line),
        local(gain_one_in, lines[0]),
        local(gain_two_in, lines[1]),
        local(b_down_in, lines[2]),
        local(bup_in, bup[0]),
        local(mask_in, mask_line),
        local(cos_in, cos_t),
        local(sin_in, sin_t),
    ]
    c_wqkv = local(wqkv_in, wqkv.at[0])
    c_wout = local(wout_in, wout.at[pl.ds(0, 192)])
    c_wup = local(wup_in, wup.at[:, pl.ds(0, D)])
    c_wdown = local(wdown_in, wdown.at[pl.ds(0, D)])
    c_tok.start()
    for copy in c_small:
        copy.start()
    c_wqkv.start()
    c_cot.start()
    c_wout.start()
    c_wup.start()
    c_wdown.start()

    barrier = pltpu.get_barrier_semaphore()
    for peer in peers:
        pl.semaphore_signal(barrier, inc=1, device_id=peer, device_id_type=MESH)
    pl.semaphore_wait(barrier, len(peers))

    r_tok = remote(tok_in, n2.at[rows_at(own0, ROWS_LOCAL, 512)], sib)
    r_cot = remote(cot, gb.at[rows_at(own0, ROWS_LOCAL, 512)], sib)
    r_tok.start()

    places = {
        "q": (wqkv_in, lambda rows: wqkv.at[1, rows], QKV_ROWS, 0),
        "o": (wout_in, lambda rows: wout.at[rows], 192, 192),
        "u": (wup_in, lambda rows: wup.at[rows, pl.ds(D, D)], D, 0),
        "d": (wdown_in, lambda rows: wdown.at[rows], D, D),
    }
    w_across, w_along, plans = {}, {}, {}
    piece_keys = []
    for matrix in PIECES:
        source, target, total_rows, shift = places[matrix]
        count = len(PIECES[matrix])
        size = total_rows // (2 * count)
        for piece in range(count):
            level = PIECES[matrix][piece]
            row = 2 * size * piece + wide_bit(level) * size
            here = target(rows_at(shift + row, size, 16))
            key = "W" + matrix + str(piece)
            piece_keys.append(key)
            w_across[key] = remote(source.at[rows_at(row, size, 16)], here, across)
            w_along[key] = remote(here, here, wide_peer(level))
    ahead = 6

    def forward_piece(at):
        w_across[piece_keys[at]].wait_recv()
        w_along[piece_keys[at]].start()
        if at + ahead < len(piece_keys):
            w_across[piece_keys[at + ahead]].start()

    for at, key in enumerate(piece_keys):
        plans[key] = [functools.partial(forward_piece, at)]
    r_bup = remote(bup_in, bup[1], across)
    for key in piece_keys[:ahead]:
        w_across[key].start()
    r_bup.start()

    def segment(name, index):
        offset, rows = CHUNKS[name]
        for dim, halved, count, _ in chunk_stages(name, n_bits)[:index]:
            if halved:
                offset = offset + wide_bit(dim) * count
                rows = count
        return offset, rows

    stage_copies, back_copies, stage_base, returns, final_copies, outbox = {}, {}, {}, {}, {}, {}
    stage_rows_used = 0
    n_stages = n_bits + 1
    for index in range(n_stages):
        base = 0
        for name in CHUNKS:
            dim, halved, count, both = chunk_stages(name, n_bits)[index]
            offset, _ = segment(name, index)
            stage_base[name, index] = base
            if dim == "y":
                sent, peer = [oth], across
            else:
                sent, peer = [acc, oth] if both else [acc], wide_peer(dim)
                if halved:
                    offset = offset + (1 - wide_bit(dim)) * count
            copies = []
            for array in sent:
                landing = stage_recv[index].at[pl.ds(base, count)]
                source = array.at[rows_at(offset, count, 16)]
                if halved and array is acc:
                    if both:
                        outbox[name, index] = (stage, stage_rows_used)
                        source = stage.at[pl.ds(stage_rows_used, count)]
                        stage_rows_used += count
                    else:
                        outbox[name, index] = (oth, offset)
                        source = oth.at[rows_at(offset, count, 16)]
                copies.append(remote(source, landing, peer))
                base += count
            stage_copies[name, index] = copies
            if halved:
                offset, count = segment(name, index + 1)
                rows = acc.at[rows_at(offset, count, 16)]
                back_copies[name, index] = remote(rows, rows, peer)
    for name in CHUNKS:
        returns[name] = [at for at in range(n_stages) if (name, at) in back_copies]
        first, count = CHUNKS[name]
        final_copies[name] = local(acc.at[pl.ds(first, count)], grads_out.at[pl.ds(first, count)])

    def start_stage(name, index):
        if index == 0 and (name, 0) in outbox:
            offset, _ = segment(name, 0)
            dim, _, count, _ = chunk_stages(name, n_bits)[0]
            box, row0 = outbox[name, 0]
            box[pl.ds(row0, count), :] = acc[rows_at(offset + (1 - wide_bit(dim)) * count, count, 16), :]
        for copy in stage_copies[name, index]:
            copy.start()

    def merge_step(name, index):
        for copy in stage_copies[name, index - 1]:
            copy.wait()
        offset, rows = segment(name, index)
        both_before = len(stage_copies[name, index - 1]) == 2
        base = stage_base[name, index - 1]
        brought = stage_recv[index - 1]

        def merge(array, row0, count, box=None):
            start = base + rows if array is oth else base
            step = 48 if count % 48 == 0 else 16
            target, target0 = box or (array, row0)

            def one(at):
                row = row0 + step * at
                here = rows_at(row, step, 16)
                value = array[here, :].astype(f32) + brought[rows_at(start + row - offset, step, 16), :].astype(f32)
                target[rows_at(target0 + step * at, step, 16), :] = value.astype(bf16)

            loop(count // step, one)

        arrays = [acc, oth] if both_before else [acc]
        if index == n_stages:
            merge(acc, offset, rows)
            back_copies[name, returns[name][-1]].start()
            return
        dim, halved, count, _ = chunk_stages(name, n_bits)[index]
        if dim == "y":
            for array in reversed(arrays):
                merge(array, offset, rows)
                if array is oth or not both_before:
                    start_stage(name, index)
        elif halved:
            for array in arrays:
                box = outbox[name, index] if array is acc else None
                merge(array, offset + (1 - wide_bit(dim)) * count, count, box)
            start_stage(name, index)
            for array in arrays:
                merge(array, offset + wide_bit(dim) * count, count)
        else:
            merge(acc, offset, rows)
            start_stage(name, index)

    def back_step(name, at):
        back_copies[name, returns[name][at]].wait()
        if at > 0:
            back_copies[name, returns[name][at - 1]].start()
        else:
            final_copies[name].start()

    for name in CHUNKS:
        plan = [functools.partial(start_stage, name, 0)]
        plan += [functools.partial(merge_step, name, index + 1) for index in range(n_stages)]
        plan += [functools.partial(back_step, name, at) for at in reversed(range(len(returns[name])))]
        plans[name] = plan

    place = 2 * wide + chip_y
    r_sib, row_copies, own_rows = [], [], []
    for part_index in range(2):
        mine = gathered_out.at[part_index, core]
        r_sib.append(remote(sums.at[part_index], sums_recv.at[part_index], sib))
        own_rows.append(local(sums_low.at[part_index], mine.at[place]))
        copies = [remote(sums_low.at[part_index], mine.at[place], across)]
        for level in range(n_bits):
            count = 2 << level
            rows = mine.at[pl.ds(lax.div(place, count) * count, count)]
            copies.append(remote(rows, rows, wide_peer(level)))
        copies.append(remote(mine, mine, sib))
        row_copies.append(copies)

    def row_step(part_index, at):
        if at == 0:
            own_rows[part_index].start()
        if at == 1:
            own_rows[part_index].wait()
        if at > 0:
            row_copies[part_index][at - 1].wait()
        if at < n_bits + 2:
            row_copies[part_index][at].start()

    for part_index, key in enumerate(("re", "rl")):
        plans[key] = [functools.partial(row_step, part_index, at) for at in range(n_bits + 3)]

    def sums_ready(part_index):
        r_sib[part_index].wait()
        cols = rows_at(core * 384, 384, 128)
        total = sums[part_index, :, cols] + sums_recv[part_index, :, cols]
        sums_low[part_index] = total.astype(bf16)

    steps_at = {}
    for name in PLACES:
        if name[0] == "w":
            keys = [key for key in piece_keys if key[1] == name[1]]
            steps_at[name] = [step for key in keys for step in plans.pop(key)]
        else:
            steps_at[name] = [plans[key].pop(0) for key in SCHEDULE.get(name, ()) if plans.get(key)]
    while any(plans.values()):
        steps_at["g3"] += [plans[key].pop(0) for key in plans if plans[key]]

    def point(name):
        for step in steps_at[name]:
            step()

    def need(matrix):
        point("w" + matrix)
        for key in piece_keys:
            if key[1] == matrix:
                w_along[key].wait_recv()

    for copy in c_small:
        copy.wait()
    time_step = step_in[chip_y]
    for row in range(3):
        vec[row : row + 1, :] = lines[row][...].reshape(1, D)

    def modulation(table, w_ada):
        copies = [local(table_in, table), local(w_ada_in, w_ada)]
        for copy in copies:
            copy.start()
        for copy in copies:
            copy.wait()
        picked = table[pl.ds(time_step, 1), :]
        cond = picked / (1.0 + jnp.exp(-picked))
        cond = jnp.broadcast_to(cond, (16, 128)).astype(bf16)
        for index in range(6):
            flat = dot(cond, w_ada[:, index * D : (index + 1) * D], NN)
            mod[index : index + 1, :] = ada_line[pl.ds(index * D, D)].reshape(1, D) + flat[0:1, :]

    pl.run_scoped(modulation, pltpu.VMEM((1000, 128), f32), pltpu.VMEM((128, 6 * D), bf16))

    def first_norm(source, src0, dst0):
        def one(index):
            values = source[rows_at(src0 + 128 * index, 128, 128), :].astype(f32)
            vhat, _ = normalize(values)
            out = vhat * vec[0:1, :] * (1.0 + mod[1:2, :]) + mod[0:1, :]
            normed[rows_at(dst0 + 128 * index, 128, 128), :] = out.astype(bf16)

        loop(4, one)

    c_tok.wait()
    first_norm(tok, 0, own0)
    point("n0")
    r_tok.wait_recv()
    first_norm(n2, sib0, sib0)
    c_cot.wait()
    mask = jnp.broadcast_to(mask_line[...].astype(f32).reshape(1, ROWS_LOCAL), (8, ROWS_LOCAL)).T[:, 0:1]
    cot[...] = (cot[...].astype(f32) * mask).astype(bf16)
    r_cot.start()
    point("n1")

    def project(shard):
        def one(index):
            cols = rows_at(256 * index, 256, 256)
            flat = dot(wqkv[shard], normed[cols, :], NT)
            cos_b, sin_b = cos_t[:, cols], sin_t[:, cols]
            for kind in (0, 1):
                scale = 0.125 if kind == 0 else 1.0
                for head in range(SHARD_HEADS):
                    at = kind * 192 + head * HD
                    low, high = flat[at : at + 32], flat[at + 32 : at + 64]
                    proj[shard, at : at + 32, cols] = ((low * cos_b - high * sin_b) * scale).astype(bf16)
                    proj[shard, at + 32 : at + 64, cols] = ((high * cos_b + low * sin_b) * scale).astype(bf16)
            proj[shard, 384:576, cols] = flat[384:576].astype(bf16)
            point_in("p", 2 * shard + lax.div(index, 2), lax.rem(index, 2) == 1, 4)

        loop(4, one)

    def point_in(prefix, index, last, count):
        for place in range(count):
            if steps_at.get(prefix + str(place)) and (prefix, place) != ("u", 3):

                @pl.when((index == place) & last)
                def _():
                    point(prefix + str(place))

    def head_rows(kind, head):
        return rows_at(kind * 192 + head * HD, HD, HD)

    def attend(shard, head):
        q_t = proj[shard, head_rows(0, head), :]
        k_t = proj[shard, head_rows(1, head), :]
        v_t = proj[shard, head_rows(2, head), :]
        scores = dot(k_t, q_t, TN)
        top = jnp.max(scores, axis=0, keepdims=True)
        weights = jnp.exp(scores - top)
        total = jnp.sum(weights, axis=0, keepdims=True)
        out = dot(v_t, weights.astype(bf16), NN) * (1.0 / total)
        index = shard * SHARD_HEADS + head
        ho[rows_at(index * HD, HD, HD), :] = out.astype(bf16)
        lse[index, 0:1, :] = top + jnp.log(total)

    c_wqkv.wait()

    def shard_heads(shard):
        @pl.when(shard == 1)
        def _():
            need("q")

        project(shard)

        def one(head):
            attend(shard, head)
            point_in("a", SHARD_HEADS * shard + head, True, 6)

        loop(SHARD_HEADS, one)

    loop(2, shard_heads)

    c_wout.wait()
    need("o")
    half = 256

    def exchange_start(recv, index):
        rows = pl.ds(half * index, half)
        copy = remote(send_a.at[rows], recv.at[rows], sib)
        copy.start()
        return copy

    r_attn = []
    for index in range(2):
        out = dot(ho[:, rows_at(sib0 + half * index, half, half)], wout[...], TN)
        send_a[half * index : half * (index + 1), :] = out.astype(bf16)
        r_attn.append(exchange_start(recv_a, index))
    for index in range(2):
        out = dot(ho[:, rows_at(own0 + half * index, half, half)], wout[...], TN)
        attn[half * index : half * (index + 1), :] = out
    point("o0")
    r_n2 = []
    for index in range(2):
        r_attn[index].wait_recv()

        def second_norm(sub):
            rows = rows_at(half * index + 128 * sub, 128, 128)
            value = attn[rows, :] + recv_a[rows, :].astype(f32)
            attn[rows, :] = value
            residual = tok[rows, :].astype(f32) + mod[2:3, :] * value
            mid[rows, :] = residual
            vhat, _ = normalize(residual)
            out = vhat * vec[1:2, :] * (1.0 + mod[4:5, :]) + mod[3:4, :]
            n2[rows_at(own0 + half * index + 128 * sub, 128, 128), :] = out.astype(bf16)

        loop(2, second_norm)
        rows = rows_at(own0 + half * index, half, half)
        r_n2.append(remote(n2.at[rows], n2.at[rows], sib))
        r_n2[index].start()
        r_attn[index].wait_send()

    r_cot.wait_recv()

    def branch_grad(index):
        rows = rows_at(own0 + 128 * index, 128, 128)
        part_rows = rows_at(128 * index, 128, 128)
        gb[rows, :] = (cot[part_rows, :].astype(f32) * mod[5:6, :]).astype(bf16)
        rows = rows_at(sib0 + 128 * index, 128, 128)
        gb[rows, :] = (gb[rows, :].astype(f32) * mod[5:6, :]).astype(bf16)

    r_cot.wait_send()
    loop(4, branch_grad)
    point("o1")

    c_wup.wait()
    r_bup.wait_recv()
    for row in range(2):
        vec[4 + row : 5 + row, :] = bup[row][...].reshape(1, D)
    gelu_c = math.sqrt(2.0 / math.pi)

    def up(index):
        shard = lax.div(index, 4)
        block = lax.rem(index, 4)

        @pl.when(index == 2)
        def _():
            r_n2[0].wait_recv()
            r_n2[1].wait_recv()

        @pl.when(index == 4)
        def _():
            point("u3")
            need("u")

        rows = rows_at(lax.rem(own0 + 256 * block, LEN), 256, 256)
        cols = rows_at(shard * D, D, D)
        pre = dot(n2[rows, :], wup[:, cols], NN) + vec[pl.ds(4 + shard, 1), :]
        square = pre * pre
        squash = jnp.tanh(gelu_c * pre * (1.0 + 0.044715 * square))
        gate = 0.5 * (1.0 + squash)
        hidden[rows, cols] = (pre * gate).astype(bf16)
        slope = gate + 0.5 * pre * (1.0 - squash * squash) * (gelu_c * (1.0 + 3.0 * 0.044715 * square))
        gel[rows, cols] = slope.astype(bf16)

        point_in("u", index, True, 8)

    loop(8, up)

    def w_down_grad(shard, target, base):
        def one(index):
            cols = rows_at(shard * D + 256 * index, 256, 256)
            out = dot(hidden[:, cols], gb[...], TN)
            target[rows_at(base + 256 * index, 256, 256), :] = out.astype(bf16)

        loop(3, one)

    w_down_grad(1, oth, 0)
    point("f0")
    w_down_grad(0, acc, 0)
    point("f1")

    sums[...] = jnp.zeros_like(sums)
    c_wdown.wait()

    def hidden_grad(shard, row):
        def one(index):
            rows = rows_at(256 * index, 256, 256)
            cols = pl.ds(shard * D, D)
            grad_act = dot(gb[rows, :], wdown[pl.ds(shard * D, D), :], NT)
            low = (grad_act * gel[rows, cols].astype(f32)).astype(bf16)
            gel[rows, cols] = low
            line = pl.ds(row, 1)
            sums[1, line, :] = sums[1, line, :] + jnp.sum(low.astype(f32), axis=0, keepdims=True)

        loop(4, one)

    def w_up_grad(shard, target):
        def one(index):
            cols = rows_at(256 * index, 256, 256)
            out = dot(n2[:, cols], gel[:, pl.ds(shard * D, D)], TN)
            target[rows_at(D + 256 * index, 256, 256), :] = out.astype(bf16)

        loop(3, one)

    hidden_grad(0, 3 + narrow)
    point("f2")
    need("d")
    hidden_grad(1, 3 + lax.rem(narrow + 2, 4))
    point("f3")
    w_up_grad(1, oth)
    point("f4")
    w_up_grad(0, acc)
    point("f5")

    r_gn2 = []
    for index in range(2):
        out = dot(gel[rows_at(sib0 + half * index, half, half), :], wup[...], NT)
        send_a[half * index : half * (index + 1), :] = out.astype(bf16)
        r_gn2.append(exchange_start(recv_b, index))
    for index in range(2):
        out = dot(gel[rows_at(own0 + half * index, half, half), :], wup[...], NT)
        part[half * index : half * (index + 1), :] = out
    point("f6")

    r_ga = []
    for index in range(2):
        r_gn2[index].wait()

        def second_back(sub):
            rows = rows_at(half * index + 128 * sub, 128, 128)
            upstream = part[rows, :] + recv_b[rows, :].astype(f32)
            vhat, inverse = normalize(mid[rows, :])
            scaled = upstream * (1.0 + mod[4:5, :])
            grad_mixed = cot[rows, :].astype(f32)
            value = grad_mixed + norm_grad(vhat, inverse, scaled * vec[1:2, :])
            grad_mid[rows, :] = value
            gb[rows_at(own0 + half * index + 128 * sub, 128, 128), :] = (value * mod[2:3, :]).astype(bf16)
            add_sum(0, 0, value * attn[rows, :])
            add_sum(0, 1, upstream)
            add_sum(0, 2, upstream * (vhat * vec[1:2, :]))
            add_sum(0, 4, scaled * vhat)
            add_sum(0, 5, grad_mixed * mod[5:6, :])

        def add_sum(part_index, row, values):
            line = slice(row, row + 1)
            sums[part_index, line, :] = sums[part_index, line, :] + jnp.sum(values, axis=0, keepdims=True)

        loop(2, second_back)
        rows = rows_at(own0 + half * index, half, half)
        r_ga.append(remote(gb.at[rows], gb.at[rows], sib))
        r_ga[index].start()
    point("f7")

    r_branch = []
    for index in range(2):
        out = dot(hidden[rows_at(sib0 + half * index, half, half), :], wdown[...], NN)
        send_a[half * index : half * (index + 1), :] = out.astype(bf16)
        r_branch.append(exchange_start(recv_c, index))
    for index in range(2):
        out = dot(hidden[rows_at(own0 + half * index, half, half), :], wdown[...], NN)
        part[half * index : half * (index + 1), :] = out
    point("f8")

    r_ga[0].wait_recv()
    r_ga[1].wait_recv()

    def head_grad(index):
        cols = rows_at(256 * index, 256, 256)
        do[:, cols] = dot(wout[...], gb[cols, :], NT).astype(bf16)

    loop(4, head_grad)
    point("h0")
    oth[1536:1728, :] = dot(ho[192:384, :], gb[...], NN).astype(bf16)
    acc[1536:1728, :] = dot(ho[0:192, :], gb[...], NN).astype(bf16)
    point("h1")

    def finish_branch(index):
        rows = rows_at(128 * index, 128, 128)
        branch = part[rows, :] + recv_c[rows, :].astype(f32) + vec[2:3, :]
        add_sum(0, 3, cot[rows, :].astype(f32) * branch)
        send_a[rows, :] = (mid[rows, :] + mod[5:6, :] * branch).astype(bf16)

    r_branch[0].wait()
    r_branch[1].wait()
    loop(4, finish_branch)
    c_mixed = local(send_a, mixed_out)
    c_mixed.start()
    on_first = (1 - core).astype(f32)
    high = lax.div(time_step, 32)
    sums[0, 6:7, :] = jnp.full((1, D), high.astype(f32) * on_first)
    sums[0, 7:8, :] = jnp.full((1, D), (time_step - 32 * high).astype(f32) * on_first)
    r_sib[0].start()
    point("h2")

    def attend_back(shard, head):
        q_t = proj[shard, head_rows(0, head), :]
        k_t = proj[shard, head_rows(1, head), :]
        v_t = proj[shard, head_rows(2, head), :]
        index = shard * SHARD_HEADS + head
        d_t = do[rows_at(index * HD, HD, HD), :]
        probs = jnp.exp(dot(k_t, q_t, TN) - lse[index, 0:1, :])
        grad_probs = dot(v_t, d_t, TN)
        inner = jnp.sum(probs * grad_probs, axis=0, keepdims=True)
        grad_scores = (probs * (grad_probs - inner)).astype(bf16)
        dq_t = dot(k_t, grad_scores, NN) * 0.125
        dk_t = dot(grad_scores, q_t, NT).T
        dv_t = dot(probs.astype(bf16), d_t, NT).T
        for kind, grad in ((0, dq_t), (1, dk_t)):
            low, high = grad[:32], grad[32:]
            turned = jnp.concatenate(
                [low * cos_t[...] + high * sin_t[...], high * cos_t[...] - low * sin_t[...]], axis=0
            )
            proj[shard, head_rows(kind, head), :] = turned.astype(bf16)
        proj[shard, head_rows(2, head), :] = dv_t.astype(bf16)

    for key in piece_keys:
        w_along[key].wait_send()
        w_across[key].wait_send()

    def w_qkv_grad(shard, target):
        def one(index):
            rows = rows_at(192 * index, 192, 64)
            out = dot(proj[shard, rows, :], normed[...], NN)
            target[rows_at(1728 + 192 * index, 192, 64), :] = out.astype(bf16)

        loop(3, one)

    def back_heads(index):
        shard = 1 - lax.div(index, SHARD_HEADS)
        head = lax.rem(index, SHARD_HEADS)
        attend_back(shard, head)

        @pl.when(index == 0)
        def _():
            sums_ready(0)

        point_in("b", index, True, 6)

        @pl.when(index == 2)
        def _():
            w_qkv_grad(1, oth)
            point("bx")

    loop(6, back_heads)
    w_qkv_grad(0, acc)
    point("by")

    def normed_grad(offset):
        first = dot(proj[0, :, offset], wqkv[0], TN)
        return first + dot(proj[1, :, offset], wqkv[1], TN)

    c_mixed.wait()
    r_gn = []
    for index in range(2):
        send_a[half * index : half * (index + 1), :] = normed_grad(
            rows_at(sib0 + half * index, half, half)
        ).astype(bf16)
        r_gn.append(exchange_start(recv_a, index))
    for index in range(2):
        part[half * index : half * (index + 1), :] = normed_grad(rows_at(own0 + half * index, half, half))
    point("g0")
    for index in range(2):
        r_gn[index].wait()

        def first_back(sub):
            rows = rows_at(half * index + 128 * sub, 128, 128)
            upstream = part[rows, :] + recv_a[rows, :].astype(f32)
            vhat, inverse = normalize(tok[rows, :].astype(f32))
            scaled = upstream * (1.0 + mod[1:2, :])
            part[rows, :] = grad_mid[rows, :] + norm_grad(vhat, inverse, scaled * vec[0:1, :])
            add_sum(1, 0, upstream)
            add_sum(1, 1, upstream * (vhat * vec[0:1, :]))
            add_sum(1, 2, scaled * vhat)

        loop(2, first_back)
    c_grad_tok = local(part, grad_tok_out)
    c_grad_tok.start()

    r_sib[1].start()
    point("g1")
    sums_ready(1)
    point("g2")
    point("g3")
    for name in CHUNKS:
        final_copies[name].wait()
    c_grad_tok.wait()
    for copy in [r_tok, r_bup] + r_n2 + r_ga:
        copy.wait_send()


def fused_block(n_wide, tokens, cot, mask, timestep, table, w_ada, b_ada, gain_one, w_qkv_t, w_out, gain_two, w_up, b_up,
                w_down, b_down, cos_t, sin_t):
    n_bits = n_wide.bit_length() - 1
    any_space = pl.BlockSpec(memory_space=pl.ANY)
    scratch = [
        pltpu.VMEM((ROWS_LOCAL, D), bf16),
        pltpu.VMEM((ROWS_LOCAL, D), bf16),
        pltpu.VMEM((LEN, D), bf16),
        pltpu.VMEM((LEN, D), bf16),
        pltpu.VMEM((LEN, D), bf16),
        pltpu.VMEM((2, QKV_ROWS, D), bf16),
        pltpu.VMEM((384, D), bf16),
        pltpu.VMEM((D, 2 * D), bf16),
        pltpu.VMEM((2 * D, D), bf16),
        pltpu.VMEM((2, QKV_ROWS, LEN), bf16),
        pltpu.VMEM((384, LEN), bf16),
        pltpu.VMEM((384, LEN), bf16),
        pltpu.VMEM((6, 8, LEN), f32),
        pltpu.VMEM((ROWS_LOCAL, D), f32),
        pltpu.VMEM((ROWS_LOCAL, D), f32),
        pltpu.VMEM((ROWS_LOCAL, D), f32),
        pltpu.VMEM((LEN, 2 * D), bf16),
        pltpu.VMEM((LEN, 2 * D), bf16),
        pltpu.VMEM((ROWS_LOCAL, D), f32),
        pltpu.VMEM((ROWS_LOCAL, D), bf16),
        pltpu.VMEM((ROWS_LOCAL, D), bf16),
        pltpu.VMEM((ROWS_LOCAL, D), bf16),
        pltpu.VMEM((ROWS_LOCAL, D), bf16),
        pltpu.VMEM((GRAD_ROWS, D), bf16),
        pltpu.VMEM((GRAD_ROWS, D), bf16),
        pltpu.VMEM((outbox_rows(n_bits), D), bf16),
        pltpu.VMEM((8, D), f32),
        pltpu.VMEM((8, D), f32),
        [pltpu.VMEM((D,), f32)] * 2,
        pltpu.VMEM((6 * D,), f32),
        [pltpu.VMEM((D,), f32)] * 3,
        pltpu.VMEM((ROWS_LOCAL,), jnp.int32),
        pltpu.VMEM((32, LEN), f32),
        pltpu.VMEM((32, LEN), f32),
        pltpu.VMEM((2, 8, D), f32),
        pltpu.VMEM((2, 8, D), f32),
        pltpu.VMEM((2, 8, D // 2), bf16),
        pltpu.SemaphoreType.DMA((240,)),
        pltpu.SemaphoreType.DMA((240,)),
        pltpu.SemaphoreType.DMA((48,)),
    ]
    for index in range(n_bits + 1):
        scratch.append(pltpu.VMEM((stage_rows(index, n_bits), D), bf16))
    specs = [any_space] * 17
    specs[3] = pl.BlockSpec(memory_space=pltpu.SMEM)
    return pl.pallas_call(
        functools.partial(block_kernel, n_bits),
        out_shape=(
            jax.ShapeDtypeStruct((ROWS_LOCAL, D), bf16),
            jax.ShapeDtypeStruct((ROWS_LOCAL, D), f32),
            jax.ShapeDtypeStruct((2, 2, 2 * n_wide, 8, D // 2), bf16),
            jax.ShapeDtypeStruct((GRAD_ROWS, D), bf16),
        ),
        in_specs=specs,
        out_specs=[any_space] * 4,
        scratch_shapes=scratch,
        compiler_params=pltpu.CompilerParams(
            collective_id=0, has_side_effects=True, vmem_limit_bytes=60 * 1024 * 1024
        ),
    )(tokens, cot, mask, timestep, table, w_ada, b_ada, gain_one, w_qkv_t, w_out, gain_two, w_up, b_up, w_down, b_down,
      cos_t, sin_t)


def finish_kernel(
    gathered_in, table_in, w_ada_in, grads_in, mixed_in, grad_tok_in,
    mixed_out, grad_tok_out, g_table, g_w_ada, g_b_ada, g_gain_one, g_wqkv, g_wout, g_gain_two, g_wup, g_bup,
    g_wdown, g_b_down,
    gathered, table, w_ada, grads, mod_low, table_out, ada_out, wide_out, late_sum, mixed_buf, tok_buf, lines, sem,
):
    pieces = GRAD_ROWS // 192
    targets = [(g_wdown, 0), (g_wup, 768), (g_wout, 1536), (g_wqkv, 1728)]
    loads = [(gathered_in, gathered), (table_in, table), (w_ada_in, w_ada)]
    loads = [pltpu.make_async_copy(src, dst, sem.at[at]) for at, (src, dst) in enumerate(loads)]
    pass_in = [
        pltpu.make_async_copy(mixed_in, mixed_buf, sem.at[3]),
        pltpu.make_async_copy(grad_tok_in, tok_buf, sem.at[4]),
    ]
    pass_out = [
        pltpu.make_async_copy(mixed_buf, mixed_out, sem.at[5]),
        pltpu.make_async_copy(tok_buf, grad_tok_out, sem.at[6]),
    ]
    grad_in, grad_out = [], []
    for piece in range(pieces):
        rows = pl.ds(192 * piece, 192)
        grad_in.append(pltpu.make_async_copy(grads_in.at[rows], grads.at[rows], sem.at[7 + piece]))
        target, first = [item for item in targets if item[1] <= 192 * piece][-1]
        grad_out.append(
            pltpu.make_async_copy(
                wide_out.at[rows], target.at[pl.ds(192 * piece - first, 192)], sem.at[7 + pieces + piece]
            )
        )
    for copy in loads + pass_in + grad_in:
        copy.start()
    for copy in loads:
        copy.wait()

    def both(index):
        return jnp.concatenate([gathered[index, 0].astype(f32), gathered[index, 1].astype(f32)], axis=-1)

    early, late = both(0), both(1)
    total_early, total_late = jnp.sum(early, axis=0), jnp.sum(late, axis=0)
    late_sum[...] = total_late
    for row, values in enumerate([late[:, 0], late[:, 1], early[:, 0], early[:, 1], early[:, 2], early[:, 3]]):
        mod_low[:, row * D : (row + 1) * D] = values.astype(bf16)
    rows = [total_late[0:1], total_late[1:2]] + [total_early[row : row + 1] for row in range(4)]
    for row, values in enumerate(rows):
        lines[0][pl.ds(row * D, D)] = values.reshape(D)
    lines[1][...] = total_late[2:3].reshape(D)
    lines[2][...] = total_early[4:5].reshape(D)
    lines[3][...] = late_sum[pl.ds(3 + lax.axis_index("narrow"), 1), :].reshape(D)
    lines[4][...] = total_early[5:6].reshape(D)
    line_out = [
        pltpu.make_async_copy(line, out, sem.at[7 + 2 * pieces + at])
        for at, (line, out) in enumerate(zip(lines, (g_b_ada, g_gain_one, g_gain_two, g_bup, g_b_down)))
    ]
    for copy in line_out:
        copy.start()
    seqs, steps = early.shape[0], table.shape[0]
    time_step = early[:, 6, 0:1] * 32.0 + early[:, 7, 0:1]
    columns = lax.broadcasted_iota(jnp.int32, (seqs, steps), 1).astype(f32)
    pick = jnp.where(columns == time_step, 1.0, 0.0).astype(f32)
    picked = lax.dot_general(pick, table[...], NN, precision=highest, preferred_element_type=f32)
    gate = 1.0 / (1.0 + jnp.exp(-picked))
    cond = (picked * gate).astype(bf16)
    ada_out[...] = dot(cond, mod_low[...], TN)
    out_ada = pltpu.make_async_copy(ada_out, g_w_ada, sem.at[7 + 2 * pieces + 5])
    out_ada.start()
    grad_cond = dot(mod_low[...], w_ada[...], NT) * (gate * (1.0 + picked * (1.0 - gate)))
    table_out[...] = lax.dot_general(pick, grad_cond, TN, precision=highest, preferred_element_type=f32)
    out_table = pltpu.make_async_copy(table_out, g_table, sem.at[7 + 2 * pieces + 6])
    out_table.start()
    for at in range(2):
        pass_in[at].wait()
        pass_out[at].start()
    for piece in range(pieces):
        grad_in[piece].wait()
        rows = pl.ds(192 * piece, 192)
        wide_out[rows, :] = grads[rows, :].astype(f32)
        grad_out[piece].start()
    for copy in line_out + [out_ada, out_table] + pass_out + grad_out:
        copy.wait()


def finish(gathered, table, w_ada, grads, mixed, grad_tokens):
    seqs, steps = gathered.shape[2], table.shape[0]
    any_space = pl.BlockSpec(memory_space=pl.ANY)
    shapes = [
        (mixed.shape, bf16), (grad_tokens.shape, f32), (table.shape, f32), (w_ada.shape, f32), ((6 * D,), f32),
        ((D,), f32), ((QKV_ROWS, D), f32), ((192, D), f32), ((D,), f32), ((D, D), f32), ((D,), f32), ((D, D), f32),
        ((D,), f32),
    ]
    return pl.pallas_call(
        finish_kernel,
        out_shape=tuple(jax.ShapeDtypeStruct(shape, kind) for shape, kind in shapes),
        in_specs=[any_space] * 6,
        out_specs=[any_space] * len(shapes),
        scratch_shapes=[
            pltpu.VMEM(gathered.shape, bf16),
            pltpu.VMEM(table.shape, f32),
            pltpu.VMEM(w_ada.shape, bf16),
            pltpu.VMEM(grads.shape, bf16),
            pltpu.VMEM((seqs, 6 * D), bf16),
            pltpu.VMEM((steps, table.shape[1]), f32),
            pltpu.VMEM(w_ada.shape, f32),
            pltpu.VMEM(grads.shape, f32),
            pltpu.VMEM((8, D), f32),
            pltpu.VMEM(mixed.shape, bf16),
            pltpu.VMEM(grad_tokens.shape, f32),
            [pltpu.VMEM((6 * D,), f32)] + [pltpu.VMEM((D,), f32)] * 4,
            pltpu.SemaphoreType.DMA((48,)),
        ],
        compiler_params=pltpu.CompilerParams(vmem_limit_bytes=56 * 1024 * 1024),
    )(gathered, table, w_ada, grads, mixed, grad_tokens)


def rope_tables():
    half_width = HD // 2
    frequency = np.float32(10000.0) ** (np.float32(-2.0) * np.arange(half_width, dtype=np.float32) / np.float32(HD))
    angles = np.arange(LEN, dtype=np.float32)[None, :] * frequency[:, None]
    return np.cos(angles).astype(np.float32), np.sin(angles).astype(np.float32)


def body(tokens, timestep, token_mask, time_table, w_ada, b_ada, gain_one, w_qkv, w_out, gain_two, w_up, b_up,
         w_down, b_down, cotangent):
    n_wide = lax.axis_size("wide")
    cos_t, sin_t = rope_tables()
    w_qkv_t = jnp.transpose(w_qkv, (0, 2, 1)).reshape(QKV_ROWS, D)
    mixed, grad_tokens, gathered, grads = fused_block(
        n_wide, tokens, cotangent, token_mask, timestep, time_table, w_ada, b_ada, gain_one, w_qkv_t, w_out, gain_two,
        w_up, b_up, w_down, b_down, cos_t, sin_t,
    )
    outs = list(finish(gathered, time_table, w_ada, grads, mixed, grad_tokens))
    outs[6] = jnp.transpose(outs[6].reshape(3, 192, D), (0, 2, 1))
    return tuple(outs)


def solution(mesh):
    return jax.shard_map(
        body,
        mesh=mesh,
        in_specs=(
            P(("wide", "narrow"), None), P("wide"), P(("wide", "narrow")), P(), P(), P(), P(),
            P(None, None, "narrow"), P("narrow", None), P(), P(None, "narrow"), P("narrow"), P("narrow", None), P(),
            P(("wide", "narrow"), None),
        ),
        out_specs=(
            P(("wide", "narrow"), None), P(("wide", "narrow"), None), P(), P(), P(), P(), P(None, None, "narrow"),
            P("narrow", None), P(), P(None, "narrow"), P("narrow"), P("narrow", None), P(),
        ),
        check_vma=False,
    )
```

```python
import functools
import math

import jax
import jax.numpy as jnp
import numpy as np
from jax import lax
from jax.experimental import pallas as pl
from jax.experimental.pallas import tpu as pltpu
from jax.sharding import PartitionSpec as P

D = 768
HD = 64
LEN = 1024
ROWS_LOCAL = 512
SHARD_HEADS = 3
QKV_ROWS = 576
GRAD_ROWS = 2304
MESH = pl.DeviceIdType.MESH
f32 = jnp.float32
bf16 = jnp.bfloat16
norm_eps = 1e-06
highest = lax.Precision.HIGHEST

NN = (((1,), (0,)), ((), ()))
NT = (((1,), (1,)), ((), ()))
TN = (((0,), (0,)), ((), ()))

CHUNKS = {
    "d0": (0, 192),
    "d1": (192, 192),
    "d2": (384, 192),
    "d3": (576, 192),
    "u0": (768, 192),
    "u1": (960, 192),
    "u2": (1152, 192),
    "u3": (1344, 192),
    "o0": (1536, 192),
    "q0": (1728, 192),
    "q1": (1920, 192),
    "q2": (2112, 96),
    "q3": (2208, 96),
}
ORDERS = {
    "d0": (0, "y", "Z"),
    "d1": (0, "y", "Z"),
    "d2": ("y", 0, "Z"),
    "d3": ("y", 0, "Z"),
    "u0": (1, 0, "y", 2),
    "u1": ("y", 0, "Z"),
    "u2": (1, "y", 0, 2),
    "u3": (0, "y", 1, 2),
    "o0": ("y", 0, "Z"),
    "q0": ("y", 0, "Z"),
    "q1": ("y", 0, 1, 2),
    "q2": ("y", 0, "Z"),
    "q3": ("y", 0, "Z"),
}
PIECES = {
    "q": (3, 2, 1,),
    "o": (2,),
    "u": (0, 3, 3, 2,),
    "d": (0, 1,),
}
LATE_OUT = False
PLACES = (
    "n0", "n1", "p0", "p1", "a0", "a1", "a2", "wq", "p2", "p3", "a3", "a4", "a5", "wo", "o0", "o1", "u3",
    "v0", "v1", "wu", "u4", "u5", "u6", "u7", "f0", "f1", "wd", "f3", "f4", "f5", "f6", "h0", "h1", "i0",
    "b0", "i1", "b1", "i2", "b2", "bx", "i3", "b3", "i4", "b4", "i5", "b5", "by", "c0", "g0", "c1", "g1",
    "g2", "g3",
)
SCHEDULE = {
    "n1": (
        "Wq0",
    ),
    "p0": (
        "Wq1",
    ),
    "a0": (
        "Wq2",
    ),
    "a1": (
        "Wq0", "Wq1", "Wo0",
    ),
    "p2": (
        "Wu0", "Wo0", "Wu1",
    ),
    "p3": (
        "Wu2",
    ),
    "a3": (
        "Wu3",
    ),
    "a5": (
        "Wu1",
    ),
    "o0": (
        "Wu2",
    ),
    "o1": (
        "Wd0",
    ),
    "u3": (
        "Wu3",
    ),
    "v1": (
        "Wd1",
    ),
    "f0": (
        "d1", "d2", "d3", "d0",
    ),
    "f5": (
        "u0", "d1", "d2", "u3", "u2", "u1",
    ),
    "h0": (
        "d3", "d0",
    ),
    "h1": (
        "o0",
    ),
    "i0": (
        "u0", "d1", "d2",
    ),
    "b1": (
        "u3", "u1",
    ),
    "i2": (
        "u2",
    ),
    "b2": (
        "d1", "d3", "d0",
    ),
    "bx": (
        "q2", "q3", "q0", "q1",
    ),
    "i3": (
        "u0", "d2",
    ),
    "b3": (
        "d1", "o0", "u1",
    ),
    "i4": (
        "d3",
    ),
    "b4": (
        "d2", "u3", "d0",
    ),
    "i5": (
        "d1", "o0",
    ),
    "b5": (
        "d3", "u2", "u1",
    ),
    "by": (
        "q2", "d2",
    ),
    "c0": (
        "d1", "u3", "d0",
    ),
    "g0": (
        "q2", "q3", "o0", "d3", "u2", "u1",
    ),
    "g1": (
        "d2", "u3",
    ),
    "g2": (
        "re", "q0", "rl", "q2", "d0", "q3",
    ),
    "g3": (
        "o0", "d3", "u2", "q1", "q0", "q2", "u1", "u0", "re", "u3", "rl", "d0", "q3", "u2", "o0", "q2", "q0",
        "q1", "u0", "u1", "q3", "u2", "re", "q1", "q0", "u3", "rl", "re", "q3", "o0", "q1", "q2", "q0", "rl",
        "u0", "re", "q3", "q1", "re", "rl", "q0", "rl", "u0", "q1",
    ),
}


def chunk_stages(name, n_bits):
    rows = CHUNKS[name][1]
    out = []
    before_y = True
    order = [dim for dim in ORDERS[name] if dim != "Z"] + list(range(3, n_bits))
    if "Z" in ORDERS[name]:
        order.append("Z")
    for dim in order:
        if dim == "y":
            out.append((dim, False, rows, False))
            before_y = False
        elif dim == "Z":
            out += [("Z1", False, rows, False), ("Z2", False, rows, False), ("Z3", False, rows, False)]
        else:
            halved = rows % 32 == 0
            rows = rows // 2 if halved else rows
            out.append((dim, halved, rows, before_y))
    return out


def recv_rows(n_bits):
    return sum(
        2 * rows if both else rows for name in CHUNKS for _, _, rows, both in chunk_stages(name, n_bits)
    )


def outbox_rows(n_bits):
    return sum(rows for name in CHUNKS for _, halved, rows, both in chunk_stages(name, n_bits) if halved and both)


def remote_count(n_bits):
    count = 15 + 2 * (n_bits + 3)
    for matrix in PIECES:
        count += sum(2 if kind < 2 else 4 for kind in PIECES[matrix])
    for name in CHUNKS:
        for _, halved, _, both in chunk_stages(name, n_bits):
            count += (2 if both else 1) + (1 if halved else 0)
    return count


def dot(left, right, dims):
    return lax.dot_general(left, right, dims, preferred_element_type=f32)


def loop(count, body):
    def step(index, carry):
        body(index)
        return carry

    lax.fori_loop(0, count, step, 0)


def rows_at(offset, size, align):
    if isinstance(offset, int):
        return pl.ds(offset, size)
    return pl.ds(pl.multiple_of(offset, align), size)


def normalize(values):
    centered = values - jnp.mean(values, axis=-1, keepdims=True)
    variance = jnp.mean(centered * centered, axis=-1, keepdims=True)
    inverse = lax.rsqrt(variance + norm_eps)
    return centered * inverse, inverse


def norm_grad(vhat, inverse, e_hat):
    mean_e = jnp.mean(e_hat, axis=-1, keepdims=True)
    mean_ev = jnp.mean(e_hat * vhat, axis=-1, keepdims=True)
    return inverse * (e_hat - mean_e - vhat * mean_ev)


def block_kernel(
    n_bits,
    tok_in, cot_in, mask_in, step_in, table_in, w_ada_in, b_ada_in, gain_one_in, wqkv_in, wout_in, gain_two_in,
    wup_in, bup_in, wdown_in, b_down_in, cos_in, sin_in,
    mixed_out, grad_tok_out, gathered_out, grads_out,
    tok, cot, gb, n2, normed, wqkv, wout, wup, wdown, proj, ho, do, lse, attn, mid, part, hidden, gel,
    grad_mid, send_a, recv_a, recv_b, recv_c, acc, oth, stage,
    mod, vec, bup, ada_line, lines, mask_line, cos_t, sin_t, sums, sums_recv, sums_low,
    ssem, rsem, lsem, stage_recv, table, w_ada,
):
    wide = lax.axis_index("wide")
    narrow = lax.axis_index("narrow")
    core = lax.rem(narrow, 2)
    chip_y = lax.div(narrow, 2)
    sib = (wide, narrow + 1 - 2 * core)
    across = (wide, lax.rem(narrow + 2, 4))

    def wide_bit(level):
        return lax.rem(lax.div(wide, 1 << level), 2)

    def wide_peer(level):
        return (wide + (1 << level) * (1 - 2 * wide_bit(level)), narrow)

    bit_lo, bit_hi = wide_bit(1), wide_bit(2)
    at_end = bit_lo == bit_hi
    inner_peer = (wide + 2 * (1 - 2 * bit_lo) + 4 * (1 - 2 * bit_hi), narrow)
    peers = [sib, across, inner_peer] + [wide_peer(level) for level in range(n_bits)]
    own0 = core * ROWS_LOCAL
    sib0 = (1 - core) * ROWS_LOCAL

    n_sems = {"remote": 0, "local": 0}

    def remote(src, dst, peer):
        at = n_sems["remote"]
        n_sems["remote"] += 1
        return pltpu.make_async_remote_copy(
            src_ref=src, dst_ref=dst, send_sem=ssem.at[at], recv_sem=rsem.at[at],
            device_id=peer, device_id_type=MESH,
        )

    def local(src, dst):
        at = n_sems["local"]
        n_sems["local"] += 1
        return pltpu.make_async_copy(src, dst, lsem.at[at])

    c_tok = local(tok_in, tok)
    c_cot = local(cot_in, cot)
    c_small = [
        local(b_ada_in, ada_line),
        local(gain_one_in, lines[0]),
        local(gain_two_in, lines[1]),
        local(b_down_in, lines[2]),
        local(bup_in, bup[0]),
        local(mask_in, mask_line),
        local(cos_in, cos_t),
        local(sin_in, sin_t),
    ]
    c_ada = [local(table_in, table), local(w_ada_in, w_ada)]
    c_wqkv = local(wqkv_in, wqkv.at[0])
    c_wout = local(wout_in, wout.at[pl.ds(0, 192)])
    c_wup = local(wup_in, wup.at[:, pl.ds(0, D)])
    c_wdown = local(wdown_in, wdown.at[pl.ds(0, D)])
    c_tok.start()
    for copy in c_small + c_ada:
        copy.start()
    c_wqkv.start()
    c_cot.start()
    c_wout.start()
    c_wup.start()
    c_wdown.start()

    barrier = pltpu.get_barrier_semaphore()
    for peer in peers:
        pl.semaphore_signal(barrier, inc=1, device_id=peer, device_id_type=MESH)
    pl.semaphore_wait(barrier, len(peers))

    r_tok = remote(tok_in, n2.at[rows_at(own0, ROWS_LOCAL, 512)], sib)
    r_cot = remote(cot, gb.at[rows_at(own0, ROWS_LOCAL, 512)], sib)
    r_tok.start()

    places = {
        "q": (wqkv_in, lambda rows: wqkv.at[1, rows], QKV_ROWS, 0),
        "o": (wout_in, lambda rows: wout.at[rows], 192, 192),
        "u": (wup_in, lambda rows: wup.at[rows, pl.ds(D, D)], D, 0),
        "d": (wdown_in, lambda rows: wdown.at[rows], D, D),
    }
    w_across, w_sent, w_last, plans = {}, {}, {}, {}
    piece_keys = []
    ahead = 6

    def pass_on(at, arrived, copies):
        arrived.wait_recv()
        for copy in copies:
            copy.start()
        if at is not None and at + ahead < len(piece_keys):
            w_across[piece_keys[at + ahead]].start()

    for matrix in PIECES:
        source, target, total_rows, shift = places[matrix]
        count = len(PIECES[matrix])
        for piece in range(count):
            kind = PIECES[matrix][piece]
            at = len(piece_keys)
            key = "W" + matrix + str(piece)
            piece_keys.append(key)
            first = piece * (total_rows // count)
            if kind < 2:
                size = total_rows // (2 * count)
                row = first + wide_bit(kind) * size
                here = target(rows_at(shift + row, size, 16))
                along = remote(here, here, wide_peer(kind))
                w_sent[key], w_last[key] = [along], [along]
                steps = [(at, [along])]
            else:
                size = total_rows // (4 * count)
                bits = (wide_bit(0), wide_bit(1))

                def quarter(bit_0, bit_1):
                    return target(rows_at(shift + first + (2 * bit_0 + bit_1) * size, size, 16))

                row = first + (2 * bits[0] + bits[1]) * size
                here = quarter(*bits)
                along = [remote(here, here, wide_peer(level)) for level in (0, 1)]
                theirs = quarter(1 - bits[0], bits[1]) if kind == 2 else quarter(bits[0], 1 - bits[1])
                last = remote(theirs, theirs, wide_peer(3 - kind))
                w_sent[key], w_last[key] = along + [last], [along[3 - kind], last]
                steps = [(at, along), (along[kind - 2], [last])]
            w_across[key] = remote(source.at[rows_at(row, size, 16)], here, across)
            plans[key] = [functools.partial(pass_on, at, w_across[key], steps[0][1])]
            plans[key] += [functools.partial(pass_on, None, arrived, copies) for arrived, copies in steps[1:]]
    r_bup = remote(bup_in, bup[1], across)
    for key in piece_keys[:ahead]:
        w_across[key].start()
    r_bup.start()

    def segment(name, index):
        offset, rows = CHUNKS[name]
        for dim, halved, count, _ in chunk_stages(name, n_bits)[:index]:
            if halved:
                offset = offset + wide_bit(dim) * count
                rows = count
        return offset, rows

    stage_copies, back_copies, stage_base, returns, final_copies, outbox = {}, {}, {}, {}, {}, {}
    stage_rows_used = 0
    base = 0
    for name in CHUNKS:
        for index, (dim, halved, count, both) in enumerate(chunk_stages(name, n_bits)):
            offset, _ = segment(name, index)
            stage_base[name, index] = base
            if dim == "y":
                sent, peer = [oth], across
            elif dim in ("Z1", "Z2", "Z3"):
                sent, peer = [acc], inner_peer if dim == "Z2" else wide_peer(1)
            else:
                sent, peer = [acc, oth] if both else [acc], wide_peer(dim)
                if halved:
                    offset = offset + (1 - wide_bit(dim)) * count
            copies = []
            for array in sent:
                landing = stage_recv.at[pl.ds(base, count)]
                source = array.at[rows_at(offset, count, 16)]
                if halved and array is acc:
                    if both:
                        outbox[name, index] = (stage, stage_rows_used)
                        source = stage.at[pl.ds(stage_rows_used, count)]
                        stage_rows_used += count
                    else:
                        outbox[name, index] = (oth, offset)
                        source = oth.at[rows_at(offset, count, 16)]
                copies.append(remote(source, landing, peer))
                base += count
            stage_copies[name, index] = copies
            if halved:
                offset, count = segment(name, index + 1)
                rows = acc.at[rows_at(offset, count, 16)]
                back_copies[name, index] = remote(rows, rows, peer)
    for name in CHUNKS:
        returns[name] = [at for at in range(len(chunk_stages(name, n_bits))) if (name, at) in back_copies]
        first, count = CHUNKS[name]
        final_copies[name] = local(acc.at[pl.ds(first, count)], grads_out.at[pl.ds(first, count)])

    def start_stage(name, index):
        if index == 0 and (name, 0) in outbox:
            offset, _ = segment(name, 0)
            dim, _, count, _ = chunk_stages(name, n_bits)[0]
            box, row0 = outbox[name, 0]
            box[pl.ds(row0, count), :] = acc[rows_at(offset + (1 - wide_bit(dim)) * count, count, 16), :]
        for copy in stage_copies[name, index]:
            copy.start()

    def merge_step(name, index):
        stages = chunk_stages(name, n_bits)
        before = stages[index - 1][0]
        copies = stage_copies[name, index - 1]
        offset, rows = segment(name, index)
        both_before = len(copies) == 2
        base = stage_base[name, index - 1]

        def merge(array, row0, count, box=None, replace=False):
            start = base + rows if array is oth else base
            step = 48 if count % 48 == 0 else 16
            target, target0 = box or (array, row0)

            def one(at):
                row = row0 + step * at
                here = rows_at(row, step, 16)
                value = stage_recv[rows_at(start + row - offset, step, 16), :]
                if not replace:
                    value = (array[here, :].astype(f32) + value.astype(f32)).astype(bf16)
                target[rows_at(target0 + step * at, step, 16), :] = value

            loop(count // step, one)

        def go_on():
            if index == len(stages):
                back_copies[name, returns[name][-1]].start()
            else:
                start_stage(name, index)

        if before == "Z1":

            @pl.when(at_end)
            def _():
                copies[0].wait_send()

            @pl.when(jnp.logical_not(at_end))
            def _():
                copies[0].wait_recv()
                merge(acc, offset, rows)
                go_on()

            return
        if before == "Z2":

            @pl.when(jnp.logical_not(at_end))
            def _():
                copies[0].wait()
                merge(acc, offset, rows)
                go_on()

            return
        if before == "Z3":

            @pl.when(at_end)
            def _():
                copies[0].wait_recv()
                merge(acc, offset, rows, replace=True)

            @pl.when(jnp.logical_not(at_end))
            def _():
                copies[0].wait_send()

            go_on()
            return
        for copy in copies:
            copy.wait()
        arrays = [acc, oth] if both_before else [acc]
        if index == len(stages):
            merge(acc, offset, rows)
            go_on()
            return
        dim, halved, count, _ = stages[index]
        if dim == "y":
            for array in reversed(arrays):
                merge(array, offset, rows)
                if array is oth or not both_before:
                    start_stage(name, index)
        elif dim == "Z1":
            merge(acc, offset, rows)

            @pl.when(at_end)
            def _():
                start_stage(name, index)

        elif halved:
            for array in arrays:
                box = outbox[name, index] if array is acc else None
                merge(array, offset + (1 - wide_bit(dim)) * count, count, box)
            start_stage(name, index)
            for array in arrays:
                merge(array, offset + wide_bit(dim) * count, count)
        else:
            merge(acc, offset, rows)
            start_stage(name, index)

    def back_step(name, at):
        back_copies[name, returns[name][at]].wait()
        if at > 0:
            back_copies[name, returns[name][at - 1]].start()
        else:
            final_copies[name].start()

    for name in CHUNKS:
        plan = [functools.partial(start_stage, name, 0)]
        plan += [functools.partial(merge_step, name, index + 1) for index in range(len(chunk_stages(name, n_bits)))]
        plan += [functools.partial(back_step, name, at) for at in reversed(range(len(returns[name])))]
        plans[name] = plan

    place = 2 * wide + chip_y
    r_sib, row_copies, own_rows = [], [], []
    for part_index in range(2):
        mine = gathered_out.at[part_index, core]
        r_sib.append(remote(sums.at[part_index], sums_recv.at[part_index], sib))
        own_rows.append(local(sums_low.at[part_index], mine.at[place]))
        copies = [remote(sums_low.at[part_index], mine.at[place], across)]
        for level in range(n_bits):
            count = 2 << level
            rows = mine.at[pl.ds(lax.div(place, count) * count, count)]
            copies.append(remote(rows, rows, wide_peer(level)))
        copies.append(remote(mine, mine, sib))
        row_copies.append(copies)

    def row_step(part_index, at):
        if at == 0:
            own_rows[part_index].start()
        if at == 1:
            own_rows[part_index].wait()
        if at > 0:
            row_copies[part_index][at - 1].wait()
        if at < n_bits + 2:
            row_copies[part_index][at].start()

    for part_index, key in enumerate(("re", "rl")):
        plans[key] = [functools.partial(row_step, part_index, at) for at in range(n_bits + 3)]

    def sums_ready(part_index):
        r_sib[part_index].wait()
        cols = rows_at(core * 384, 384, 128)
        total = sums[part_index, :, cols] + sums_recv[part_index, :, cols]
        sums_low[part_index] = total.astype(bf16)

    steps_at = {}
    for name in PLACES:
        if name[0] == "w":
            keys = [key for key in piece_keys if key[1] == name[1]]
            steps_at[name] = [step for key in keys for step in plans.pop(key)]
        else:
            steps_at[name] = [plans[key].pop(0) for key in SCHEDULE.get(name, ()) if plans.get(key)]
    while any(plans.values()):
        steps_at["g3"] += [plans[key].pop(0) for key in plans if plans[key]]

    def point(name):
        for step in steps_at[name]:
            step()

    def need(matrix):
        point("w" + matrix)
        for key in piece_keys:
            if key[1] == matrix:
                for copy in w_last[key]:
                    copy.wait_recv()

    for copy in c_small:
        copy.wait()
    time_step = step_in[chip_y]
    for row in range(3):
        vec[row : row + 1, :] = lines[row][...].reshape(1, D)

    for copy in c_ada:
        copy.wait()
    picked = table[pl.ds(time_step, 1), :]
    cond = picked / (1.0 + jnp.exp(-picked))
    cond = jnp.broadcast_to(cond, (16, 128)).astype(bf16)
    for index in range(6):
        flat = dot(cond, w_ada[:, index * D : (index + 1) * D], NN)
        mod[index : index + 1, :] = ada_line[pl.ds(index * D, D)].reshape(1, D) + flat[0:1, :]

    def first_norm(source, src0, dst0):
        def one(index):
            values = source[rows_at(src0 + 128 * index, 128, 128), :].astype(f32)
            vhat, _ = normalize(values)
            out = vhat * vec[0:1, :] * (1.0 + mod[1:2, :]) + mod[0:1, :]
            normed[rows_at(dst0 + 128 * index, 128, 128), :] = out.astype(bf16)

        loop(4, one)

    c_tok.wait()
    first_norm(tok, 0, own0)
    point("n0")
    r_tok.wait_recv()
    first_norm(n2, sib0, sib0)
    c_cot.wait()
    mask = jnp.broadcast_to(mask_line[...].astype(f32).reshape(1, ROWS_LOCAL), (8, ROWS_LOCAL)).T[:, 0:1]
    cot[...] = (cot[...].astype(f32) * mask).astype(bf16)
    r_cot.start()
    point("n1")

    def project(shard):
        def one(index):
            cols = rows_at(256 * index, 256, 256)
            flat = dot(wqkv[shard], normed[cols, :], NT)
            cos_b, sin_b = cos_t[:, cols], sin_t[:, cols]
            for kind in (0, 1):
                scale = 0.125 if kind == 0 else 1.0
                for head in range(SHARD_HEADS):
                    at = kind * 192 + head * HD
                    low, high = flat[at : at + 32], flat[at + 32 : at + 64]
                    proj[shard, at : at + 32, cols] = ((low * cos_b - high * sin_b) * scale).astype(bf16)
                    proj[shard, at + 32 : at + 64, cols] = ((high * cos_b + low * sin_b) * scale).astype(bf16)
            proj[shard, 384:576, cols] = flat[384:576].astype(bf16)
            point_in("p", 2 * shard + lax.div(index, 2), lax.rem(index, 2) == 1, 4)

        loop(4, one)

    def point_in(prefix, index, last, count):
        for place in range(count):
            if steps_at.get(prefix + str(place)) and (prefix, place) != ("u", 3):

                @pl.when((index == place) & last)
                def _():
                    point(prefix + str(place))

    def head_rows(kind, head):
        return rows_at(kind * 192 + head * HD, HD, HD)

    def attend(shard, head):
        q_t = proj[shard, head_rows(0, head), :]
        k_t = proj[shard, head_rows(1, head), :]
        v_t = proj[shard, head_rows(2, head), :]
        scores = dot(k_t, q_t, TN)
        top = jnp.max(scores, axis=0, keepdims=True)
        weights = jnp.exp(scores - top)
        total = jnp.sum(weights, axis=0, keepdims=True)
        out = dot(v_t, weights.astype(bf16), NN) * (1.0 / total)
        index = shard * SHARD_HEADS + head
        ho[rows_at(index * HD, HD, HD), :] = out.astype(bf16)
        lse[index, 0:1, :] = top + jnp.log(total)

    c_wqkv.wait()

    def shard_heads(shard):
        @pl.when(shard == 1)
        def _():
            need("q")

        project(shard)

        def one(head):
            attend(shard, head)
            point_in("a", SHARD_HEADS * shard + head, True, 6)

        loop(SHARD_HEADS, one)

    loop(2, shard_heads)

    c_wout.wait()
    need("o")
    half = 256

    def exchange_start(recv, index):
        rows = pl.ds(half * index, half)
        copy = remote(send_a.at[rows], recv.at[rows], sib)
        copy.start()
        return copy

    r_attn = []
    for index in range(2):
        out = dot(ho[:, rows_at(sib0 + half * index, half, half)], wout[...], TN)
        send_a[half * index : half * (index + 1), :] = out.astype(bf16)
        r_attn.append(exchange_start(recv_a, index))
    for index in range(2):
        out = dot(ho[:, rows_at(own0 + half * index, half, half)], wout[...], TN)
        attn[half * index : half * (index + 1), :] = out
    point("o0")
    r_n2 = []
    for index in range(2):
        r_attn[index].wait_recv()

        def second_norm(sub):
            rows = rows_at(half * index + 128 * sub, 128, 128)
            value = attn[rows, :] + recv_a[rows, :].astype(f32)
            attn[rows, :] = value
            residual = tok[rows, :].astype(f32) + mod[2:3, :] * value
            mid[rows, :] = residual
            vhat, _ = normalize(residual)
            out = vhat * vec[1:2, :] * (1.0 + mod[4:5, :]) + mod[3:4, :]
            n2[rows_at(own0 + half * index + 128 * sub, 128, 128), :] = out.astype(bf16)

        loop(2, second_norm)
        rows = rows_at(own0 + half * index, half, half)
        r_n2.append(remote(n2.at[rows], n2.at[rows], sib))
        r_n2[index].start()
        r_attn[index].wait_send()

    r_cot.wait_recv()

    def branch_grad(index):
        rows = rows_at(own0 + 128 * index, 128, 128)
        part_rows = rows_at(128 * index, 128, 128)
        gb[rows, :] = (cot[part_rows, :].astype(f32) * mod[5:6, :]).astype(bf16)
        rows = rows_at(sib0 + 128 * index, 128, 128)
        gb[rows, :] = (gb[rows, :].astype(f32) * mod[5:6, :]).astype(bf16)

    r_cot.wait_send()
    loop(4, branch_grad)
    point("o1")

    c_wup.wait()
    r_bup.wait_recv()
    for row in range(2):
        vec[4 + row : 5 + row, :] = bup[row][...].reshape(1, D)
    gelu_c = math.sqrt(2.0 / math.pi)

    def up(shard, block):
        @pl.when((shard == 0) & (block == 2))
        def _():
            r_n2[0].wait_recv()
            r_n2[1].wait_recv()

        rows = rows_at(lax.rem(own0 + 256 * block, LEN), 256, 256)
        cols = rows_at(shard * D, D, D)
        pre = dot(n2[rows, :], wup[:, cols], NN) + vec[pl.ds(4 + shard, 1), :]
        square = pre * pre
        squash = jnp.tanh(gelu_c * pre * (1.0 + 0.044715 * square))
        gate = 0.5 * (1.0 + squash)
        hidden[rows, cols] = (pre * gate).astype(bf16)
        slope = gate + 0.5 * pre * (1.0 - squash * squash) * (gelu_c * (1.0 + 3.0 * 0.044715 * square))
        gel[rows, cols] = slope.astype(bf16)

    loop(4, functools.partial(up, 0))
    point("u3")

    def w_down_grad(shard, target, base):
        def one(index):
            cols = rows_at(shard * D + 256 * index, 256, 256)
            out = dot(hidden[:, cols], gb[...], TN)
            target[rows_at(base + 256 * index, 256, 256), :] = out.astype(bf16)

        loop(3, one)

    w_down_grad(0, acc, 0)
    point("v0")
    sums[...] = jnp.zeros_like(sums)
    c_wdown.wait()

    def hidden_grad(shard, row):
        def one(index):
            rows = rows_at(256 * index, 256, 256)
            cols = pl.ds(shard * D, D)
            grad_act = dot(gb[rows, :], wdown[pl.ds(shard * D, D), :], NT)
            low = (grad_act * gel[rows, cols].astype(f32)).astype(bf16)
            gel[rows, cols] = low
            line = pl.ds(row, 1)
            sums[1, line, :] = sums[1, line, :] + jnp.sum(low.astype(f32), axis=0, keepdims=True)

        loop(4, one)

    def w_up_grad(shard, target):
        def one(index):
            cols = rows_at(256 * index, 256, 256)
            out = dot(n2[:, cols], gel[:, pl.ds(shard * D, D)], TN)
            target[rows_at(D + 256 * index, 256, 256), :] = out.astype(bf16)

        loop(3, one)

    hidden_grad(0, 3 + narrow)
    point("v1")
    need("u")

    def up_other(block):
        up(1, block)
        point_in("u", block + 4, True, 8)

    loop(4, up_other)
    w_down_grad(1, oth, 0)
    point("f0")
    w_up_grad(0, acc)
    point("f1")
    need("d")
    hidden_grad(1, 3 + lax.rem(narrow + 2, 4))
    point("f3")

    r_gn2 = []
    for index in range(2):
        out = dot(gel[rows_at(sib0 + half * index, half, half), :], wup[...], NT)
        send_a[half * index : half * (index + 1), :] = out.astype(bf16)
        r_gn2.append(exchange_start(recv_b, index))
    for index in range(2):
        out = dot(gel[rows_at(own0 + half * index, half, half), :], wup[...], NT)
        part[half * index : half * (index + 1), :] = out
    point("f4")
    w_up_grad(1, oth)
    point("f5")

    r_ga = []
    for index in range(2):
        r_gn2[index].wait()

        def second_back(sub):
            rows = rows_at(half * index + 128 * sub, 128, 128)
            upstream = part[rows, :] + recv_b[rows, :].astype(f32)
            vhat, inverse = normalize(mid[rows, :])
            scaled = upstream * (1.0 + mod[4:5, :])
            grad_mixed = cot[rows, :].astype(f32)
            value = grad_mixed + norm_grad(vhat, inverse, scaled * vec[1:2, :])
            grad_mid[rows, :] = value
            gb[rows_at(own0 + half * index + 128 * sub, 128, 128), :] = (value * mod[2:3, :]).astype(bf16)
            add_sum(0, 0, value * attn[rows, :])
            add_sum(0, 1, upstream)
            add_sum(0, 2, upstream * (vhat * vec[1:2, :]))
            add_sum(0, 4, scaled * vhat)
            add_sum(0, 5, grad_mixed * mod[5:6, :])

        def add_sum(part_index, row, values):
            line = slice(row, row + 1)
            sums[part_index, line, :] = sums[part_index, line, :] + jnp.sum(values, axis=0, keepdims=True)

        loop(2, second_back)
        rows = rows_at(own0 + half * index, half, half)
        r_ga.append(remote(gb.at[rows], gb.at[rows], sib))
        r_ga[index].start()
    point("f6")

    r_ga[0].wait_recv()
    r_ga[1].wait_recv()

    def head_grad(index):
        cols = rows_at(256 * index, 256, 256)
        do[:, cols] = dot(wout[...], gb[cols, :], NT).astype(bf16)

    loop(4, head_grad)
    point("h0")

    def w_out_grad():
        oth[1536:1728, :] = dot(ho[192:384, :], gb[...], NN).astype(bf16)
        acc[1536:1728, :] = dot(ho[0:192, :], gb[...], NN).astype(bf16)
        point("h1")

    if not LATE_OUT:
        w_out_grad()

    def attend_back(shard, head, between):
        q_t = proj[shard, head_rows(0, head), :]
        k_t = proj[shard, head_rows(1, head), :]
        v_t = proj[shard, head_rows(2, head), :]
        index = shard * SHARD_HEADS + head
        d_t = do[rows_at(index * HD, HD, HD), :]
        probs = jnp.exp(dot(k_t, q_t, TN) - lse[index, 0:1, :])
        grad_probs = dot(v_t, d_t, TN)
        inner = jnp.sum(probs * grad_probs, axis=0, keepdims=True)
        grad_scores = (probs * (grad_probs - inner)).astype(bf16)
        between()
        dq_t = dot(k_t, grad_scores, NN) * 0.125
        dk_t = dot(grad_scores, q_t, NT).T
        dv_t = dot(probs.astype(bf16), d_t, NT).T
        for kind, grad in ((0, dq_t), (1, dk_t)):
            low, high = grad[:32], grad[32:]
            turned = jnp.concatenate(
                [low * cos_t[...] + high * sin_t[...], high * cos_t[...] - low * sin_t[...]], axis=0
            )
            proj[shard, head_rows(kind, head), :] = turned.astype(bf16)
        proj[shard, head_rows(2, head), :] = dv_t.astype(bf16)

    for key in piece_keys:
        for copy in w_sent[key] + [w_across[key]]:
            copy.wait_send()

    def w_qkv_grad(shard, target):
        def one(index):
            rows = rows_at(192 * index, 192, 64)
            out = dot(proj[shard, rows, :], normed[...], NN)
            target[rows_at(1728 + 192 * index, 192, 64), :] = out.astype(bf16)

        loop(3, one)

    def back_heads(index):
        shard = 1 - lax.div(index, SHARD_HEADS)
        head = lax.rem(index, SHARD_HEADS)
        attend_back(shard, head, lambda: point_in("i", index, True, 6))
        point_in("b", index, True, 6)

        @pl.when(index == 2)
        def _():
            w_qkv_grad(1, oth)
            point("bx")

    loop(6, back_heads)
    w_qkv_grad(0, acc)
    point("by")
    if LATE_OUT:
        w_out_grad()

    r_branch = []
    for index in range(2):
        out = dot(hidden[rows_at(sib0 + half * index, half, half), :], wdown[...], NN)
        send_a[half * index : half * (index + 1), :] = out.astype(bf16)
        r_branch.append(exchange_start(recv_c, index))
    for index in range(2):
        out = dot(hidden[rows_at(own0 + half * index, half, half), :], wdown[...], NN)
        part[half * index : half * (index + 1), :] = out
    point("c0")


    def normed_grad(offset):
        first = dot(proj[0, :, offset], wqkv[0], TN)
        return first + dot(proj[1, :, offset], wqkv[1], TN)

    r_gn = []
    for index in range(2):
        rows = pl.ds(half * index, half)
        recv_b[rows, :] = normed_grad(rows_at(sib0 + half * index, half, half)).astype(bf16)
        r_gn.append(remote(recv_b.at[rows], recv_a.at[rows], sib))
        r_gn[index].start()
    for index in range(2):
        attn[half * index : half * (index + 1), :] = normed_grad(rows_at(own0 + half * index, half, half))
    point("g0")

    def finish_branch(index):
        rows = rows_at(128 * index, 128, 128)
        branch = part[rows, :] + recv_c[rows, :].astype(f32) + vec[2:3, :]
        add_sum(0, 3, cot[rows, :].astype(f32) * branch)
        send_a[rows, :] = (mid[rows, :] + mod[5:6, :] * branch).astype(bf16)

    r_branch[0].wait()
    r_branch[1].wait()
    loop(4, finish_branch)
    c_mixed = local(send_a, mixed_out)
    c_mixed.start()
    on_first = (1 - core).astype(f32)
    high = lax.div(time_step, 32)
    sums[0, 6:7, :] = jnp.full((1, D), high.astype(f32) * on_first)
    sums[0, 7:8, :] = jnp.full((1, D), (time_step - 32 * high).astype(f32) * on_first)
    r_sib[0].start()
    point("c1")

    for index in range(2):
        r_gn[index].wait()

        def first_back(sub):
            rows = rows_at(half * index + 128 * sub, 128, 128)
            upstream = attn[rows, :] + recv_a[rows, :].astype(f32)
            vhat, inverse = normalize(tok[rows, :].astype(f32))
            scaled = upstream * (1.0 + mod[1:2, :])
            attn[rows, :] = grad_mid[rows, :] + norm_grad(vhat, inverse, scaled * vec[0:1, :])
            add_sum(1, 0, upstream)
            add_sum(1, 1, upstream * (vhat * vec[0:1, :]))
            add_sum(1, 2, scaled * vhat)

        loop(2, first_back)
    c_grad_tok = local(attn, grad_tok_out)
    c_grad_tok.start()

    r_sib[1].start()
    point("g1")
    sums_ready(0)
    sums_ready(1)
    point("g2")
    point("g3")
    for name in CHUNKS:
        final_copies[name].wait()
    c_grad_tok.wait()
    c_mixed.wait()
    for copy in [r_tok, r_bup] + r_n2 + r_ga:
        copy.wait_send()


def fused_block(n_wide, tokens, cot, mask, timestep, table, w_ada, b_ada, gain_one, w_qkv_t, w_out, gain_two, w_up, b_up,
                w_down, b_down, cos_t, sin_t):
    n_bits = n_wide.bit_length() - 1
    any_space = pl.BlockSpec(memory_space=pl.ANY)
    scratch = [
        pltpu.VMEM((ROWS_LOCAL, D), bf16),
        pltpu.VMEM((ROWS_LOCAL, D), bf16),
        pltpu.VMEM((LEN, D), bf16),
        pltpu.VMEM((LEN, D), bf16),
        pltpu.VMEM((LEN, D), bf16),
        pltpu.VMEM((2, QKV_ROWS, D), bf16),
        pltpu.VMEM((384, D), bf16),
        pltpu.VMEM((D, 2 * D), bf16),
        pltpu.VMEM((2 * D, D), bf16),
        pltpu.VMEM((2, QKV_ROWS, LEN), bf16),
        pltpu.VMEM((384, LEN), bf16),
        pltpu.VMEM((384, LEN), bf16),
        pltpu.VMEM((6, 8, LEN), f32),
        pltpu.VMEM((ROWS_LOCAL, D), f32),
        pltpu.VMEM((ROWS_LOCAL, D), f32),
        pltpu.VMEM((ROWS_LOCAL, D), f32),
        pltpu.VMEM((LEN, 2 * D), bf16),
        pltpu.VMEM((LEN, 2 * D), bf16),
        pltpu.VMEM((ROWS_LOCAL, D), f32),
        pltpu.VMEM((ROWS_LOCAL, D), bf16),
        pltpu.VMEM((ROWS_LOCAL, D), bf16),
        pltpu.VMEM((ROWS_LOCAL, D), bf16),
        pltpu.VMEM((ROWS_LOCAL, D), bf16),
        pltpu.VMEM((GRAD_ROWS, D), bf16),
        pltpu.VMEM((GRAD_ROWS, D), bf16),
        pltpu.VMEM((outbox_rows(n_bits), D), bf16),
        pltpu.VMEM((8, D), f32),
        pltpu.VMEM((8, D), f32),
        [pltpu.VMEM((D,), f32)] * 2,
        pltpu.VMEM((6 * D,), f32),
        [pltpu.VMEM((D,), f32)] * 3,
        pltpu.VMEM((ROWS_LOCAL,), jnp.int32),
        pltpu.VMEM((32, LEN), f32),
        pltpu.VMEM((32, LEN), f32),
        pltpu.VMEM((2, 8, D), f32),
        pltpu.VMEM((2, 8, D), f32),
        pltpu.VMEM((2, 8, D // 2), bf16),
        pltpu.SemaphoreType.DMA((remote_count(n_bits),)),
        pltpu.SemaphoreType.DMA((remote_count(n_bits),)),
        pltpu.SemaphoreType.DMA((20 + len(CHUNKS),)),
        pltpu.VMEM((recv_rows(n_bits), D), bf16),
        pltpu.VMEM(table.shape, f32),
        pltpu.VMEM(w_ada.shape, bf16),
    ]
    specs = [any_space] * 17
    specs[3] = pl.BlockSpec(memory_space=pltpu.SMEM)
    return pl.pallas_call(
        functools.partial(block_kernel, n_bits),
        out_shape=(
            jax.ShapeDtypeStruct((ROWS_LOCAL, D), bf16),
            jax.ShapeDtypeStruct((ROWS_LOCAL, D), f32),
            jax.ShapeDtypeStruct((2, 2, 2 * n_wide, 8, D // 2), bf16),
            jax.ShapeDtypeStruct((GRAD_ROWS, D), bf16),
        ),
        in_specs=specs,
        out_specs=[any_space] * 4,
        scratch_shapes=scratch,
        compiler_params=pltpu.CompilerParams(
            collective_id=0, has_side_effects=True, vmem_limit_bytes=60 * 1024 * 1024
        ),
    )(tokens, cot, mask, timestep, table, w_ada, b_ada, gain_one, w_qkv_t, w_out, gain_two, w_up, b_up, w_down, b_down,
      cos_t, sin_t)


def finish_kernel(
    gathered_in, table_in, w_ada_in, grads_in, mixed_in, grad_tok_in,
    mixed_out, grad_tok_out, g_table, g_w_ada, g_b_ada, g_gain_one, g_wqkv, g_wout, g_gain_two, g_wup, g_bup,
    g_wdown, g_b_down,
    gathered, table, w_ada, grads, mod_low, table_out, ada_out, wide_out, late_sum, mixed_buf, tok_buf, lines, sem,
):
    pieces = GRAD_ROWS // 192
    targets = [(g_wdown, 0), (g_wup, 768), (g_wout, 1536), (g_wqkv, 1728)]
    loads = [(gathered_in, gathered), (table_in, table), (w_ada_in, w_ada)]
    loads = [pltpu.make_async_copy(src, dst, sem.at[at]) for at, (src, dst) in enumerate(loads)]
    pass_in = [
        pltpu.make_async_copy(mixed_in, mixed_buf, sem.at[3]),
        pltpu.make_async_copy(grad_tok_in, tok_buf, sem.at[4]),
    ]
    pass_out = [
        pltpu.make_async_copy(mixed_buf, mixed_out, sem.at[5]),
        pltpu.make_async_copy(tok_buf, grad_tok_out, sem.at[6]),
    ]
    grad_in, grad_out = [], []
    for piece in range(pieces):
        rows = pl.ds(192 * piece, 192)
        grad_in.append(pltpu.make_async_copy(grads_in.at[rows], grads.at[rows], sem.at[7 + piece]))
        target, first = [item for item in targets if item[1] <= 192 * piece][-1]
        grad_out.append(
            pltpu.make_async_copy(
                wide_out.at[rows], target.at[pl.ds(192 * piece - first, 192)], sem.at[7 + pieces + piece]
            )
        )
    for copy in grad_in[: pieces // 2] + loads + pass_in + grad_in[pieces // 2 :]:
        copy.start()

    def widen(piece):
        grad_in[piece].wait()
        rows = pl.ds(192 * piece, 192)
        wide_out[rows, :] = grads[rows, :].astype(f32)
        grad_out[piece].start()

    for piece in range(pieces // 2):
        widen(piece)
    for copy in loads:
        copy.wait()

    def both(index):
        return jnp.concatenate([gathered[index, 0].astype(f32), gathered[index, 1].astype(f32)], axis=-1)

    early, late = both(0), both(1)
    total_early, total_late = jnp.sum(early, axis=0), jnp.sum(late, axis=0)
    late_sum[...] = total_late
    for row, values in enumerate([late[:, 0], late[:, 1], early[:, 0], early[:, 1], early[:, 2], early[:, 3]]):
        mod_low[:, row * D : (row + 1) * D] = values.astype(bf16)
    rows = [total_late[0:1], total_late[1:2]] + [total_early[row : row + 1] for row in range(4)]
    for row, values in enumerate(rows):
        lines[0][pl.ds(row * D, D)] = values.reshape(D)
    lines[1][...] = total_late[2:3].reshape(D)
    lines[2][...] = total_early[4:5].reshape(D)
    lines[3][...] = late_sum[pl.ds(3 + lax.axis_index("narrow"), 1), :].reshape(D)
    lines[4][...] = total_early[5:6].reshape(D)
    line_out = [
        pltpu.make_async_copy(line, out, sem.at[7 + 2 * pieces + at])
        for at, (line, out) in enumerate(zip(lines, (g_b_ada, g_gain_one, g_gain_two, g_bup, g_b_down)))
    ]
    for copy in line_out:
        copy.start()
    seqs, steps = early.shape[0], table.shape[0]
    time_step = early[:, 6, 0:1] * 32.0 + early[:, 7, 0:1]
    columns = lax.broadcasted_iota(jnp.int32, (seqs, steps), 1).astype(f32)
    pick = jnp.where(columns == time_step, 1.0, 0.0).astype(f32)
    picked = lax.dot_general(pick, table[...], NN, precision=highest, preferred_element_type=f32)
    gate = 1.0 / (1.0 + jnp.exp(-picked))
    cond = (picked * gate).astype(bf16)
    ada_out[...] = dot(cond, mod_low[...], TN)
    out_ada = pltpu.make_async_copy(ada_out, g_w_ada, sem.at[7 + 2 * pieces + 5])
    out_ada.start()
    grad_cond = dot(mod_low[...], w_ada[...], NT) * (gate * (1.0 + picked * (1.0 - gate)))
    table_out[...] = lax.dot_general(pick, grad_cond, TN, precision=highest, preferred_element_type=f32)
    out_table = pltpu.make_async_copy(table_out, g_table, sem.at[7 + 2 * pieces + 6])
    out_table.start()
    for piece in range(pieces // 2, pieces):
        widen(piece)
    for at in range(2):
        pass_in[at].wait()
        pass_out[at].start()
    for copy in line_out + [out_ada, out_table] + pass_out + grad_out:
        copy.wait()


def finish(gathered, table, w_ada, grads, mixed, grad_tokens):
    seqs, steps = gathered.shape[2], table.shape[0]
    any_space = pl.BlockSpec(memory_space=pl.ANY)
    shapes = [
        (mixed.shape, bf16), (grad_tokens.shape, f32), (table.shape, f32), (w_ada.shape, f32), ((6 * D,), f32),
        ((D,), f32), ((QKV_ROWS, D), f32), ((192, D), f32), ((D,), f32), ((D, D), f32), ((D,), f32), ((D, D), f32),
        ((D,), f32),
    ]
    return pl.pallas_call(
        finish_kernel,
        out_shape=tuple(jax.ShapeDtypeStruct(shape, kind) for shape, kind in shapes),
        in_specs=[any_space] * 6,
        out_specs=[any_space] * len(shapes),
        scratch_shapes=[
            pltpu.VMEM(gathered.shape, bf16),
            pltpu.VMEM(table.shape, f32),
            pltpu.VMEM(w_ada.shape, bf16),
            pltpu.VMEM(grads.shape, bf16),
            pltpu.VMEM((seqs, 6 * D), bf16),
            pltpu.VMEM((steps, table.shape[1]), f32),
            pltpu.VMEM(w_ada.shape, f32),
            pltpu.VMEM(grads.shape, f32),
            pltpu.VMEM((8, D), f32),
            pltpu.VMEM(mixed.shape, bf16),
            pltpu.VMEM(grad_tokens.shape, f32),
            [pltpu.VMEM((6 * D,), f32)] + [pltpu.VMEM((D,), f32)] * 4,
            pltpu.SemaphoreType.DMA((48,)),
        ],
        compiler_params=pltpu.CompilerParams(vmem_limit_bytes=56 * 1024 * 1024),
    )(gathered, table, w_ada, grads, mixed, grad_tokens)


def rope_tables():
    half_width = HD // 2
    frequency = np.float32(10000.0) ** (np.float32(-2.0) * np.arange(half_width, dtype=np.float32) / np.float32(HD))
    angles = np.arange(LEN, dtype=np.float32)[None, :] * frequency[:, None]
    return np.cos(angles).astype(np.float32), np.sin(angles).astype(np.float32)


def body(tokens, timestep, token_mask, time_table, w_ada, b_ada, gain_one, w_qkv, w_out, gain_two, w_up, b_up,
         w_down, b_down, cotangent):
    n_wide = lax.axis_size("wide")
    cos_t, sin_t = rope_tables()
    w_qkv_t = jnp.transpose(w_qkv, (0, 2, 1)).reshape(QKV_ROWS, D)
    mixed, grad_tokens, gathered, grads = fused_block(
        n_wide, tokens, cotangent, token_mask, timestep, time_table, w_ada, b_ada, gain_one, w_qkv_t, w_out, gain_two,
        w_up, b_up, w_down, b_down, cos_t, sin_t,
    )
    outs = list(finish(gathered, time_table, w_ada, grads, mixed, grad_tokens))
    outs[6] = jnp.transpose(outs[6].reshape(3, 192, D), (0, 2, 1))
    return tuple(outs)


def solution(mesh):
    return jax.shard_map(
        body,
        mesh=mesh,
        in_specs=(
            P(("wide", "narrow"), None), P("wide"), P(("wide", "narrow")), P(), P(), P(), P(),
            P(None, None, "narrow"), P("narrow", None), P(), P(None, "narrow"), P("narrow"), P("narrow", None), P(),
            P(("wide", "narrow"), None),
        ),
        out_specs=(
            P(("wide", "narrow"), None), P(("wide", "narrow"), None), P(), P(), P(), P(), P(None, None, "narrow"),
            P("narrow", None), P(), P(None, "narrow"), P("narrow"), P("narrow", None), P(),
        ),
        check_vma=False,
    )
```

```python
import functools
import math

import jax
import jax.numpy as jnp
import numpy as np
from jax import lax
from jax.experimental import pallas as pl
from jax.experimental.pallas import tpu as pltpu
from jax.sharding import PartitionSpec as P

D = 768
HD = 64
LEN = 1024
ROWS_LOCAL = 512
SHARD_HEADS = 3
QKV_ROWS = 576
GRAD_ROWS = 2304
MESH = pl.DeviceIdType.MESH
f32 = jnp.float32
bf16 = jnp.bfloat16
norm_eps = 1e-06
highest = lax.Precision.HIGHEST

NN = (((1,), (0,)), ((), ()))
NT = (((1,), (1,)), ((), ()))
TN = (((0,), (0,)), ((), ()))

CHUNKS = {
    "d0": (0, 192),
    "d1": (192, 192),
    "d2": (384, 192),
    "d3": (576, 192),
    "u0": (768, 192),
    "u1": (960, 192),
    "u2": (1152, 192),
    "u3": (1344, 192),
    "o0": (1536, 192),
    "q0": (1728, 192),
    "q1": (1920, 192),
    "q2": (2112, 96),
    "q3": (2208, 96),
}
ORDERS = {
    "d0": (0, "y", 1, 2),
    "d1": (0, "y", "Z"),
    "d2": ("y", 0, "Z"),
    "d3": ("y", 0, "Z"),
    "u0": (0, "y", "Z"),
    "u1": (0, "y", "Z"),
    "u2": (1, 0, "y", 2),
    "u3": (1, "y", 0, 2),
    "o0": ("y", 0, "Z"),
    "q0": ("y", 0, "Z"),
    "q1": ("y", 0, "Z"),
    "q2": ("y", 0, "Z"),
    "q3": ("y", 0, "Z"),
}
PIECES = {
    "q": (3, 2, 0,),
    "o": (3,),
    "u": (3, 2, 1, 0,),
    "d": (2, 2,),
}
LATE_OUT = False
PLACES = (
    "n0", "n1", "p0", "p1", "a0", "a1", "a2", "wq", "p2", "p3", "a3", "a4", "a5", "wo", "o0", "o1", "u3",
    "v0", "v1", "wu", "u4", "u5", "u6", "u7", "f0", "f1", "wd", "f3", "f4", "f5", "f6", "h0", "h1", "i0",
    "b0", "i1", "b1", "i2", "b2", "bx", "i3", "b3", "i4", "b4", "i5", "b5", "by", "c0", "g0", "c1", "g1",
    "g2", "g3",
)
SCHEDULE = {
    "n1": (
        "Wq0",
    ),
    "p0": (
        "Wq1",
    ),
    "a0": (
        "Wq2",
    ),
    "a1": (
        "Wq1", "Wq0", "Wo0",
    ),
    "a2": (
        "Wu0",
    ),
    "p2": (
        "Wu1", "Wo0",
    ),
    "p3": (
        "Wu2",
    ),
    "a3": (
        "Wu0",
    ),
    "a4": (
        "Wu3", "Wu1",
    ),
    "o0": (
        "Wd0",
    ),
    "u3": (
        "Wd1",
    ),
    "v0": (
        "Wd0",
    ),
    "u6": (
        "Wd1",
    ),
    "f0": (
        "d2", "d3", "d1", "d0",
    ),
    "f5": (
        "u2", "u1", "d2", "d1", "u3", "u0",
    ),
    "h0": (
        "d3", "d0",
    ),
    "h1": (
        "o0",
    ),
    "i0": (
        "u2", "d1",
    ),
    "i1": (
        "u1", "d0",
    ),
    "i2": (
        "d2", "u3",
    ),
    "b2": (
        "d1",
    ),
    "bx": (
        "q1", "q3", "o0", "q0", "d0", "q2",
    ),
    "i3": (
        "u1", "u0",
    ),
    "b3": (
        "d2", "d1",
    ),
    "i4": (
        "d3", "u3",
    ),
    "b4": (
        "d0",
    ),
    "i5": (
        "u2", "u1", "d2", "d1",
    ),
    "b5": (
        "d3", "o0",
    ),
    "by": (
        "q1", "u3", "d0",
    ),
    "c0": (
        "u1", "q3", "d2", "d1",
    ),
    "g0": (
        "q1", "d3", "o0",
    ),
    "g1": (
        "q0", "u3", "d0",
    ),
    "g2": (
        "u1", "re", "rl",
    ),
    "g3": (
        "q2", "q3", "q1", "o0", "d3", "u0", "d2", "q3", "u2", "re", "rl", "q1", "o0", "q0", "u0", "u3", "q3",
        "u2", "u1", "q1", "q0", "q2", "u0", "u3", "d3", "re", "rl", "q3", "q2", "q0", "o0", "u0", "re", "q2",
        "u2", "rl", "q1", "q0", "q3", "re", "q2", "re", "u0", "u2", "q0", "rl", "rl", "q2",
    ),
}


def chunk_stages(name, n_bits):
    rows = CHUNKS[name][1]
    out = []
    before_y = True
    order = [dim for dim in ORDERS[name] if dim != "Z"] + list(range(3, n_bits))
    if "Z" in ORDERS[name]:
        order.append("Z")
    for dim in order:
        if dim == "y":
            out.append((dim, False, rows, False))
            before_y = False
        elif dim == "Z":
            out += [("Z1", False, rows, False), ("Z2", False, rows, False), ("Z3", False, rows, False)]
        else:
            halved = rows % 32 == 0
            rows = rows // 2 if halved else rows
            out.append((dim, halved, rows, before_y))
    return out


def recv_rows(n_bits):
    return sum(
        2 * rows if both else rows for name in CHUNKS for _, _, rows, both in chunk_stages(name, n_bits)
    )


def outbox_rows(n_bits):
    return sum(rows for name in CHUNKS for _, halved, rows, both in chunk_stages(name, n_bits) if halved and both)


def remote_count(n_bits):
    count = 15 + 2 * (n_bits + 3)
    for matrix in PIECES:
        count += sum(2 if kind < 2 else 4 for kind in PIECES[matrix])
    for name in CHUNKS:
        for _, halved, _, both in chunk_stages(name, n_bits):
            count += (2 if both else 1) + (1 if halved else 0)
    return count


def dot(left, right, dims):
    return lax.dot_general(left, right, dims, preferred_element_type=f32)


def loop(count, body):
    def step(index, carry):
        body(index)
        return carry

    lax.fori_loop(0, count, step, 0)


def rows_at(offset, size, align):
    if isinstance(offset, int):
        return pl.ds(offset, size)
    return pl.ds(pl.multiple_of(offset, align), size)


def normalize(values):
    centered = values - jnp.mean(values, axis=-1, keepdims=True)
    variance = jnp.mean(centered * centered, axis=-1, keepdims=True)
    inverse = lax.rsqrt(variance + norm_eps)
    return centered * inverse, inverse


def norm_grad(vhat, inverse, e_hat):
    mean_e = jnp.mean(e_hat, axis=-1, keepdims=True)
    mean_ev = jnp.mean(e_hat * vhat, axis=-1, keepdims=True)
    return inverse * (e_hat - mean_e - vhat * mean_ev)


def block_kernel(
    n_bits,
    tok_in, cot_in, mask_in, step_in, table_in, w_ada_in, b_ada_in, gain_one_in, wqkv_in, wout_in, gain_two_in,
    wup_in, bup_in, wdown_in, b_down_in, cos_in, sin_in,
    mixed_out, grad_tok_out, gathered_out, grads_out,
    tok, cot, gb, n2, normed, wqkv, wout, wup, wdown, proj, ho, do, lse, attn, mid, part, hidden, gel,
    grad_mid, send_a, recv_a, recv_b, recv_c, acc, oth, stage,
    mod, vec, bup, ada_line, lines, mask_line, cos_t, sin_t, sums, sums_recv, sums_low,
    ssem, rsem, lsem, stage_recv, table, w_ada,
):
    wide = lax.axis_index("wide")
    narrow = lax.axis_index("narrow")
    core = lax.rem(narrow, 2)
    chip_y = lax.div(narrow, 2)
    sib = (wide, narrow + 1 - 2 * core)
    across = (wide, lax.rem(narrow + 2, 4))

    def wide_bit(level):
        return lax.rem(lax.div(wide, 1 << level), 2)

    def wide_peer(level):
        return (wide + (1 << level) * (1 - 2 * wide_bit(level)), narrow)

    bit_lo, bit_hi = wide_bit(1), wide_bit(2)
    at_end = bit_lo == bit_hi
    inner_peer = (wide + 2 * (1 - 2 * bit_lo) + 4 * (1 - 2 * bit_hi), narrow)
    peers = [sib, across, inner_peer] + [wide_peer(level) for level in range(n_bits)]
    own0 = core * ROWS_LOCAL
    sib0 = (1 - core) * ROWS_LOCAL

    n_sems = {"remote": 0, "local": 0}

    def remote(src, dst, peer):
        at = n_sems["remote"]
        n_sems["remote"] += 1
        return pltpu.make_async_remote_copy(
            src_ref=src, dst_ref=dst, send_sem=ssem.at[at], recv_sem=rsem.at[at],
            device_id=peer, device_id_type=MESH,
        )

    def local(src, dst):
        at = n_sems["local"]
        n_sems["local"] += 1
        return pltpu.make_async_copy(src, dst, lsem.at[at])

    c_tok = local(tok_in, tok)
    c_cot = local(cot_in, cot)
    c_small = [
        local(b_ada_in, ada_line),
        local(gain_one_in, lines[0]),
        local(gain_two_in, lines[1]),
        local(b_down_in, lines[2]),
        local(bup_in, bup[0]),
        local(mask_in, mask_line),
        local(cos_in, cos_t),
        local(sin_in, sin_t),
    ]
    c_ada = [local(table_in, table), local(w_ada_in, w_ada)]
    c_wqkv = local(wqkv_in, wqkv.at[0])
    c_wout = local(wout_in, wout.at[pl.ds(0, 192)])
    c_wup = local(wup_in, wup.at[:, pl.ds(0, D)])
    c_wdown = local(wdown_in, wdown.at[pl.ds(0, D)])
    barrier = pltpu.get_barrier_semaphore()
    for peer in peers:
        pl.semaphore_signal(barrier, inc=1, device_id=peer, device_id_type=MESH)
    c_tok.start()
    for copy in c_small + c_ada:
        copy.start()
    c_wqkv.start()
    c_cot.start()
    c_wout.start()
    c_wup.start()
    c_wdown.start()

    pl.semaphore_wait(barrier, len(peers))

    r_tok = remote(tok_in, n2.at[rows_at(own0, ROWS_LOCAL, 512)], sib)
    r_cot = remote(cot, gb.at[rows_at(own0, ROWS_LOCAL, 512)], sib)
    r_tok.start()

    places = {
        "q": (wqkv_in, lambda rows: wqkv.at[1, rows], QKV_ROWS, 0),
        "o": (wout_in, lambda rows: wout.at[rows], 192, 192),
        "u": (wup_in, lambda rows: wup.at[rows, pl.ds(D, D)], D, 0),
        "d": (wdown_in, lambda rows: wdown.at[rows], D, D),
    }
    w_across, w_sent, w_last, plans = {}, {}, {}, {}
    piece_keys = []
    ahead = 6

    def pass_on(at, arrived, copies):
        arrived.wait_recv()
        for copy in copies:
            copy.start()
        if at is not None and at + ahead < len(piece_keys):
            w_across[piece_keys[at + ahead]].start()

    for matrix in PIECES:
        source, target, total_rows, shift = places[matrix]
        count = len(PIECES[matrix])
        for piece in range(count):
            kind = PIECES[matrix][piece]
            at = len(piece_keys)
            key = "W" + matrix + str(piece)
            piece_keys.append(key)
            first = piece * (total_rows // count)
            if kind < 2:
                size = total_rows // (2 * count)
                row = first + wide_bit(kind) * size
                here = target(rows_at(shift + row, size, 16))
                along = remote(here, here, wide_peer(kind))
                w_sent[key], w_last[key] = [along], [along]
                steps = [(at, [along])]
            else:
                size = total_rows // (4 * count)
                bits = (wide_bit(0), wide_bit(1))

                def quarter(bit_0, bit_1):
                    return target(rows_at(shift + first + (2 * bit_0 + bit_1) * size, size, 16))

                row = first + (2 * bits[0] + bits[1]) * size
                here = quarter(*bits)
                along = [remote(here, here, wide_peer(level)) for level in (0, 1)]
                theirs = quarter(1 - bits[0], bits[1]) if kind == 2 else quarter(bits[0], 1 - bits[1])
                last = remote(theirs, theirs, wide_peer(3 - kind))
                w_sent[key], w_last[key] = along + [last], [along[3 - kind], last]
                steps = [(at, along), (along[kind - 2], [last])]
            w_across[key] = remote(source.at[rows_at(row, size, 16)], here, across)
            plans[key] = [functools.partial(pass_on, at, w_across[key], steps[0][1])]
            plans[key] += [functools.partial(pass_on, None, arrived, copies) for arrived, copies in steps[1:]]
    r_bup = remote(bup_in, bup[1], across)
    for key in piece_keys[:ahead]:
        w_across[key].start()
    r_bup.start()

    def segment(name, index):
        offset, rows = CHUNKS[name]
        for dim, halved, count, _ in chunk_stages(name, n_bits)[:index]:
            if halved:
                offset = offset + wide_bit(dim) * count
                rows = count
        return offset, rows

    stage_copies, back_copies, stage_base, returns, final_copies, outbox = {}, {}, {}, {}, {}, {}
    stage_rows_used = 0
    base = 0
    for name in CHUNKS:
        for index, (dim, halved, count, both) in enumerate(chunk_stages(name, n_bits)):
            offset, _ = segment(name, index)
            stage_base[name, index] = base
            if dim == "y":
                sent, peer = [oth], across
            elif dim in ("Z1", "Z2", "Z3"):
                sent, peer = [acc], inner_peer if dim == "Z2" else wide_peer(1)
            else:
                sent, peer = [acc, oth] if both else [acc], wide_peer(dim)
                if halved:
                    offset = offset + (1 - wide_bit(dim)) * count
            copies = []
            for array in sent:
                landing = stage_recv.at[pl.ds(base, count)]
                source = array.at[rows_at(offset, count, 16)]
                if halved and array is acc:
                    if both:
                        outbox[name, index] = (stage, stage_rows_used)
                        source = stage.at[pl.ds(stage_rows_used, count)]
                        stage_rows_used += count
                    else:
                        outbox[name, index] = (oth, offset)
                        source = oth.at[rows_at(offset, count, 16)]
                copies.append(remote(source, landing, peer))
                base += count
            stage_copies[name, index] = copies
            if halved:
                offset, count = segment(name, index + 1)
                rows = acc.at[rows_at(offset, count, 16)]
                back_copies[name, index] = remote(rows, rows, peer)
    for name in CHUNKS:
        returns[name] = [at for at in range(len(chunk_stages(name, n_bits))) if (name, at) in back_copies]
        first, count = CHUNKS[name]
        final_copies[name] = local(acc.at[pl.ds(first, count)], grads_out.at[pl.ds(first, count)])

    def start_stage(name, index):
        if index == 0 and (name, 0) in outbox:
            offset, _ = segment(name, 0)
            dim, _, count, _ = chunk_stages(name, n_bits)[0]
            box, row0 = outbox[name, 0]
            box[pl.ds(row0, count), :] = acc[rows_at(offset + (1 - wide_bit(dim)) * count, count, 16), :]
        for copy in stage_copies[name, index]:
            copy.start()

    def merge_step(name, index):
        stages = chunk_stages(name, n_bits)
        before = stages[index - 1][0]
        copies = stage_copies[name, index - 1]
        offset, rows = segment(name, index)
        both_before = len(copies) == 2
        base = stage_base[name, index - 1]

        def merge(array, row0, count, box=None, replace=False):
            start = base + rows if array is oth else base
            step = 48 if count % 48 == 0 else 16
            target, target0 = box or (array, row0)

            def one(at):
                row = row0 + step * at
                here = rows_at(row, step, 16)
                value = stage_recv[rows_at(start + row - offset, step, 16), :]
                if not replace:
                    value = (array[here, :].astype(f32) + value.astype(f32)).astype(bf16)
                target[rows_at(target0 + step * at, step, 16), :] = value

            loop(count // step, one)

        def go_on():
            if index == len(stages):
                back_copies[name, returns[name][-1]].start()
            else:
                start_stage(name, index)

        if before == "Z1":

            @pl.when(at_end)
            def _():
                copies[0].wait_send()

            @pl.when(jnp.logical_not(at_end))
            def _():
                copies[0].wait_recv()
                merge(acc, offset, rows)
                go_on()

            return
        if before == "Z2":

            @pl.when(jnp.logical_not(at_end))
            def _():
                copies[0].wait()
                merge(acc, offset, rows)
                go_on()

            return
        if before == "Z3":

            @pl.when(at_end)
            def _():
                copies[0].wait_recv()
                merge(acc, offset, rows, replace=True)

            @pl.when(jnp.logical_not(at_end))
            def _():
                copies[0].wait_send()

            go_on()
            return
        for copy in copies:
            copy.wait()
        arrays = [acc, oth] if both_before else [acc]
        if index == len(stages):
            merge(acc, offset, rows)
            go_on()
            return
        dim, halved, count, _ = stages[index]
        if dim == "y":
            for array in reversed(arrays):
                merge(array, offset, rows)
                if array is oth or not both_before:
                    start_stage(name, index)
        elif dim == "Z1":
            merge(acc, offset, rows)

            @pl.when(at_end)
            def _():
                start_stage(name, index)

        elif halved:
            for array in arrays:
                box = outbox[name, index] if array is acc else None
                merge(array, offset + (1 - wide_bit(dim)) * count, count, box)
            start_stage(name, index)
            for array in arrays:
                merge(array, offset + wide_bit(dim) * count, count)
        else:
            merge(acc, offset, rows)
            start_stage(name, index)

    def back_step(name, at):
        back_copies[name, returns[name][at]].wait()
        if at > 0:
            back_copies[name, returns[name][at - 1]].start()
        else:
            final_copies[name].start()

    for name in CHUNKS:
        plan = [functools.partial(start_stage, name, 0)]
        plan += [functools.partial(merge_step, name, index + 1) for index in range(len(chunk_stages(name, n_bits)))]
        plan += [functools.partial(back_step, name, at) for at in reversed(range(len(returns[name])))]
        plans[name] = plan

    place = 2 * wide + chip_y
    r_sib, row_copies, own_rows = [], [], []
    for part_index in range(2):
        mine = gathered_out.at[part_index, core]
        r_sib.append(remote(sums.at[part_index], sums_recv.at[part_index], sib))
        own_rows.append(local(sums_low.at[part_index], mine.at[place]))
        copies = [remote(sums_low.at[part_index], mine.at[place], across)]
        for level in range(n_bits):
            count = 2 << level
            rows = mine.at[pl.ds(lax.div(place, count) * count, count)]
            copies.append(remote(rows, rows, wide_peer(level)))
        copies.append(remote(mine, mine, sib))
        row_copies.append(copies)

    def row_step(part_index, at):
        if at == 0:
            own_rows[part_index].start()
        if at == 1:
            own_rows[part_index].wait()
        if at > 0:
            row_copies[part_index][at - 1].wait()
        if at < n_bits + 2:
            row_copies[part_index][at].start()

    for part_index, key in enumerate(("re", "rl")):
        plans[key] = [functools.partial(row_step, part_index, at) for at in range(n_bits + 3)]

    def sums_ready(part_index):
        r_sib[part_index].wait()
        cols = rows_at(core * 384, 384, 128)
        total = sums[part_index, :, cols] + sums_recv[part_index, :, cols]
        sums_low[part_index] = total.astype(bf16)

    steps_at = {}
    for name in PLACES:
        if name[0] == "w":
            keys = [key for key in piece_keys if key[1] == name[1]]
            steps_at[name] = [step for key in keys for step in plans.pop(key)]
        else:
            steps_at[name] = [plans[key].pop(0) for key in SCHEDULE.get(name, ()) if plans.get(key)]
    while any(plans.values()):
        steps_at["g3"] += [plans[key].pop(0) for key in plans if plans[key]]

    def point(name):
        for step in steps_at[name]:
            step()

    def need(matrix):
        point("w" + matrix)
        for key in piece_keys:
            if key[1] == matrix:
                for copy in w_last[key]:
                    copy.wait_recv()

    for copy in c_small:
        copy.wait()
    time_step = step_in[chip_y]
    for row in range(3):
        vec[row : row + 1, :] = lines[row][...].reshape(1, D)

    for copy in c_ada:
        copy.wait()
    picked = table[pl.ds(time_step, 1), :]
    vec[3:4, 0:128] = picked
    cond = picked / (1.0 + jnp.exp(-picked))
    cond = jnp.broadcast_to(cond, (16, 128)).astype(bf16)
    for index in range(6):
        flat = dot(cond, w_ada[:, index * D : (index + 1) * D], NN)
        mod[index : index + 1, :] = ada_line[pl.ds(index * D, D)].reshape(1, D) + flat[0:1, :]

    def first_norm(source, src0, dst0):
        def one(index):
            values = source[rows_at(src0 + 128 * index, 128, 128), :].astype(f32)
            vhat, _ = normalize(values)
            out = vhat * vec[0:1, :] * (1.0 + mod[1:2, :]) + mod[0:1, :]
            normed[rows_at(dst0 + 128 * index, 128, 128), :] = out.astype(bf16)

        loop(4, one)

    c_tok.wait()
    first_norm(tok, 0, own0)
    point("n0")
    r_tok.wait_recv()
    first_norm(n2, sib0, sib0)
    c_cot.wait()
    mask = jnp.broadcast_to(mask_line[...].astype(f32).reshape(1, ROWS_LOCAL), (8, ROWS_LOCAL)).T[:, 0:1]
    cot[...] = (cot[...].astype(f32) * mask).astype(bf16)
    r_cot.start()
    point("n1")

    def project(shard):
        def one(index):
            cols = rows_at(256 * index, 256, 256)
            flat = dot(wqkv[shard], normed[cols, :], NT)
            cos_b, sin_b = cos_t[:, cols], sin_t[:, cols]
            for kind in (0, 1):
                scale = 0.125 if kind == 0 else 1.0
                for head in range(SHARD_HEADS):
                    at = kind * 192 + head * HD
                    low, high = flat[at : at + 32], flat[at + 32 : at + 64]
                    proj[shard, at : at + 32, cols] = ((low * cos_b - high * sin_b) * scale).astype(bf16)
                    proj[shard, at + 32 : at + 64, cols] = ((high * cos_b + low * sin_b) * scale).astype(bf16)
            proj[shard, 384:576, cols] = flat[384:576].astype(bf16)
            point_in("p", 2 * shard + lax.div(index, 2), lax.rem(index, 2) == 1, 4)

        loop(4, one)

    def point_in(prefix, index, last, count):
        for place in range(count):
            if steps_at.get(prefix + str(place)) and (prefix, place) != ("u", 3):

                @pl.when((index == place) & last)
                def _():
                    point(prefix + str(place))

    def head_rows(kind, head):
        return rows_at(kind * 192 + head * HD, HD, HD)

    def attend(shard, head):
        q_t = proj[shard, head_rows(0, head), :]
        k_t = proj[shard, head_rows(1, head), :]
        v_t = proj[shard, head_rows(2, head), :]
        scores = dot(k_t, q_t, TN)
        top = jnp.max(scores, axis=0, keepdims=True)
        weights = jnp.exp(scores - top)
        total = jnp.sum(weights, axis=0, keepdims=True)
        out = dot(v_t, weights.astype(bf16), NN) * (1.0 / total)
        index = shard * SHARD_HEADS + head
        ho[rows_at(index * HD, HD, HD), :] = out.astype(bf16)
        lse[index, 0:1, :] = top + jnp.log(total)

    c_wqkv.wait()

    def shard_heads(shard):
        @pl.when(shard == 1)
        def _():
            need("q")

        project(shard)

        def one(head):
            attend(shard, head)
            point_in("a", SHARD_HEADS * shard + head, True, 6)

        loop(SHARD_HEADS, one)

    loop(2, shard_heads)

    c_wout.wait()
    need("o")
    half = 256

    def exchange_start(recv, index):
        rows = pl.ds(half * index, half)
        copy = remote(send_a.at[rows], recv.at[rows], sib)
        copy.start()
        return copy

    r_attn = []
    for index in range(2):
        out = dot(ho[:, rows_at(sib0 + half * index, half, half)], wout[...], TN)
        send_a[half * index : half * (index + 1), :] = out.astype(bf16)
        r_attn.append(exchange_start(recv_a, index))
    for index in range(2):
        out = dot(ho[:, rows_at(own0 + half * index, half, half)], wout[...], TN)
        attn[half * index : half * (index + 1), :] = out
    point("o0")
    r_n2 = []
    for index in range(2):
        r_attn[index].wait_recv()

        def second_norm(sub):
            rows = rows_at(half * index + 128 * sub, 128, 128)
            value = attn[rows, :] + recv_a[rows, :].astype(f32)
            attn[rows, :] = value
            residual = tok[rows, :].astype(f32) + mod[2:3, :] * value
            mid[rows, :] = residual
            vhat, _ = normalize(residual)
            out = vhat * vec[1:2, :] * (1.0 + mod[4:5, :]) + mod[3:4, :]
            n2[rows_at(own0 + half * index + 128 * sub, 128, 128), :] = out.astype(bf16)

        loop(2, second_norm)
        rows = rows_at(own0 + half * index, half, half)
        r_n2.append(remote(n2.at[rows], n2.at[rows], sib))
        r_n2[index].start()
        r_attn[index].wait_send()

    r_cot.wait_recv()

    def branch_grad(index):
        rows = rows_at(own0 + 128 * index, 128, 128)
        part_rows = rows_at(128 * index, 128, 128)
        gb[rows, :] = (cot[part_rows, :].astype(f32) * mod[5:6, :]).astype(bf16)
        rows = rows_at(sib0 + 128 * index, 128, 128)
        gb[rows, :] = (gb[rows, :].astype(f32) * mod[5:6, :]).astype(bf16)

    r_cot.wait_send()
    loop(4, branch_grad)
    point("o1")

    c_wup.wait()
    r_bup.wait_recv()
    for row in range(2):
        vec[4 + row : 5 + row, :] = bup[row][...].reshape(1, D)
    gelu_c = math.sqrt(2.0 / math.pi)

    def up(shard, block):
        @pl.when((shard == 0) & (block == 2))
        def _():
            r_n2[0].wait_recv()
            r_n2[1].wait_recv()

        rows = rows_at(lax.rem(own0 + 256 * block, LEN), 256, 256)
        cols = rows_at(shard * D, D, D)
        pre = dot(n2[rows, :], wup[:, cols], NN) + vec[pl.ds(4 + shard, 1), :]
        square = pre * pre
        squash = jnp.tanh(gelu_c * pre * (1.0 + 0.044715 * square))
        gate = 0.5 * (1.0 + squash)
        hidden[rows, cols] = (pre * gate).astype(bf16)
        slope = gate + 0.5 * pre * (1.0 - squash * squash) * (gelu_c * (1.0 + 3.0 * 0.044715 * square))
        gel[rows, cols] = slope.astype(bf16)

    loop(4, functools.partial(up, 0))
    point("u3")

    def w_down_grad(shard, target, base):
        def one(index):
            cols = rows_at(shard * D + 256 * index, 256, 256)
            out = dot(hidden[:, cols], gb[...], TN)
            target[rows_at(base + 256 * index, 256, 256), :] = out.astype(bf16)

        loop(3, one)

    w_down_grad(0, acc, 0)
    point("v0")
    sums[...] = jnp.zeros_like(sums)
    c_wdown.wait()

    def hidden_grad(shard, row):
        def one(index):
            rows = rows_at(256 * index, 256, 256)
            cols = pl.ds(shard * D, D)
            grad_act = dot(gb[rows, :], wdown[pl.ds(shard * D, D), :], NT)
            low = (grad_act * gel[rows, cols].astype(f32)).astype(bf16)
            gel[rows, cols] = low
            line = pl.ds(row, 1)
            sums[1, line, :] = sums[1, line, :] + jnp.sum(low.astype(f32), axis=0, keepdims=True)

        loop(4, one)

    def w_up_grad(shard, target):
        def one(index):
            cols = rows_at(256 * index, 256, 256)
            out = dot(n2[:, cols], gel[:, pl.ds(shard * D, D)], TN)
            target[rows_at(D + 256 * index, 256, 256), :] = out.astype(bf16)

        loop(3, one)

    hidden_grad(0, 3 + narrow)
    point("v1")
    need("u")

    def up_other(block):
        up(1, block)
        point_in("u", block + 4, True, 8)

    loop(4, up_other)
    w_down_grad(1, oth, 0)
    point("f0")
    w_up_grad(0, acc)
    point("f1")
    need("d")
    hidden_grad(1, 3 + lax.rem(narrow + 2, 4))
    point("f3")

    r_gn2 = []
    for index in range(2):
        out = dot(gel[rows_at(sib0 + half * index, half, half), :], wup[...], NT)
        send_a[half * index : half * (index + 1), :] = out.astype(bf16)
        r_gn2.append(exchange_start(recv_b, index))
    for index in range(2):
        out = dot(gel[rows_at(own0 + half * index, half, half), :], wup[...], NT)
        part[half * index : half * (index + 1), :] = out
    point("f4")
    w_up_grad(1, oth)
    point("f5")

    r_ga = []
    for index in range(2):
        r_gn2[index].wait()

        def second_back(sub):
            rows = rows_at(half * index + 128 * sub, 128, 128)
            upstream = part[rows, :] + recv_b[rows, :].astype(f32)
            vhat, inverse = normalize(mid[rows, :])
            scaled = upstream * (1.0 + mod[4:5, :])
            grad_mixed = cot[rows, :].astype(f32)
            value = grad_mixed + norm_grad(vhat, inverse, scaled * vec[1:2, :])
            grad_mid[rows, :] = value
            gb[rows_at(own0 + half * index + 128 * sub, 128, 128), :] = (value * mod[2:3, :]).astype(bf16)
            add_sum(0, 0, value * attn[rows, :])
            add_sum(0, 1, upstream)
            add_sum(0, 2, upstream * (vhat * vec[1:2, :]))
            add_sum(0, 4, scaled * vhat)
            add_sum(0, 5, grad_mixed * mod[5:6, :])

        def add_sum(part_index, row, values):
            line = slice(row, row + 1)
            sums[part_index, line, :] = sums[part_index, line, :] + jnp.sum(values, axis=0, keepdims=True)

        loop(2, second_back)
        rows = rows_at(own0 + half * index, half, half)
        r_ga.append(remote(gb.at[rows], gb.at[rows], sib))
        r_ga[index].start()
    point("f6")

    r_ga[0].wait_recv()
    r_ga[1].wait_recv()

    def head_grad(index):
        cols = rows_at(256 * index, 256, 256)
        do[:, cols] = dot(wout[...], gb[cols, :], NT).astype(bf16)

    loop(4, head_grad)
    point("h0")

    def w_out_grad():
        oth[1536:1728, :] = dot(ho[192:384, :], gb[...], NN).astype(bf16)
        acc[1536:1728, :] = dot(ho[0:192, :], gb[...], NN).astype(bf16)
        point("h1")

    if not LATE_OUT:
        w_out_grad()

    def attend_back(shard, head, between):
        q_t = proj[shard, head_rows(0, head), :]
        k_t = proj[shard, head_rows(1, head), :]
        v_t = proj[shard, head_rows(2, head), :]
        index = shard * SHARD_HEADS + head
        d_t = do[rows_at(index * HD, HD, HD), :]
        probs = jnp.exp(dot(k_t, q_t, TN) - lse[index, 0:1, :])
        grad_probs = dot(v_t, d_t, TN)
        inner = jnp.sum(probs * grad_probs, axis=0, keepdims=True)
        grad_scores = (probs * (grad_probs - inner)).astype(bf16)
        between()
        dq_t = dot(k_t, grad_scores, NN) * 0.125
        dk_t = dot(grad_scores, q_t, NT).T
        dv_t = dot(probs.astype(bf16), d_t, NT).T
        for kind, grad in ((0, dq_t), (1, dk_t)):
            low, high = grad[:32], grad[32:]
            turned = jnp.concatenate(
                [low * cos_t[...] + high * sin_t[...], high * cos_t[...] - low * sin_t[...]], axis=0
            )
            proj[shard, head_rows(kind, head), :] = turned.astype(bf16)
        proj[shard, head_rows(2, head), :] = dv_t.astype(bf16)

    for key in piece_keys:
        for copy in w_sent[key] + [w_across[key]]:
            copy.wait_send()

    def w_qkv_grad(shard, target):
        def one(index):
            rows = rows_at(192 * index, 192, 64)
            out = dot(proj[shard, rows, :], normed[...], NN)
            target[rows_at(1728 + 192 * index, 192, 64), :] = out.astype(bf16)

        loop(3, one)

    def back_heads(index):
        shard = 1 - lax.div(index, SHARD_HEADS)
        head = lax.rem(index, SHARD_HEADS)
        attend_back(shard, head, lambda: point_in("i", index, True, 6))
        point_in("b", index, True, 6)

        @pl.when(index == 2)
        def _():
            w_qkv_grad(1, oth)
            point("bx")

    loop(6, back_heads)
    w_qkv_grad(0, acc)
    point("by")
    if LATE_OUT:
        w_out_grad()

    r_branch = []
    for index in range(2):
        out = dot(hidden[rows_at(sib0 + half * index, half, half), :], wdown[...], NN)
        send_a[half * index : half * (index + 1), :] = out.astype(bf16)
        r_branch.append(exchange_start(recv_c, index))
    for index in range(2):
        out = dot(hidden[rows_at(own0 + half * index, half, half), :], wdown[...], NN)
        part[half * index : half * (index + 1), :] = out
    point("c0")


    def normed_grad(offset):
        first = dot(proj[0, :, offset], wqkv[0], TN)
        return first + dot(proj[1, :, offset], wqkv[1], TN)

    r_gn = []
    for index in range(2):
        rows = pl.ds(half * index, half)
        recv_b[rows, :] = normed_grad(rows_at(sib0 + half * index, half, half)).astype(bf16)
        r_gn.append(remote(recv_b.at[rows], recv_a.at[rows], sib))
        r_gn[index].start()
    for index in range(2):
        attn[half * index : half * (index + 1), :] = normed_grad(rows_at(own0 + half * index, half, half))
    point("g0")

    def finish_branch(index):
        rows = rows_at(128 * index, 128, 128)
        branch = part[rows, :] + recv_c[rows, :].astype(f32) + vec[2:3, :]
        add_sum(0, 3, cot[rows, :].astype(f32) * branch)
        send_a[rows, :] = (mid[rows, :] + mod[5:6, :] * branch).astype(bf16)

    r_branch[0].wait()
    r_branch[1].wait()
    loop(4, finish_branch)
    c_mixed = local(send_a, mixed_out)
    c_mixed.start()
    on_first = (1 - core).astype(f32)
    high = lax.div(time_step, 32)
    picked = vec[3:4, 0:128]
    sigma = 1.0 / (1.0 + jnp.exp(-picked))
    slope = sigma * (1.0 + picked * (1.0 - sigma))
    slope_high = slope.astype(bf16).astype(f32)
    entries = [
        jnp.full((1, 128), high.astype(f32)),
        jnp.full((1, 128), (time_step - 32 * high).astype(f32)),
        (picked / (1.0 + jnp.exp(-picked))).astype(bf16).astype(f32),
        slope_high,
        slope - slope_high,
    ]
    for at, entry in enumerate(entries):
        sums[0, 6:7, 128 * at : 128 * (at + 1)] = entry * on_first
    r_sib[0].start()
    point("c1")

    for index in range(2):
        r_gn[index].wait()

        def first_back(sub):
            rows = rows_at(half * index + 128 * sub, 128, 128)
            upstream = attn[rows, :] + recv_a[rows, :].astype(f32)
            vhat, inverse = normalize(tok[rows, :].astype(f32))
            scaled = upstream * (1.0 + mod[1:2, :])
            attn[rows, :] = grad_mid[rows, :] + norm_grad(vhat, inverse, scaled * vec[0:1, :])
            add_sum(1, 0, upstream)
            add_sum(1, 1, upstream * (vhat * vec[0:1, :]))
            add_sum(1, 2, scaled * vhat)

        loop(2, first_back)
    c_grad_tok = local(attn, grad_tok_out)
    c_grad_tok.start()

    r_sib[1].start()
    point("g1")
    sums_ready(0)
    sums_ready(1)
    point("g2")
    point("g3")
    for name in CHUNKS:
        final_copies[name].wait()
    c_grad_tok.wait()
    c_mixed.wait()
    for copy in [r_tok, r_bup] + r_n2 + r_ga:
        copy.wait_send()


def fused_block(n_wide, tokens, cot, mask, timestep, table, w_ada, b_ada, gain_one, w_qkv_t, w_out, gain_two, w_up, b_up,
                w_down, b_down, cos_t, sin_t):
    n_bits = n_wide.bit_length() - 1
    any_space = pl.BlockSpec(memory_space=pl.ANY)
    scratch = [
        pltpu.VMEM((ROWS_LOCAL, D), bf16),
        pltpu.VMEM((ROWS_LOCAL, D), bf16),
        pltpu.VMEM((LEN, D), bf16),
        pltpu.VMEM((LEN, D), bf16),
        pltpu.VMEM((LEN, D), bf16),
        pltpu.VMEM((2, QKV_ROWS, D), bf16),
        pltpu.VMEM((384, D), bf16),
        pltpu.VMEM((D, 2 * D), bf16),
        pltpu.VMEM((2 * D, D), bf16),
        pltpu.VMEM((2, QKV_ROWS, LEN), bf16),
        pltpu.VMEM((384, LEN), bf16),
        pltpu.VMEM((384, LEN), bf16),
        pltpu.VMEM((6, 8, LEN), f32),
        pltpu.VMEM((ROWS_LOCAL, D), f32),
        pltpu.VMEM((ROWS_LOCAL, D), f32),
        pltpu.VMEM((ROWS_LOCAL, D), f32),
        pltpu.VMEM((LEN, 2 * D), bf16),
        pltpu.VMEM((LEN, 2 * D), bf16),
        pltpu.VMEM((ROWS_LOCAL, D), f32),
        pltpu.VMEM((ROWS_LOCAL, D), bf16),
        pltpu.VMEM((ROWS_LOCAL, D), bf16),
        pltpu.VMEM((ROWS_LOCAL, D), bf16),
        pltpu.VMEM((ROWS_LOCAL, D), bf16),
        pltpu.VMEM((GRAD_ROWS, D), bf16),
        pltpu.VMEM((GRAD_ROWS, D), bf16),
        pltpu.VMEM((outbox_rows(n_bits), D), bf16),
        pltpu.VMEM((8, D), f32),
        pltpu.VMEM((8, D), f32),
        [pltpu.VMEM((D,), f32)] * 2,
        pltpu.VMEM((6 * D,), f32),
        [pltpu.VMEM((D,), f32)] * 3,
        pltpu.VMEM((ROWS_LOCAL,), jnp.int32),
        pltpu.VMEM((32, LEN), f32),
        pltpu.VMEM((32, LEN), f32),
        pltpu.VMEM((2, 8, D), f32),
        pltpu.VMEM((2, 8, D), f32),
        pltpu.VMEM((2, 8, D // 2), bf16),
        pltpu.SemaphoreType.DMA((remote_count(n_bits),)),
        pltpu.SemaphoreType.DMA((remote_count(n_bits),)),
        pltpu.SemaphoreType.DMA((20 + len(CHUNKS),)),
        pltpu.VMEM((recv_rows(n_bits), D), bf16),
        pltpu.VMEM(table.shape, f32),
        pltpu.VMEM(w_ada.shape, bf16),
    ]
    specs = [any_space] * 17
    specs[3] = pl.BlockSpec(memory_space=pltpu.SMEM)
    return pl.pallas_call(
        functools.partial(block_kernel, n_bits),
        out_shape=(
            jax.ShapeDtypeStruct((ROWS_LOCAL, D), bf16),
            jax.ShapeDtypeStruct((ROWS_LOCAL, D), f32),
            jax.ShapeDtypeStruct((2, 2, 2 * n_wide, 8, D // 2), bf16),
            jax.ShapeDtypeStruct((GRAD_ROWS, D), bf16),
        ),
        in_specs=specs,
        out_specs=[any_space] * 4,
        scratch_shapes=scratch,
        compiler_params=pltpu.CompilerParams(
            collective_id=0, has_side_effects=True, vmem_limit_bytes=61 * 1024 * 1024
        ),
    )(tokens, cot, mask, timestep, table, w_ada, b_ada, gain_one, w_qkv_t, w_out, gain_two, w_up, b_up, w_down, b_down,
      cos_t, sin_t)


def finish_kernel(
    gathered_in, w_ada_in, grads_in, mixed_in, grad_tok_in,
    mixed_out, grad_tok_out, g_table, g_w_ada, g_b_ada, g_gain_one, g_wqkv, g_wout, g_gain_two, g_wup, g_bup,
    g_wdown, g_b_down,
    gathered, w_ada, grads, mod_low, table_out, ada_out, wide_out, late_sum, mixed_buf, tok_buf, lines, sem,
):
    pieces = GRAD_ROWS // 192
    targets = [(g_wdown, 0), (g_wup, 768), (g_wout, 1536), (g_wqkv, 1728)]
    loads = [(gathered_in, gathered), (w_ada_in, w_ada)]
    loads = [pltpu.make_async_copy(src, dst, sem.at[at]) for at, (src, dst) in enumerate(loads)]
    pass_in = [
        pltpu.make_async_copy(mixed_in, mixed_buf, sem.at[3]),
        pltpu.make_async_copy(grad_tok_in, tok_buf, sem.at[4]),
    ]
    pass_out = [
        pltpu.make_async_copy(mixed_buf, mixed_out, sem.at[5]),
        pltpu.make_async_copy(tok_buf, grad_tok_out, sem.at[6]),
    ]
    grad_in, grad_out = [], []
    for piece in range(pieces):
        rows = pl.ds(192 * piece, 192)
        grad_in.append(pltpu.make_async_copy(grads_in.at[rows], grads.at[rows], sem.at[7 + piece]))
        target, first = [item for item in targets if item[1] <= 192 * piece][-1]
        grad_out.append(
            pltpu.make_async_copy(
                wide_out.at[rows], target.at[pl.ds(192 * piece - first, 192)], sem.at[7 + pieces + piece]
            )
        )
    for copy in loads + grad_in + pass_in:
        copy.start()

    def widen(piece):
        grad_in[piece].wait()
        rows = pl.ds(192 * piece, 192)
        wide_out[rows, :] = grads[rows, :].astype(f32)
        grad_out[piece].start()

    for piece in range(pieces // 4):
        widen(piece)
    for copy in loads:
        copy.wait()

    def both(index):
        return jnp.concatenate([gathered[index, 0].astype(f32), gathered[index, 1].astype(f32)], axis=-1)

    early, late = both(0), both(1)
    total_early, total_late = jnp.sum(early, axis=0), jnp.sum(late, axis=0)
    late_sum[...] = total_late
    for row, values in enumerate([late[:, 0], late[:, 1], early[:, 0], early[:, 1], early[:, 2], early[:, 3]]):
        mod_low[:, row * D : (row + 1) * D] = values.astype(bf16)
    rows = [total_late[0:1], total_late[1:2]] + [total_early[row : row + 1] for row in range(4)]
    for row, values in enumerate(rows):
        lines[0][pl.ds(row * D, D)] = values.reshape(D)
    lines[1][...] = total_late[2:3].reshape(D)
    lines[2][...] = total_early[4:5].reshape(D)
    lines[3][...] = late_sum[pl.ds(3 + lax.axis_index("narrow"), 1), :].reshape(D)
    lines[4][...] = total_early[5:6].reshape(D)
    line_out = [
        pltpu.make_async_copy(line, out, sem.at[7 + 2 * pieces + at])
        for at, (line, out) in enumerate(zip(lines, (g_b_ada, g_gain_one, g_gain_two, g_bup, g_b_down)))
    ]
    for copy in line_out:
        copy.start()
    seqs, steps = early.shape[0], table_out.shape[0]
    time_step = early[:, 6, 0:1] * 32.0 + early[:, 6, 128:129]
    columns = lax.broadcasted_iota(jnp.int32, (seqs, steps), 1).astype(f32)
    pick = jnp.where(columns == time_step, 1.0, 0.0).astype(bf16)
    cond = early[:, 6, 256:384].astype(bf16)
    ada_out[...] = dot(cond, mod_low[...], TN)
    out_ada = pltpu.make_async_copy(ada_out, g_w_ada, sem.at[7 + 2 * pieces + 5])
    out_ada.start()
    grad_cond = dot(mod_low[...], w_ada[...], NT) * (early[:, 6, 384:512] + early[:, 6, 512:640])
    rest, picked_sum = grad_cond, None
    for _ in range(3):
        low = rest.astype(bf16)
        rest = rest - low.astype(f32)
        term = dot(pick, low, TN)
        picked_sum = term if picked_sum is None else picked_sum + term
    table_out[...] = picked_sum
    out_table = pltpu.make_async_copy(table_out, g_table, sem.at[7 + 2 * pieces + 6])
    out_table.start()
    for piece in range(pieces // 4, pieces):
        widen(piece)
    for at in range(2):
        pass_in[at].wait()
        pass_out[at].start()
    for copy in line_out + [out_ada, out_table] + pass_out + grad_out:
        copy.wait()


def finish(gathered, table, w_ada, grads, mixed, grad_tokens):
    seqs, steps = gathered.shape[2], table.shape[0]
    any_space = pl.BlockSpec(memory_space=pl.ANY)
    shapes = [
        (mixed.shape, bf16), (grad_tokens.shape, f32), (table.shape, f32), (w_ada.shape, f32), ((6 * D,), f32),
        ((D,), f32), ((QKV_ROWS, D), f32), ((192, D), f32), ((D,), f32), ((D, D), f32), ((D,), f32), ((D, D), f32),
        ((D,), f32),
    ]
    return pl.pallas_call(
        finish_kernel,
        out_shape=tuple(jax.ShapeDtypeStruct(shape, kind) for shape, kind in shapes),
        in_specs=[any_space] * 5,
        out_specs=[any_space] * len(shapes),
        scratch_shapes=[
            pltpu.VMEM(gathered.shape, bf16),
            pltpu.VMEM(w_ada.shape, bf16),
            pltpu.VMEM(grads.shape, bf16),
            pltpu.VMEM((seqs, 6 * D), bf16),
            pltpu.VMEM((steps, table.shape[1]), f32),
            pltpu.VMEM(w_ada.shape, f32),
            pltpu.VMEM(grads.shape, f32),
            pltpu.VMEM((8, D), f32),
            pltpu.VMEM(mixed.shape, bf16),
            pltpu.VMEM(grad_tokens.shape, f32),
            [pltpu.VMEM((6 * D,), f32)] + [pltpu.VMEM((D,), f32)] * 4,
            pltpu.SemaphoreType.DMA((48,)),
        ],
        compiler_params=pltpu.CompilerParams(vmem_limit_bytes=56 * 1024 * 1024),
    )(gathered, w_ada, grads, mixed, grad_tokens)


def rope_tables():
    half_width = HD // 2
    frequency = np.float32(10000.0) ** (np.float32(-2.0) * np.arange(half_width, dtype=np.float32) / np.float32(HD))
    angles = np.arange(LEN, dtype=np.float32)[None, :] * frequency[:, None]
    return np.cos(angles).astype(np.float32), np.sin(angles).astype(np.float32)


def body(tokens, timestep, token_mask, time_table, w_ada, b_ada, gain_one, w_qkv, w_out, gain_two, w_up, b_up,
         w_down, b_down, cotangent):
    n_wide = lax.axis_size("wide")
    cos_t, sin_t = rope_tables()
    w_qkv_t = jnp.transpose(w_qkv, (0, 2, 1)).reshape(QKV_ROWS, D)
    mixed, grad_tokens, gathered, grads = fused_block(
        n_wide, tokens, cotangent, token_mask, timestep, time_table, w_ada, b_ada, gain_one, w_qkv_t, w_out, gain_two,
        w_up, b_up, w_down, b_down, cos_t, sin_t,
    )
    outs = list(finish(gathered, time_table, w_ada, grads, mixed, grad_tokens))
    outs[6] = jnp.transpose(outs[6].reshape(3, 192, D), (0, 2, 1))
    return tuple(outs)


def solution(mesh):
    return jax.shard_map(
        body,
        mesh=mesh,
        in_specs=(
            P(("wide", "narrow"), None), P("wide"), P(("wide", "narrow")), P(), P(), P(), P(),
            P(None, None, "narrow"), P("narrow", None), P(), P(None, "narrow"), P("narrow"), P("narrow", None), P(),
            P(("wide", "narrow"), None),
        ),
        out_specs=(
            P(("wide", "narrow"), None), P(("wide", "narrow"), None), P(), P(), P(), P(), P(None, None, "narrow"),
            P("narrow", None), P(), P(None, "narrow"), P("narrow"), P("narrow", None), P(),
        ),
        check_vma=False,
    )
```

```python
import functools
import math

import jax
import jax.numpy as jnp
import numpy as np
from jax import lax
from jax.experimental import pallas as pl
from jax.experimental.pallas import tpu as pltpu
from jax.sharding import PartitionSpec as P

D = 768
HD = 64
LEN = 1024
ROWS_LOCAL = 512
SHARD_HEADS = 3
QKV_ROWS = 576
GRAD_ROWS = 2304
MESH = pl.DeviceIdType.MESH
f32 = jnp.float32
bf16 = jnp.bfloat16
norm_eps = 1e-06
highest = lax.Precision.HIGHEST

NN = (((1,), (0,)), ((), ()))
NT = (((1,), (1,)), ((), ()))
TN = (((0,), (0,)), ((), ()))

CHUNKS = {
    "d0": (0, 192),
    "d1": (192, 192),
    "d2": (384, 192),
    "d3": (576, 192),
    "u0": (768, 192),
    "u1": (960, 192),
    "u2": (1152, 192),
    "u3": (1344, 192),
    "o0": (1536, 192),
    "q0": (1728, 192),
    "q1": (1920, 192),
    "q2": (2112, 96),
    "q3": (2208, 96),
}
ORDERS = {
    "d0": (0, "y", 1, 2),
    "d1": (0, "y", "Z"),
    "d2": ("y", 0, "Z"),
    "d3": ("y", 0, "Z"),
    "u0": (0, "y", "Z"),
    "u1": (0, "y", "Z"),
    "u2": (1, 0, "y", 2),
    "u3": (1, "y", 0, 2),
    "o0": ("y", 0, "Z"),
    "q0": ("y", 0, "Z"),
    "q1": ("y", 0, "Z"),
    "q2": ("y", 0, "Z"),
    "q3": ("y", 0, "Z"),
}
PIECES = {
    "q": (3, 2, 0,),
    "o": (3,),
    "u": (3, 2, 1, 0,),
    "d": (2, 2,),
}
LATE_OUT = False
PLACES = (
    "n0", "n1", "p0", "p1", "a0", "a1", "a2", "wq", "p2", "p3", "a3", "a4", "a5", "wo", "o0", "o1", "u3",
    "v0", "v1", "wu", "u4", "u5", "u6", "u7", "f0", "f1", "wd", "f3", "f4", "f5", "f6", "h0", "h1", "i0",
    "b0", "i1", "b1", "i2", "b2", "bx", "i3", "b3", "i4", "b4", "i5", "b5", "by", "c0", "g0", "c1", "g1",
    "g2", "g3",
)
SCHEDULE = {
    "n1": (
        "Wq0",
    ),
    "p0": (
        "Wq1",
    ),
    "a0": (
        "Wq2",
    ),
    "a1": (
        "Wq1", "Wq0", "Wo0",
    ),
    "a2": (
        "Wu0",
    ),
    "p2": (
        "Wu1", "Wo0",
    ),
    "p3": (
        "Wu2",
    ),
    "a3": (
        "Wu0",
    ),
    "a4": (
        "Wu3", "Wu1",
    ),
    "o0": (
        "Wd0",
    ),
    "u3": (
        "Wd1",
    ),
    "v0": (
        "Wd0",
    ),
    "u6": (
        "Wd1",
    ),
    "f0": (
        "d2", "d3", "d1", "d0",
    ),
    "f5": (
        "u2", "u1", "d2", "d1", "u3", "u0",
    ),
    "h0": (
        "d3", "d0",
    ),
    "h1": (
        "o0",
    ),
    "i0": (
        "u2", "d1",
    ),
    "i1": (
        "u1", "d0",
    ),
    "i2": (
        "d2", "u3",
    ),
    "b2": (
        "d1",
    ),
    "bx": (
        "q1", "q3", "o0", "q0", "d0", "q2",
    ),
    "i3": (
        "u1", "u0",
    ),
    "b3": (
        "d2", "d1",
    ),
    "i4": (
        "d3", "u3",
    ),
    "b4": (
        "d0",
    ),
    "i5": (
        "u2", "u1", "d2", "d1",
    ),
    "b5": (
        "d3", "o0",
    ),
    "by": (
        "q1", "u3", "d0",
    ),
    "c0": (
        "u1", "q3", "d2", "d1",
    ),
    "g0": (
        "q1", "d3", "o0",
    ),
    "g1": (
        "q0", "u3", "d0",
    ),
    "g2": (
        "u1", "re", "rl",
    ),
    "g3": (
        "q2", "q3", "q1", "o0", "d3", "u0", "d2", "q3", "u2", "re", "rl", "q1", "o0", "q0", "u0", "u3", "q3",
        "u2", "u1", "q1", "q0", "q2", "u0", "u3", "d3", "re", "rl", "q3", "q2", "q0", "o0", "u0", "re", "q2",
        "u2", "rl", "q1", "q0", "q3", "re", "q2", "re", "u0", "u2", "q0", "rl", "rl", "q2",
    ),
}


def chunk_stages(name, n_bits):
    rows = CHUNKS[name][1]
    out = []
    before_y = True
    order = [dim for dim in ORDERS[name] if dim != "Z"] + list(range(3, n_bits))
    if "Z" in ORDERS[name]:
        order.append("Z")
    for dim in order:
        if dim == "y":
            out.append((dim, False, rows, False))
            before_y = False
        elif dim == "Z":
            out += [("Z1", False, rows, False), ("Z2", False, rows, False), ("Z3", False, rows, False)]
        else:
            halved = rows % 32 == 0
            rows = rows // 2 if halved else rows
            out.append((dim, halved, rows, before_y))
    return out


def recv_rows(n_bits):
    return sum(
        2 * rows if both else rows for name in CHUNKS for _, _, rows, both in chunk_stages(name, n_bits)
    )


def outbox_rows(n_bits):
    return sum(rows for name in CHUNKS for _, halved, rows, both in chunk_stages(name, n_bits) if halved and both)


def remote_count(n_bits):
    count = 15 + 2 * (n_bits + 3)
    for matrix in PIECES:
        count += sum(2 if kind < 2 else 4 for kind in PIECES[matrix])
    for name in CHUNKS:
        for _, halved, _, both in chunk_stages(name, n_bits):
            count += (2 if both else 1) + (1 if halved else 0)
    return count


def dot(left, right, dims):
    return lax.dot_general(left, right, dims, preferred_element_type=f32)


def loop(count, body):
    def step(index, carry):
        body(index)
        return carry

    lax.fori_loop(0, count, step, 0)


def rows_at(offset, size, align):
    if isinstance(offset, int):
        return pl.ds(offset, size)
    return pl.ds(pl.multiple_of(offset, align), size)


def normalize(values):
    centered = values - jnp.mean(values, axis=-1, keepdims=True)
    variance = jnp.mean(centered * centered, axis=-1, keepdims=True)
    inverse = lax.rsqrt(variance + norm_eps)
    return centered * inverse, inverse


def norm_grad(vhat, inverse, e_hat):
    mean_e = jnp.mean(e_hat, axis=-1, keepdims=True)
    mean_ev = jnp.mean(e_hat * vhat, axis=-1, keepdims=True)
    return inverse * (e_hat - mean_e - vhat * mean_ev)


def block_kernel(
    n_bits,
    tok_in, cot_in, mask_in, step_in, table_in, w_ada_in, b_ada_in, gain_one_in, wqkv_in, wout_in, gain_two_in,
    wup_in, bup_in, wdown_in, b_down_in, cos_in, sin_in,
    mixed_out, grad_tok_out, gathered_out, grads_out,
    tok, cot, gb, n2, normed, wqkv, wout, wup, wdown, proj, ho, do, lse, attn, mid, part, hidden, gel,
    grad_mid, send_a, recv_a, recv_b, recv_c, acc, oth, stage,
    mod, vec, bup, ada_line, lines, mask_line, cos_t, sin_t, sums, sums_recv, sums_low,
    ssem, rsem, lsem, stage_recv, table, w_ada,
):
    wide = lax.axis_index("wide")
    narrow = lax.axis_index("narrow")
    core = lax.rem(narrow, 2)
    chip_y = lax.div(narrow, 2)
    sib = (wide, narrow + 1 - 2 * core)
    across = (wide, lax.rem(narrow + 2, 4))

    def wide_bit(level):
        return lax.rem(lax.div(wide, 1 << level), 2)

    def wide_peer(level):
        return (wide + (1 << level) * (1 - 2 * wide_bit(level)), narrow)

    bit_lo, bit_hi = wide_bit(1), wide_bit(2)
    at_end = bit_lo == bit_hi
    inner_peer = (wide + 2 * (1 - 2 * bit_lo) + 4 * (1 - 2 * bit_hi), narrow)
    peers = [sib, across, inner_peer] + [wide_peer(level) for level in range(n_bits)]
    own0 = core * ROWS_LOCAL
    sib0 = (1 - core) * ROWS_LOCAL

    n_sems = {"remote": 0, "local": 0}

    def remote(src, dst, peer):
        at = n_sems["remote"]
        n_sems["remote"] += 1
        return pltpu.make_async_remote_copy(
            src_ref=src, dst_ref=dst, send_sem=ssem.at[at], recv_sem=rsem.at[at],
            device_id=peer, device_id_type=MESH,
        )

    def local(src, dst):
        at = n_sems["local"]
        n_sems["local"] += 1
        return pltpu.make_async_copy(src, dst, lsem.at[at])

    c_tok = local(tok_in, tok)
    c_cot = local(cot_in, cot)
    c_small = [
        local(b_ada_in, ada_line),
        local(gain_one_in, lines[0]),
        local(gain_two_in, lines[1]),
        local(b_down_in, lines[2]),
        local(bup_in, bup[0]),
        local(mask_in, mask_line),
        local(cos_in, cos_t),
        local(sin_in, sin_t),
    ]
    c_ada = [local(table_in, table), local(w_ada_in, w_ada)]
    c_wqkv = local(wqkv_in, wqkv.at[0])
    c_wout = local(wout_in, wout.at[pl.ds(0, 192)])
    c_wup = local(wup_in, wup.at[:, pl.ds(0, D)])
    c_wdown = local(wdown_in, wdown.at[pl.ds(0, D)])
    barrier = pltpu.get_barrier_semaphore()
    for peer in peers:
        pl.semaphore_signal(barrier, inc=1, device_id=peer, device_id_type=MESH)
    c_tok.start()
    for copy in c_small + c_ada:
        copy.start()
    c_wqkv.start()
    c_cot.start()
    c_wout.start()
    c_wup.start()
    c_wdown.start()

    pl.semaphore_wait(barrier, len(peers))

    r_tok = remote(tok_in, n2.at[rows_at(own0, ROWS_LOCAL, 512)], sib)
    r_cot = remote(cot, gb.at[rows_at(own0, ROWS_LOCAL, 512)], sib)
    r_tok.start()

    places = {
        "q": (wqkv_in, lambda rows: wqkv.at[1, rows], QKV_ROWS, 0),
        "o": (wout_in, lambda rows: wout.at[rows], 192, 192),
        "u": (wup_in, lambda rows: wup.at[rows, pl.ds(D, D)], D, 0),
        "d": (wdown_in, lambda rows: wdown.at[rows], D, D),
    }
    w_across, w_sent, w_last, plans = {}, {}, {}, {}
    piece_keys = []
    ahead = 6

    def pass_on(at, arrived, copies):
        arrived.wait_recv()
        for copy in copies:
            copy.start()
        if at is not None and at + ahead < len(piece_keys):
            w_across[piece_keys[at + ahead]].start()

    for matrix in PIECES:
        source, target, total_rows, shift = places[matrix]
        count = len(PIECES[matrix])
        for piece in range(count):
            kind = PIECES[matrix][piece]
            at = len(piece_keys)
            key = "W" + matrix + str(piece)
            piece_keys.append(key)
            first = piece * (total_rows // count)
            if kind < 2:
                size = total_rows // (2 * count)
                row = first + wide_bit(kind) * size
                here = target(rows_at(shift + row, size, 16))
                along = remote(here, here, wide_peer(kind))
                w_sent[key], w_last[key] = [along], [along]
                steps = [(at, [along])]
            else:
                size = total_rows // (4 * count)
                bits = (wide_bit(0), wide_bit(1))

                def quarter(bit_0, bit_1):
                    return target(rows_at(shift + first + (2 * bit_0 + bit_1) * size, size, 16))

                row = first + (2 * bits[0] + bits[1]) * size
                here = quarter(*bits)
                along = [remote(here, here, wide_peer(level)) for level in (0, 1)]
                theirs = quarter(1 - bits[0], bits[1]) if kind == 2 else quarter(bits[0], 1 - bits[1])
                last = remote(theirs, theirs, wide_peer(3 - kind))
                w_sent[key], w_last[key] = along + [last], [along[3 - kind], last]
                steps = [(at, along), (along[kind - 2], [last])]
            w_across[key] = remote(source.at[rows_at(row, size, 16)], here, across)
            plans[key] = [functools.partial(pass_on, at, w_across[key], steps[0][1])]
            plans[key] += [functools.partial(pass_on, None, arrived, copies) for arrived, copies in steps[1:]]
    r_bup = remote(bup_in, bup[1], across)
    for key in piece_keys[:ahead]:
        w_across[key].start()
    r_bup.start()

    def segment(name, index):
        offset, rows = CHUNKS[name]
        for dim, halved, count, _ in chunk_stages(name, n_bits)[:index]:
            if halved:
                offset = offset + wide_bit(dim) * count
                rows = count
        return offset, rows

    stage_copies, back_copies, stage_base, returns, final_copies, outbox = {}, {}, {}, {}, {}, {}
    stage_rows_used = 0
    base = 0
    for name in CHUNKS:
        for index, (dim, halved, count, both) in enumerate(chunk_stages(name, n_bits)):
            offset, _ = segment(name, index)
            stage_base[name, index] = base
            if dim == "y":
                sent, peer = [oth], across
            elif dim in ("Z1", "Z2", "Z3"):
                sent, peer = [acc], inner_peer if dim == "Z2" else wide_peer(1)
            else:
                sent, peer = [acc, oth] if both else [acc], wide_peer(dim)
                if halved:
                    offset = offset + (1 - wide_bit(dim)) * count
            copies = []
            for array in sent:
                landing = stage_recv.at[pl.ds(base, count)]
                source = array.at[rows_at(offset, count, 16)]
                if halved and array is acc:
                    if both:
                        outbox[name, index] = (stage, stage_rows_used)
                        source = stage.at[pl.ds(stage_rows_used, count)]
                        stage_rows_used += count
                    else:
                        outbox[name, index] = (oth, offset)
                        source = oth.at[rows_at(offset, count, 16)]
                copies.append(remote(source, landing, peer))
                base += count
            stage_copies[name, index] = copies
            if halved:
                offset, count = segment(name, index + 1)
                rows = acc.at[rows_at(offset, count, 16)]
                back_copies[name, index] = remote(rows, rows, peer)
    for name in CHUNKS:
        returns[name] = [at for at in range(len(chunk_stages(name, n_bits))) if (name, at) in back_copies]
        first, count = CHUNKS[name]
        final_copies[name] = local(acc.at[pl.ds(first, count)], grads_out.at[pl.ds(first, count)])

    def start_stage(name, index):
        if index == 0 and (name, 0) in outbox:
            offset, _ = segment(name, 0)
            dim, _, count, _ = chunk_stages(name, n_bits)[0]
            box, row0 = outbox[name, 0]
            box[pl.ds(row0, count), :] = acc[rows_at(offset + (1 - wide_bit(dim)) * count, count, 16), :]
        for copy in stage_copies[name, index]:
            copy.start()

    def merge_step(name, index):
        stages = chunk_stages(name, n_bits)
        before = stages[index - 1][0]
        copies = stage_copies[name, index - 1]
        offset, rows = segment(name, index)
        both_before = len(copies) == 2
        base = stage_base[name, index - 1]

        def merge(array, row0, count, box=None, replace=False):
            start = base + rows if array is oth else base
            step = 48 if count % 48 == 0 else 16
            target, target0 = box or (array, row0)

            def one(at):
                row = row0 + step * at
                here = rows_at(row, step, 16)
                value = stage_recv[rows_at(start + row - offset, step, 16), :]
                if not replace:
                    value = (array[here, :].astype(f32) + value.astype(f32)).astype(bf16)
                target[rows_at(target0 + step * at, step, 16), :] = value

            loop(count // step, one)

        def go_on():
            if index == len(stages):
                back_copies[name, returns[name][-1]].start()
            else:
                start_stage(name, index)

        if before == "Z1":

            @pl.when(at_end)
            def _():
                copies[0].wait_send()

            @pl.when(jnp.logical_not(at_end))
            def _():
                copies[0].wait_recv()
                merge(acc, offset, rows)
                go_on()

            return
        if before == "Z2":

            @pl.when(jnp.logical_not(at_end))
            def _():
                copies[0].wait()
                merge(acc, offset, rows)
                go_on()

            return
        if before == "Z3":

            @pl.when(at_end)
            def _():
                copies[0].wait_recv()
                merge(acc, offset, rows, replace=True)

            @pl.when(jnp.logical_not(at_end))
            def _():
                copies[0].wait_send()

            go_on()
            return
        for copy in copies:
            copy.wait()
        arrays = [acc, oth] if both_before else [acc]
        if index == len(stages):
            merge(acc, offset, rows)
            go_on()
            return
        dim, halved, count, _ = stages[index]
        if dim == "y":
            for array in reversed(arrays):
                merge(array, offset, rows)
                if array is oth or not both_before:
                    start_stage(name, index)
        elif dim == "Z1":
            merge(acc, offset, rows)

            @pl.when(at_end)
            def _():
                start_stage(name, index)

        elif halved:
            for array in arrays:
                box = outbox[name, index] if array is acc else None
                merge(array, offset + (1 - wide_bit(dim)) * count, count, box)
            start_stage(name, index)
            for array in arrays:
                merge(array, offset + wide_bit(dim) * count, count)
        else:
            merge(acc, offset, rows)
            start_stage(name, index)

    def back_step(name, at):
        back_copies[name, returns[name][at]].wait()
        if at > 0:
            back_copies[name, returns[name][at - 1]].start()
        else:
            final_copies[name].start()

    for name in CHUNKS:
        plan = [functools.partial(start_stage, name, 0)]
        plan += [functools.partial(merge_step, name, index + 1) for index in range(len(chunk_stages(name, n_bits)))]
        plan += [functools.partial(back_step, name, at) for at in reversed(range(len(returns[name])))]
        plans[name] = plan

    place = 2 * wide + chip_y
    r_sib, row_copies, own_rows = [], [], []
    for part_index in range(2):
        mine = gathered_out.at[part_index, core]
        r_sib.append(remote(sums.at[part_index], sums_recv.at[part_index], sib))
        own_rows.append(local(sums_low.at[part_index], mine.at[place]))
        copies = [remote(sums_low.at[part_index], mine.at[place], across)]
        for level in range(n_bits):
            count = 2 << level
            rows = mine.at[pl.ds(lax.div(place, count) * count, count)]
            copies.append(remote(rows, rows, wide_peer(level)))
        copies.append(remote(mine, mine, sib))
        row_copies.append(copies)

    def row_step(part_index, at):
        if at == 0:
            own_rows[part_index].start()
        if at == 1:
            own_rows[part_index].wait()
        if at > 0:
            row_copies[part_index][at - 1].wait()
        if at < n_bits + 2:
            row_copies[part_index][at].start()

    for part_index, key in enumerate(("re", "rl")):
        plans[key] = [functools.partial(row_step, part_index, at) for at in range(n_bits + 3)]

    def sums_ready(part_index):
        r_sib[part_index].wait()
        cols = rows_at(core * 384, 384, 128)
        total = sums[part_index, :, cols] + sums_recv[part_index, :, cols]
        sums_low[part_index] = total.astype(bf16)

    steps_at = {}
    for name in PLACES:
        if name[0] == "w":
            keys = [key for key in piece_keys if key[1] == name[1]]
            steps_at[name] = [step for key in keys for step in plans.pop(key)]
        else:
            steps_at[name] = [plans[key].pop(0) for key in SCHEDULE.get(name, ()) if plans.get(key)]
    while any(plans.values()):
        steps_at["g3"] += [plans[key].pop(0) for key in plans if plans[key]]

    def point(name):
        for step in steps_at[name]:
            step()

    def need(matrix):
        point("w" + matrix)
        for key in piece_keys:
            if key[1] == matrix:
                for copy in w_last[key]:
                    copy.wait_recv()

    for copy in c_small:
        copy.wait()
    time_step = step_in[chip_y]
    for row in range(3):
        vec[row : row + 1, :] = lines[row][...].reshape(1, D)

    for copy in c_ada:
        copy.wait()
    picked = table[pl.ds(time_step, 1), :]
    vec[3:4, 0:128] = picked
    cond = picked / (1.0 + jnp.exp(-picked))
    cond = jnp.broadcast_to(cond, (16, 128)).astype(bf16)
    for index in range(6):
        flat = dot(cond, w_ada[:, index * D : (index + 1) * D], NN)
        mod[index : index + 1, :] = ada_line[pl.ds(index * D, D)].reshape(1, D) + flat[0:1, :]

    def first_norm(source, src0, dst0):
        def one(index):
            values = source[rows_at(src0 + 128 * index, 128, 128), :].astype(f32)
            vhat, _ = normalize(values)
            out = vhat * vec[0:1, :] * (1.0 + mod[1:2, :]) + mod[0:1, :]
            normed[rows_at(dst0 + 128 * index, 128, 128), :] = out.astype(bf16)

        loop(4, one)

    c_tok.wait()
    first_norm(tok, 0, own0)
    point("n0")
    r_tok.wait_recv()
    first_norm(n2, sib0, sib0)
    c_cot.wait()
    mask = jnp.broadcast_to(mask_line[...].astype(f32).reshape(1, ROWS_LOCAL), (8, ROWS_LOCAL)).T[:, 0:1]
    cot[...] = (cot[...].astype(f32) * mask).astype(bf16)
    r_cot.start()
    point("n1")

    def project(shard):
        def one(index):
            cols = rows_at(256 * index, 256, 256)
            flat = dot(wqkv[shard], normed[cols, :], NT)
            cos_b, sin_b = cos_t[:, cols], sin_t[:, cols]
            for kind in (0, 1):
                scale = 0.125 if kind == 0 else 1.0
                for head in range(SHARD_HEADS):
                    at = kind * 192 + head * HD
                    low, high = flat[at : at + 32], flat[at + 32 : at + 64]
                    proj[shard, at : at + 32, cols] = ((low * cos_b - high * sin_b) * scale).astype(bf16)
                    proj[shard, at + 32 : at + 64, cols] = ((high * cos_b + low * sin_b) * scale).astype(bf16)
            proj[shard, 384:576, cols] = flat[384:576].astype(bf16)
            point_in("p", 2 * shard + lax.div(index, 2), lax.rem(index, 2) == 1, 4)

        loop(4, one)

    def point_in(prefix, index, last, count):
        for place in range(count):
            if steps_at.get(prefix + str(place)) and (prefix, place) != ("u", 3):

                @pl.when((index == place) & last)
                def _():
                    point(prefix + str(place))

    def head_rows(kind, head):
        return rows_at(kind * 192 + head * HD, HD, HD)

    def attend(shard, head):
        q_t = proj[shard, head_rows(0, head), :]
        k_t = proj[shard, head_rows(1, head), :]
        v_t = proj[shard, head_rows(2, head), :]
        scores = dot(k_t, q_t, TN)
        top = jnp.max(scores, axis=0, keepdims=True)
        weights = jnp.exp(scores - top)
        total = jnp.sum(weights, axis=0, keepdims=True)
        out = dot(v_t, weights.astype(bf16), NN) * (1.0 / total)
        index = shard * SHARD_HEADS + head
        ho[rows_at(index * HD, HD, HD), :] = out.astype(bf16)
        lse[index, 0:1, :] = top + jnp.log(total)

    c_wqkv.wait()

    def shard_heads(shard):
        @pl.when(shard == 1)
        def _():
            need("q")

        project(shard)

        def one(head):
            attend(shard, head)
            point_in("a", SHARD_HEADS * shard + head, True, 6)

        loop(SHARD_HEADS, one)

    loop(2, shard_heads)

    c_wout.wait()
    need("o")
    half = 256

    def exchange_start(recv, index):
        rows = pl.ds(half * index, half)
        copy = remote(send_a.at[rows], recv.at[rows], sib)
        copy.start()
        return copy

    r_attn = []
    for index in range(2):
        out = dot(ho[:, rows_at(sib0 + half * index, half, half)], wout[...], TN)
        send_a[half * index : half * (index + 1), :] = out.astype(bf16)
        r_attn.append(exchange_start(recv_a, index))
    for index in range(2):
        out = dot(ho[:, rows_at(own0 + half * index, half, half)], wout[...], TN)
        attn[half * index : half * (index + 1), :] = out
    point("o0")
    r_n2 = []
    for index in range(2):
        r_attn[index].wait_recv()

        def second_norm(sub):
            rows = rows_at(half * index + 128 * sub, 128, 128)
            value = attn[rows, :] + recv_a[rows, :].astype(f32)
            attn[rows, :] = value
            residual = tok[rows, :].astype(f32) + mod[2:3, :] * value
            mid[rows, :] = residual
            vhat, _ = normalize(residual)
            out = vhat * vec[1:2, :] * (1.0 + mod[4:5, :]) + mod[3:4, :]
            n2[rows_at(own0 + half * index + 128 * sub, 128, 128), :] = out.astype(bf16)

        loop(2, second_norm)
        rows = rows_at(own0 + half * index, half, half)
        r_n2.append(remote(n2.at[rows], n2.at[rows], sib))
        r_n2[index].start()
        r_attn[index].wait_send()

    r_cot.wait_recv()

    def branch_grad(index):
        rows = rows_at(own0 + 128 * index, 128, 128)
        part_rows = rows_at(128 * index, 128, 128)
        gb[rows, :] = (cot[part_rows, :].astype(f32) * mod[5:6, :]).astype(bf16)
        rows = rows_at(sib0 + 128 * index, 128, 128)
        gb[rows, :] = (gb[rows, :].astype(f32) * mod[5:6, :]).astype(bf16)

    r_cot.wait_send()
    loop(4, branch_grad)
    point("o1")

    c_wup.wait()
    r_bup.wait_recv()
    for row in range(2):
        vec[4 + row : 5 + row, :] = bup[row][...].reshape(1, D)
    gelu_c = math.sqrt(2.0 / math.pi)

    def up(shard, block):
        @pl.when((shard == 0) & (block == 2))
        def _():
            r_n2[0].wait_recv()
            r_n2[1].wait_recv()

        rows = rows_at(lax.rem(own0 + 256 * block, LEN), 256, 256)
        cols = rows_at(shard * D, D, D)
        pre = dot(n2[rows, :], wup[:, cols], NN) + vec[pl.ds(4 + shard, 1), :]
        square = pre * pre
        squash = jnp.tanh(gelu_c * pre * (1.0 + 0.044715 * square))
        gate = 0.5 * (1.0 + squash)
        hidden[rows, cols] = (pre * gate).astype(bf16)
        slope = gate + 0.5 * pre * (1.0 - squash * squash) * (gelu_c * (1.0 + 3.0 * 0.044715 * square))
        gel[rows, cols] = slope.astype(bf16)

    loop(4, functools.partial(up, 0))
    point("u3")

    def w_down_grad(shard, target, base):
        def one(index):
            cols = rows_at(shard * D + 256 * index, 256, 256)
            out = dot(hidden[:, cols], gb[...], TN)
            target[rows_at(base + 256 * index, 256, 256), :] = out.astype(bf16)

        loop(3, one)

    w_down_grad(0, acc, 0)
    point("v0")
    sums[...] = jnp.zeros_like(sums)
    c_wdown.wait()

    def hidden_grad(shard, row):
        def one(index):
            rows = rows_at(256 * index, 256, 256)
            cols = pl.ds(shard * D, D)
            grad_act = dot(gb[rows, :], wdown[pl.ds(shard * D, D), :], NT)
            low = (grad_act * gel[rows, cols].astype(f32)).astype(bf16)
            gel[rows, cols] = low
            line = pl.ds(row, 1)
            sums[1, line, :] = sums[1, line, :] + jnp.sum(low.astype(f32), axis=0, keepdims=True)

        loop(4, one)

    def w_up_grad(shard, target):
        def one(index):
            cols = rows_at(256 * index, 256, 256)
            out = dot(n2[:, cols], gel[:, pl.ds(shard * D, D)], TN)
            target[rows_at(D + 256 * index, 256, 256), :] = out.astype(bf16)

        loop(3, one)

    hidden_grad(0, 3 + narrow)
    point("v1")
    need("u")

    def up_other(block):
        up(1, block)
        point_in("u", block + 4, True, 8)

    loop(4, up_other)
    w_down_grad(1, oth, 0)
    point("f0")
    w_up_grad(0, acc)
    point("f1")
    need("d")
    hidden_grad(1, 3 + lax.rem(narrow + 2, 4))
    point("f3")

    r_gn2 = []
    for index in range(2):
        out = dot(gel[rows_at(sib0 + half * index, half, half), :], wup[...], NT)
        send_a[half * index : half * (index + 1), :] = out.astype(bf16)
        r_gn2.append(exchange_start(recv_b, index))
    for index in range(2):
        out = dot(gel[rows_at(own0 + half * index, half, half), :], wup[...], NT)
        part[half * index : half * (index + 1), :] = out
    point("f4")
    w_up_grad(1, oth)
    point("f5")

    r_ga = []
    for index in range(2):
        r_gn2[index].wait()

        def second_back(sub):
            rows = rows_at(half * index + 128 * sub, 128, 128)
            upstream = part[rows, :] + recv_b[rows, :].astype(f32)
            vhat, inverse = normalize(mid[rows, :])
            scaled = upstream * (1.0 + mod[4:5, :])
            grad_mixed = cot[rows, :].astype(f32)
            value = grad_mixed + norm_grad(vhat, inverse, scaled * vec[1:2, :])
            grad_mid[rows, :] = value
            gb[rows_at(own0 + half * index + 128 * sub, 128, 128), :] = (value * mod[2:3, :]).astype(bf16)
            add_sum(0, 0, value * attn[rows, :])
            add_sum(0, 1, upstream)
            add_sum(0, 2, upstream * (vhat * vec[1:2, :]))
            add_sum(0, 4, scaled * vhat)
            add_sum(0, 5, grad_mixed * mod[5:6, :])

        def add_sum(part_index, row, values):
            line = slice(row, row + 1)
            sums[part_index, line, :] = sums[part_index, line, :] + jnp.sum(values, axis=0, keepdims=True)

        loop(2, second_back)
        rows = rows_at(own0 + half * index, half, half)
        r_ga.append(remote(gb.at[rows], gb.at[rows], sib))
        r_ga[index].start()
    point("f6")

    r_ga[0].wait_recv()
    r_ga[1].wait_recv()

    def head_grad(index):
        cols = rows_at(256 * index, 256, 256)
        do[:, cols] = dot(wout[...], gb[cols, :], NT).astype(bf16)

    loop(4, head_grad)
    point("h0")

    def w_out_grad():
        oth[1536:1728, :] = dot(ho[192:384, :], gb[...], NN).astype(bf16)
        acc[1536:1728, :] = dot(ho[0:192, :], gb[...], NN).astype(bf16)
        point("h1")

    if not LATE_OUT:
        w_out_grad()

    def attend_back(shard, head, between):
        q_t = proj[shard, head_rows(0, head), :]
        k_t = proj[shard, head_rows(1, head), :]
        v_t = proj[shard, head_rows(2, head), :]
        index = shard * SHARD_HEADS + head
        d_t = do[rows_at(index * HD, HD, HD), :]
        probs = jnp.exp(dot(k_t, q_t, TN) - lse[index, 0:1, :])
        grad_probs = dot(v_t, d_t, TN)
        inner = jnp.sum(probs * grad_probs, axis=0, keepdims=True)
        grad_scores = (probs * (grad_probs - inner)).astype(bf16)
        between()
        dq_t = dot(k_t, grad_scores, NN) * 0.125
        dk_t = dot(grad_scores, q_t, NT).T
        dv_t = dot(probs.astype(bf16), d_t, NT).T
        for kind, grad in ((0, dq_t), (1, dk_t)):
            low, high = grad[:32], grad[32:]
            turned = jnp.concatenate(
                [low * cos_t[...] + high * sin_t[...], high * cos_t[...] - low * sin_t[...]], axis=0
            )
            proj[shard, head_rows(kind, head), :] = turned.astype(bf16)
        proj[shard, head_rows(2, head), :] = dv_t.astype(bf16)

    for key in piece_keys:
        for copy in w_sent[key] + [w_across[key]]:
            copy.wait_send()

    def w_qkv_grad(shard, target):
        def one(index):
            rows = rows_at(192 * index, 192, 64)
            out = dot(proj[shard, rows, :], normed[...], NN)
            target[rows_at(1728 + 192 * index, 192, 64), :] = out.astype(bf16)

        loop(3, one)

    def back_heads(index):
        shard = 1 - lax.div(index, SHARD_HEADS)
        head = lax.rem(index, SHARD_HEADS)
        attend_back(shard, head, lambda: point_in("i", index, True, 6))
        point_in("b", index, True, 6)

        @pl.when(index == 2)
        def _():
            w_qkv_grad(1, oth)
            point("bx")

    loop(6, back_heads)
    w_qkv_grad(0, acc)
    point("by")
    if LATE_OUT:
        w_out_grad()

    r_branch = []
    for index in range(2):
        out = dot(hidden[rows_at(sib0 + half * index, half, half), :], wdown[...], NN)
        send_a[half * index : half * (index + 1), :] = out.astype(bf16)
        r_branch.append(exchange_start(recv_c, index))
    for index in range(2):
        out = dot(hidden[rows_at(own0 + half * index, half, half), :], wdown[...], NN)
        part[half * index : half * (index + 1), :] = out
    point("c0")


    def normed_grad(offset):
        first = dot(proj[0, :, offset], wqkv[0], TN)
        return first + dot(proj[1, :, offset], wqkv[1], TN)

    r_gn = []
    for index in range(2):
        rows = pl.ds(half * index, half)
        recv_b[rows, :] = normed_grad(rows_at(sib0 + half * index, half, half)).astype(bf16)
        r_gn.append(remote(recv_b.at[rows], recv_a.at[rows], sib))
        r_gn[index].start()
    for index in range(2):
        attn[half * index : half * (index + 1), :] = normed_grad(rows_at(own0 + half * index, half, half))
    point("g0")

    def finish_branch(index):
        rows = rows_at(128 * index, 128, 128)
        branch = part[rows, :] + recv_c[rows, :].astype(f32) + vec[2:3, :]
        add_sum(0, 3, cot[rows, :].astype(f32) * branch)
        send_a[rows, :] = (mid[rows, :] + mod[5:6, :] * branch).astype(bf16)

    r_branch[0].wait()
    r_branch[1].wait()
    loop(4, finish_branch)
    c_mixed = local(send_a, mixed_out)
    c_mixed.start()
    on_first = (1 - core).astype(f32)
    high = lax.div(time_step, 32)
    picked = vec[3:4, 0:128]
    sigma = 1.0 / (1.0 + jnp.exp(-picked))
    slope = sigma * (1.0 + picked * (1.0 - sigma))
    slope_high = slope.astype(bf16).astype(f32)
    entries = [
        jnp.full((1, 128), high.astype(f32)),
        jnp.full((1, 128), (time_step - 32 * high).astype(f32)),
        (picked / (1.0 + jnp.exp(-picked))).astype(bf16).astype(f32),
        slope_high,
        slope - slope_high,
    ]
    for at, entry in enumerate(entries):
        sums[0, 6:7, 128 * at : 128 * (at + 1)] = entry * on_first
    r_sib[0].start()
    point("c1")

    for index in range(2):
        r_gn[index].wait()

        def first_back(sub):
            rows = rows_at(half * index + 128 * sub, 128, 128)
            upstream = attn[rows, :] + recv_a[rows, :].astype(f32)
            vhat, inverse = normalize(tok[rows, :].astype(f32))
            scaled = upstream * (1.0 + mod[1:2, :])
            attn[rows, :] = grad_mid[rows, :] + norm_grad(vhat, inverse, scaled * vec[0:1, :])
            add_sum(1, 0, upstream)
            add_sum(1, 1, upstream * (vhat * vec[0:1, :]))
            add_sum(1, 2, scaled * vhat)

        loop(2, first_back)
    c_grad_tok = local(attn, grad_tok_out)
    c_grad_tok.start()

    r_sib[1].start()
    point("g1")
    sums_ready(0)
    sums_ready(1)
    point("g2")
    point("g3")
    for name in CHUNKS:
        final_copies[name].wait()
    c_grad_tok.wait()
    c_mixed.wait()
    for copy in [r_tok, r_bup] + r_n2 + r_ga:
        copy.wait_send()


def fused_block(n_wide, tokens, cot, mask, timestep, table, w_ada, b_ada, gain_one, w_qkv_t, w_out, gain_two, w_up, b_up,
                w_down, b_down, cos_t, sin_t):
    n_bits = n_wide.bit_length() - 1
    any_space = pl.BlockSpec(memory_space=pl.ANY)
    scratch = [
        pltpu.VMEM((ROWS_LOCAL, D), bf16),
        pltpu.VMEM((ROWS_LOCAL, D), bf16),
        pltpu.VMEM((LEN, D), bf16),
        pltpu.VMEM((LEN, D), bf16),
        pltpu.VMEM((LEN, D), bf16),
        pltpu.VMEM((2, QKV_ROWS, D), bf16),
        pltpu.VMEM((384, D), bf16),
        pltpu.VMEM((D, 2 * D), bf16),
        pltpu.VMEM((2 * D, D), bf16),
        pltpu.VMEM((2, QKV_ROWS, LEN), bf16),
        pltpu.VMEM((384, LEN), bf16),
        pltpu.VMEM((384, LEN), bf16),
        pltpu.VMEM((6, 8, LEN), f32),
        pltpu.VMEM((ROWS_LOCAL, D), f32),
        pltpu.VMEM((ROWS_LOCAL, D), f32),
        pltpu.VMEM((ROWS_LOCAL, D), f32),
        pltpu.VMEM((LEN, 2 * D), bf16),
        pltpu.VMEM((LEN, 2 * D), bf16),
        pltpu.VMEM((ROWS_LOCAL, D), f32),
        pltpu.VMEM((ROWS_LOCAL, D), bf16),
        pltpu.VMEM((ROWS_LOCAL, D), bf16),
        pltpu.VMEM((ROWS_LOCAL, D), bf16),
        pltpu.VMEM((ROWS_LOCAL, D), bf16),
        pltpu.VMEM((GRAD_ROWS, D), bf16),
        pltpu.VMEM((GRAD_ROWS, D), bf16),
        pltpu.VMEM((outbox_rows(n_bits), D), bf16),
        pltpu.VMEM((8, D), f32),
        pltpu.VMEM((8, D), f32),
        [pltpu.VMEM((D,), f32)] * 2,
        pltpu.VMEM((6 * D,), f32),
        [pltpu.VMEM((D,), f32)] * 3,
        pltpu.VMEM((ROWS_LOCAL,), jnp.int32),
        pltpu.VMEM((32, LEN), f32),
        pltpu.VMEM((32, LEN), f32),
        pltpu.VMEM((2, 8, D), f32),
        pltpu.VMEM((2, 8, D), f32),
        pltpu.VMEM((2, 8, D // 2), bf16),
        pltpu.SemaphoreType.DMA((remote_count(n_bits),)),
        pltpu.SemaphoreType.DMA((remote_count(n_bits),)),
        pltpu.SemaphoreType.DMA((20 + len(CHUNKS),)),
        pltpu.VMEM((recv_rows(n_bits), D), bf16),
        pltpu.VMEM(table.shape, f32),
        pltpu.VMEM(w_ada.shape, bf16),
    ]
    specs = [any_space] * 17
    specs[3] = pl.BlockSpec(memory_space=pltpu.SMEM)
    return pl.pallas_call(
        functools.partial(block_kernel, n_bits),
        out_shape=(
            jax.ShapeDtypeStruct((ROWS_LOCAL, D), bf16),
            jax.ShapeDtypeStruct((ROWS_LOCAL, D), f32),
            jax.ShapeDtypeStruct((2, 2, 2 * n_wide, 8, D // 2), bf16),
            jax.ShapeDtypeStruct((GRAD_ROWS, D), bf16),
        ),
        in_specs=specs,
        out_specs=[any_space] * 4,
        scratch_shapes=scratch,
        compiler_params=pltpu.CompilerParams(
            collective_id=0, has_side_effects=True, vmem_limit_bytes=61 * 1024 * 1024
        ),
    )(tokens, cot, mask, timestep, table, w_ada, b_ada, gain_one, w_qkv_t, w_out, gain_two, w_up, b_up, w_down, b_down,
      cos_t, sin_t)


def finish_kernel(
    gathered_in, w_ada_in, grads_in, mixed_in, grad_tok_in,
    mixed_out, grad_tok_out, g_table, g_w_ada, g_b_ada, g_gain_one, g_wqkv, g_wout, g_gain_two, g_wup, g_bup,
    g_wdown, g_b_down,
    gathered, w_ada, grads, mod_low, table_out, ada_out, wide_out, late_sum, mixed_buf, tok_buf, lines, sem,
):
    pieces = GRAD_ROWS // 192
    targets = [(g_wdown, 0), (g_wup, 768), (g_wout, 1536), (g_wqkv, 1728)]
    loads = [(gathered_in, gathered), (w_ada_in, w_ada)]
    loads = [pltpu.make_async_copy(src, dst, sem.at[at]) for at, (src, dst) in enumerate(loads)]
    pass_in = [
        pltpu.make_async_copy(mixed_in, mixed_buf, sem.at[3]),
        pltpu.make_async_copy(grad_tok_in, tok_buf, sem.at[4]),
    ]
    pass_out = [
        pltpu.make_async_copy(mixed_buf, mixed_out, sem.at[5]),
        pltpu.make_async_copy(tok_buf, grad_tok_out, sem.at[6]),
    ]
    grad_in, grad_out = [], []
    for piece in range(pieces):
        rows = pl.ds(192 * piece, 192)
        grad_in.append(pltpu.make_async_copy(grads_in.at[rows], grads.at[rows], sem.at[7 + piece]))
        target, first = [item for item in targets if item[1] <= 192 * piece][-1]
        grad_out.append(
            pltpu.make_async_copy(
                wide_out.at[rows], target.at[pl.ds(192 * piece - first, 192)], sem.at[7 + pieces + piece]
            )
        )
    for copy in grad_in[: pieces // 4] + loads + pass_in + grad_in[pieces // 4 :]:
        copy.start()

    def widen(piece):
        grad_in[piece].wait()
        rows = pl.ds(192 * piece, 192)
        wide_out[rows, :] = grads[rows, :].astype(f32)
        grad_out[piece].start()

    for piece in range(pieces // 4):
        widen(piece)
    for copy in loads:
        copy.wait()
    for at in range(2):
        pass_in[at].wait()
        pass_out[at].start()

    def both(index):
        return jnp.concatenate([gathered[index, 0].astype(f32), gathered[index, 1].astype(f32)], axis=-1)

    early, late = both(0), both(1)
    total_early, total_late = jnp.sum(early, axis=0), jnp.sum(late, axis=0)
    late_sum[...] = total_late
    for row, values in enumerate([late[:, 0], late[:, 1], early[:, 0], early[:, 1], early[:, 2], early[:, 3]]):
        mod_low[:, row * D : (row + 1) * D] = values.astype(bf16)
    rows = [total_late[0:1], total_late[1:2]] + [total_early[row : row + 1] for row in range(4)]
    for row, values in enumerate(rows):
        lines[0][pl.ds(row * D, D)] = values.reshape(D)
    lines[1][...] = total_late[2:3].reshape(D)
    lines[2][...] = total_early[4:5].reshape(D)
    lines[3][...] = late_sum[pl.ds(3 + lax.axis_index("narrow"), 1), :].reshape(D)
    lines[4][...] = total_early[5:6].reshape(D)
    line_out = [
        pltpu.make_async_copy(line, out, sem.at[7 + 2 * pieces + at])
        for at, (line, out) in enumerate(zip(lines, (g_b_ada, g_gain_one, g_gain_two, g_bup, g_b_down)))
    ]
    for copy in line_out:
        copy.start()
    seqs, steps = early.shape[0], table_out.shape[0]
    time_step = early[:, 6, 0:1] * 32.0 + early[:, 6, 128:129]
    columns = lax.broadcasted_iota(jnp.int32, (seqs, steps), 1).astype(f32)
    pick = jnp.where(columns == time_step, 1.0, 0.0).astype(bf16)
    cond = early[:, 6, 256:384].astype(bf16)
    ada_out[...] = dot(cond, mod_low[...], TN)
    out_ada = pltpu.make_async_copy(ada_out, g_w_ada, sem.at[7 + 2 * pieces + 5])
    out_ada.start()
    grad_cond = dot(mod_low[...], w_ada[...], NT) * (early[:, 6, 384:512] + early[:, 6, 512:640])
    rest, picked_sum = grad_cond, None
    for _ in range(3):
        low = rest.astype(bf16)
        rest = rest - low.astype(f32)
        term = dot(pick, low, TN)
        picked_sum = term if picked_sum is None else picked_sum + term
    table_out[...] = picked_sum
    out_table = pltpu.make_async_copy(table_out, g_table, sem.at[7 + 2 * pieces + 6])
    out_table.start()
    for piece in range(pieces // 4, pieces):
        widen(piece)
    for copy in line_out + [out_ada, out_table] + pass_out + grad_out:
        copy.wait()


def finish(gathered, table, w_ada, grads, mixed, grad_tokens):
    seqs, steps = gathered.shape[2], table.shape[0]
    any_space = pl.BlockSpec(memory_space=pl.ANY)
    shapes = [
        (mixed.shape, bf16), (grad_tokens.shape, f32), (table.shape, f32), (w_ada.shape, f32), ((6 * D,), f32),
        ((D,), f32), ((QKV_ROWS, D), f32), ((192, D), f32), ((D,), f32), ((D, D), f32), ((D,), f32), ((D, D), f32),
        ((D,), f32),
    ]
    return pl.pallas_call(
        finish_kernel,
        out_shape=tuple(jax.ShapeDtypeStruct(shape, kind) for shape, kind in shapes),
        in_specs=[any_space] * 5,
        out_specs=[any_space] * len(shapes),
        scratch_shapes=[
            pltpu.VMEM(gathered.shape, bf16),
            pltpu.VMEM(w_ada.shape, bf16),
            pltpu.VMEM(grads.shape, bf16),
            pltpu.VMEM((seqs, 6 * D), bf16),
            pltpu.VMEM((steps, table.shape[1]), f32),
            pltpu.VMEM(w_ada.shape, f32),
            pltpu.VMEM(grads.shape, f32),
            pltpu.VMEM((8, D), f32),
            pltpu.VMEM(mixed.shape, bf16),
            pltpu.VMEM(grad_tokens.shape, f32),
            [pltpu.VMEM((6 * D,), f32)] + [pltpu.VMEM((D,), f32)] * 4,
            pltpu.SemaphoreType.DMA((48,)),
        ],
        compiler_params=pltpu.CompilerParams(vmem_limit_bytes=56 * 1024 * 1024),
    )(gathered, w_ada, grads, mixed, grad_tokens)


def rope_tables():
    half_width = HD // 2
    frequency = np.float32(10000.0) ** (np.float32(-2.0) * np.arange(half_width, dtype=np.float32) / np.float32(HD))
    angles = np.arange(LEN, dtype=np.float32)[None, :] * frequency[:, None]
    return np.cos(angles).astype(np.float32), np.sin(angles).astype(np.float32)


def body(tokens, timestep, token_mask, time_table, w_ada, b_ada, gain_one, w_qkv, w_out, gain_two, w_up, b_up,
         w_down, b_down, cotangent):
    n_wide = lax.axis_size("wide")
    cos_t, sin_t = rope_tables()
    w_qkv_t = jnp.transpose(w_qkv, (0, 2, 1)).reshape(QKV_ROWS, D)
    mixed, grad_tokens, gathered, grads = fused_block(
        n_wide, tokens, cotangent, token_mask, timestep, time_table, w_ada, b_ada, gain_one, w_qkv_t, w_out, gain_two,
        w_up, b_up, w_down, b_down, cos_t, sin_t,
    )
    outs = list(finish(gathered, time_table, w_ada, grads, mixed, grad_tokens))
    outs[6] = jnp.transpose(outs[6].reshape(3, 192, D), (0, 2, 1))
    return tuple(outs)


def solution(mesh):
    return jax.shard_map(
        body,
        mesh=mesh,
        in_specs=(
            P(("wide", "narrow"), None), P("wide"), P(("wide", "narrow")), P(), P(), P(), P(),
            P(None, None, "narrow"), P("narrow", None), P(), P(None, "narrow"), P("narrow"), P("narrow", None), P(),
            P(("wide", "narrow"), None),
        ),
        out_specs=(
            P(("wide", "narrow"), None), P(("wide", "narrow"), None), P(), P(), P(), P(), P(None, None, "narrow"),
            P("narrow", None), P(), P(None, "narrow"), P("narrow"), P("narrow", None), P(),
        ),
        check_vma=False,
    )
```
